512 devices in a mesh: row: 64 (over x, y, z_hi, core), col: 8 (over z_lo).
Axes of the slice: x: 4, y: 4, z: 16 (z_hi: 2, z_lo: 8; z = z_hi * 8 + z_lo), core: 2. Of those that a mesh axis runs over, the one named last changes fastest.
Arguments:
- inputs: bfloat16 [256, 1024, 256], P('row', 'col'), may hold values from -6 to 6
- preactivation: bfloat16 [256, 1024, 256], P('row', 'col'), may hold values from -6 to 6
- cotangent: bfloat16 [256, 1024, 256], P('row', 'col'), may hold values from -6 to 6
- spectral: bfloat16 [2, 128, 64, 5, 1024], P(None, 'row', 'col'), may hold values from -2 to 2
- bypass: bfloat16 [32, 32], replicated, may hold values from -1 to 1
Outputs:
- grad_inputs: bfloat16 [256, 1024, 256], P('row', 'col')
- grad_spectral: float32 [2, 128, 64, 5, 1024], P(None, 'row', 'col')
- grad_bypass: float32 [32, 32], replicated
The draws below stay inside these ranges and needn't reach their ends.
All inputs are finite; a program needn't handle non-finite values.
Results may differ from the reference program's by a relative error of at most 0.022.
Values may be sent and summed in bfloat16 or wider, within the bound.
A program may use at most 64 MiB of HBM per device.

```python
import math
import jax
import jax.numpy as jnp
from jax import lax

ROWS_DEV = 4
COLS_DEV = 128
NT = 8
C = 32
KX = 128
KY = 64
KT = 5
NX = 256
NY = 1024
N_COL = 8


def block_scale(own_key, extent, shards, low, largest):
    gain = 1.0
    for axis_at, shards_of in shards:
        steps = jax.random.uniform(jax.random.fold_in(jax.random.fold_in(own_key, 6), axis_at), (shards_of,), jnp.float32, low / len(shards), largest / len(shards))
        gain = gain * jnp.repeat(jnp.exp(steps), extent[axis_at] // shards_of).reshape((-1,) + (1,) * (len(extent) - 1 - axis_at))
    return gain


def normal_values(stream_key, shape, deviation, most, pieces=(), kind=jnp.bfloat16):
    drawn = deviation * jax.random.normal(stream_key, shape, jnp.float32)
    if pieces:
        drawn = drawn * block_scale(stream_key, shape, pieces, -0.22, 0.18)
    return jnp.clip(drawn, -most, most).astype(kind)


def setup_inputs(seed: int = 0) -> dict:
    splits = jax.random.split(jax.random.key(seed), 6)
    inputs = normal_values(splits[0], (NX, NY, NT * C), 1.0, 6.0, ((0, 64), (1, 8)))
    preactivation = normal_values(splits[1], (NX, NY, NT * C), 1.0, 6.0, ((0, 64), (1, 8)))
    cotangent = normal_values(splits[2], (NX, NY, NT * C), 1.0, 6.0, ((0, 64), (1, 8)))
    spectral = normal_values(splits[3], (2, KX, KY, KT, C * C), (C // 4) ** -0.5, 2.0, ((1, 64), (2, 8)))
    bypass = normal_values(splits[4], (C, C), C ** -0.5, 1.0)
    return {"inputs": inputs, "preactivation": preactivation, "cotangent": cotangent, "spectral": spectral, "bypass": bypass}


exact_mode = lax.Precision.HIGHEST

def counting(length):
    return jnp.arange(length, dtype=jnp.int32)

def kept_freq(slot_index, keep_count):
    return jnp.where(slot_index < keep_count // 2, slot_index, slot_index - keep_count)

def phase_table(outer_index, inner_index, length, direction):
    turn_count = jnp.mod(outer_index[:, None] * inner_index[None, :], length)
    angles = turn_count.astype(jnp.float32) * (2.0 * math.pi / length)
    cosine = jnp.cos(angles)
    sine_part = direction * jnp.sin(angles)
    top_rows = jnp.stack([cosine, -sine_part], axis=1)
    low_rows = jnp.stack([sine_part, cosine], axis=1)
    return jnp.stack([top_rows, low_rows], axis=0)

def time_forward(step_count, time_modes):
    turn_count = jnp.mod(counting(step_count)[:, None] * counting(time_modes)[None, :], step_count)
    angles = turn_count.astype(jnp.float32) * (2.0 * math.pi / step_count)
    return jnp.stack([jnp.cos(angles), -jnp.sin(angles)], axis=1)

def time_inverse(step_count, time_modes):
    turn_count = jnp.mod(counting(time_modes)[:, None] * counting(step_count)[None, :], step_count)
    angles = turn_count.astype(jnp.float32) * (2.0 * math.pi / step_count)
    return jnp.stack([jnp.cos(angles), -jnp.sin(angles)], axis=0)

def gelu_slope(values):
    normal_cdf = 0.5 * (1.0 + lax.erf(values * (1.0 / math.sqrt(2.0))))
    density = jnp.exp(-0.5 * values * values) * (1.0 / math.sqrt(2.0 * math.pi))
    return normal_cdf + values * density

def mix_modes(modes_in, modes_grad, weight, factor):
    in_real = modes_in[:, 0]
    in_imag = modes_in[:, 1]
    grad_real = modes_grad[:, 0]
    grad_imag = modes_grad[:, 1]
    real_part = factor * (in_real[..., :, None] * grad_real[..., None, :] + in_imag[..., :, None] * grad_imag[..., None, :])
    imag_part = factor * (in_real[..., :, None] * grad_imag[..., None, :] - in_imag[..., :, None] * grad_real[..., None, :])
    weight_grad = jnp.stack([real_part, imag_part], axis=0)
    w_real = weight[0]
    w_imag = weight[1]
    back_real = factor * (jnp.einsum('kyscd,kysd->kysc', w_real, grad_real, precision=exact_mode) + jnp.einsum('kyscd,kysd->kysc', w_imag, grad_imag, precision=exact_mode))
    back_imag = factor * (jnp.einsum('kyscd,kysd->kysc', w_real, grad_imag, precision=exact_mode) - jnp.einsum('kyscd,kysd->kysc', w_imag, grad_real, precision=exact_mode))
    return (weight_grad, jnp.stack([back_real, back_imag], axis=1))

def reference(inputs, preactivation, cotangent, spectral, bypass):
    factor = 1.0 / math.sqrt(float(NX * NY * NT * KX * KY * KT))
    forward_t = time_forward(NT, KT)
    inverse_t = time_inverse(NT, KT)
    col_table = phase_table(counting(KY), counting(NY), NY, -1.0).reshape(2, KY, 2, N_COL, COLS_DEV)
    inverse_cols = phase_table(counting(NY), counting(KY), NY, 1.0)
    row_freqs = kept_freq(counting(KX), KX)
    block_count = NX // ROWS_DEV

    def block_grad(first_row):
        pre_block = lax.dynamic_slice_in_dim(preactivation, first_row, ROWS_DEV, 0)
        cot_block = lax.dynamic_slice_in_dim(cotangent, first_row, ROWS_DEV, 0)
        slopes = gelu_slope(pre_block.astype(jnp.float32))
        return (cot_block.astype(jnp.float32) * slopes).astype(jnp.bfloat16)

    def to_cols(field):
        cube_view = field.astype(jnp.float32).reshape(ROWS_DEV, N_COL, COLS_DEV, NT, C)
        in_time = jnp.einsum('rjytc,tqs->rjyqsc', cube_view, forward_t, precision=exact_mode)
        partial_sums = jnp.einsum('akpjy,rjypsc->jraksc', col_table, in_time, precision=exact_mode)
        rounded = lax.optimization_barrier(partial_sums.astype(jnp.bfloat16))
        return lax.optimization_barrier(jnp.sum(rounded.astype(jnp.float32), axis=0))

    def forward_step(running, block_index):
        modes_in, modes_grad, bypass_acc = running
        first_row = (block_index * ROWS_DEV).astype(jnp.int32)
        block_in = lax.dynamic_slice_in_dim(inputs, first_row, ROWS_DEV, 0)
        pre_grad = block_grad(first_row)
        bypass_acc = bypass_acc + jnp.einsum('nc,nd->cd', block_in.reshape(-1, C), pre_grad.reshape(-1, C), preferred_element_type=jnp.float32)
        phases = phase_table(row_freqs, first_row + counting(ROWS_DEV), NX, -1.0)
        modes_in = modes_in + jnp.einsum('akpr,rpysc->kaysc', phases, to_cols(block_in), precision=exact_mode)
        modes_grad = modes_grad + jnp.einsum('akpr,rpysc->kaysc', phases, to_cols(pre_grad), precision=exact_mode)
        return ((modes_in, modes_grad, bypass_acc), None)
    start_state = (jnp.zeros((KX, 2, KY, KT, C), jnp.float32), jnp.zeros((KX, 2, KY, KT, C), jnp.float32), jnp.zeros((C, C), jnp.float32))
    final_state, unused_out = lax.scan(forward_step, start_state, counting(block_count))
    modes_in, modes_grad, bypass_acc = final_state
    weight = spectral.astype(jnp.float32).reshape(2, KX, KY, KT, C, C)
    weight_grad, back_modes = mix_modes(modes_in, modes_grad, weight, factor)
    grad_spectral = weight_grad.reshape(2, KX, KY, KT, C * C)
    grad_bypass = bypass_acc * (1.0 / math.sqrt(float(NX * NY * NT)))

    def backward_block(block_index):
        first_row = (block_index * ROWS_DEV).astype(jnp.int32)
        phases = phase_table(first_row + counting(ROWS_DEV), row_freqs, NX, 1.0)
        rows_back = jnp.einsum('axpk,kpysc->xaysc', phases, back_modes, precision=exact_mode)
        cells_y = jnp.einsum('aypk,rpksc->ryasc', inverse_cols, rows_back, precision=exact_mode)
        kernel_grad = jnp.einsum('ryasc,ast->rytc', cells_y, inverse_t, precision=exact_mode)
        pre_grad = block_grad(first_row)
        bypass_grad = jnp.einsum('nd,cd->nc', pre_grad.reshape(-1, C), bypass, preferred_element_type=jnp.float32)
        total_grad = kernel_grad.reshape(-1, C) + bypass_grad
        return total_grad.reshape(ROWS_DEV, NY, NT * C).astype(jnp.bfloat16)
    grad_inputs = lax.map(backward_block, counting(block_count)).reshape(NX, NY, NT * C)
    return (grad_inputs, grad_spectral, grad_bypass)
```

```python
import math

import jax
import jax.numpy as jnp
import numpy as np
from jax import lax
from jax.experimental import pallas as pl
from jax.experimental.pallas import tpu as pltpu
from jax.sharding import PartitionSpec as P

MESH = pl.DeviceIdType.MESH
F32 = jnp.float32
BF16 = jnp.bfloat16
NX, NY, NT, C = 256, 1024, 8, 32
KX, KY, KT = 128, 64, 5
FACTOR = 1.0 / math.sqrt(float(NX * NY * NT * KX * KY * KT))
BYPASS_SCALE = 1.0 / math.sqrt(float(NX * NY * NT))


def turns(a, b, n):
    angle = 2.0 * np.pi * (np.multiply.outer(a, b) % n) / n
    return np.cos(angle), np.sin(angle)


def column_tables():
    forward, inverse = [], []
    for j in range(8):
        cos, sin = turns(np.arange(64), 128 * j + np.arange(128), NY)
        forward.append(np.concatenate([cos, -sin], 0))
        inverse.append(np.concatenate([cos.T, -sin.T], 1))
    return np.stack(forward), np.stack(inverse)


def time_tables():
    cos, sin = turns(np.arange(NT), np.arange(KT), NT)
    eye = np.eye(C)
    low = np.zeros((2, NT, C, 2, 4, C))
    for t in range(NT):
        for k in range(4):
            low[0, t, :, 0, k, :] = eye * cos[t, k]
            low[1, t, :, 0, k, :] = eye * sin[t, k]
            low[0, t, :, 1, k, :] = -eye * sin[t, k]
            low[1, t, :, 1, k, :] = eye * cos[t, k]
    high = np.zeros((2, 2, NT, C, 2, 2, C))
    for f in range(2):
        for t in range(NT):
            high[f, 0, t, :, f, 0, :] = eye * cos[t, 4]
            high[f, 1, t, :, f, 1, :] = eye * cos[t, 4]
    forward = np.stack(
        [
            np.concatenate([low.reshape(512, 256), high[f].reshape(512, 128)], 1)
            for f in range(2)
        ]
    )
    inverse = np.zeros((3, 4, C, 2, NT, C))
    for t in range(NT):
        for k in range(4):
            inverse[0, k, :, 0, t, :] = eye * cos[t, k]
            inverse[1, k, :, 0, t, :] = -eye * sin[t, k]
            inverse[0, k, :, 1, t, :] = eye * sin[t, k]
            inverse[1, k, :, 1, t, :] = eye * cos[t, k]
        inverse[2, 0, :, 0, t, :] = eye * cos[t, 4]
        inverse[2, 1, :, 1, t, :] = eye * cos[t, 4]
    return forward, inverse.reshape(384, 512)


def regroup_tables():
    direct = np.zeros((8, 3, 2, 4, 5, 4, 8))
    swapped = np.zeros((8, 3, 2, 4, 5, 4, 8))
    back = np.zeros((4, 3, 8, 8, 2, 2, 4))
    for k in range(8):
        for x in range(4):
            for tile in range(5):
                direct[k, tile // 2, tile % 2, x, tile, x, k] = 1.0
            swapped[k, 2, 1, x, 4, x, k] = 1.0
            for tile in range(3):
                back[x, tile, k, k, tile // 2, tile % 2, x] = 1.0
    lanes = np.zeros((2, 2, C, 2, 2, C))
    for f in range(2):
        lanes[f, 1, :, f, 0, :] = np.eye(C)
        lanes[f, 0, :, f, 1, :] = -np.eye(C)
    return (
        direct.reshape(192, 160),
        swapped.reshape(192, 160),
        lanes.reshape(128, 128),
        back.reshape(96, 128),
    )


def row_tables():
    k = np.arange(KX)
    freq = np.where(k < KX // 2, k, k - KX) % NX
    cos, sin = turns(freq, np.arange(NX), NX)
    cos = cos.reshape(4, 16, 2, 4, 4, 2, 2, 4)
    sin = sin.reshape(4, 16, 2, 4, 4, 2, 2, 4)
    forward = np.zeros((4, 4, 16, 2, 2, 2, 2, 2, 4, 2, 2, 4))
    for xx in range(4):
        for slab in range(2):
            c = cos[:, :, :, xx].transpose(0, 1, 2, 4, 3, 5, 6)
            s = sin[:, :, :, xx].transpose(0, 1, 2, 4, 3, 5, 6)
            forward[xx, :, :, slab, :, 0, slab, :, :, :, 0, :] = c
            forward[xx, :, :, slab, :, 0, slab, :, :, :, 1, :] = s
            forward[xx, :, :, slab, :, 1, slab, :, :, :, 1, :] = c
            forward[xx, :, :, slab, :, 1, slab, :, :, :, 0, :] = -s
    forward = forward.reshape(4, 512, 256)
    inverse = np.zeros((4, 2, 4, 2, 2, 2, 4, 4, 16, 2, 2, 2))
    for xx in range(4):
        for zh in range(2):
            for slab in range(2):
                c = cos[:, :, :, xx, :, zh].transpose(3, 4, 5, 0, 1, 2)
                s = sin[:, :, :, xx, :, zh].transpose(3, 4, 5, 0, 1, 2)
                inverse[xx, zh, :, :, slab, 0, :, :, :, slab, :, 0] = c
                inverse[xx, zh, :, :, slab, 0, :, :, :, slab, :, 1] = -s
                inverse[xx, zh, :, :, slab, 1, :, :, :, slab, :, 1] = c
                inverse[xx, zh, :, :, slab, 1, :, :, :, slab, :, 0] = s
    return forward, inverse.reshape(8, 128, 512)


def mixing_tables():
    pick = np.zeros((2, 2, 2, 5, 8, 16, 2, 2, 2))
    pick_mask = np.zeros((2, 2, 2, 5, 8, 4, C))
    spread = np.zeros((8, 2, 2, 2, 4, 2, 5, 8))
    spread_mask = np.zeros((4, 2, 5, 8, 4, C))
    for ky in range(8):
        for e in range(2):
            for f in range(2):
                source = (ky // 2) * 4 + f * 2 + ky % 2
                for ri in range(2):
                    for kt in range(4):
                        pick[f, ri, e, kt, ky, source, 0, e, ri] = 1.0
                        pick_mask[f, ri, e, kt, ky, kt, :] = 1.0
                    pick[f, ri, e, 4, ky, source, 1, e, 0] = 1.0
                    pick_mask[f, ri, e, 4, ky, f * 2 + ri, :] = 1.0
            for kt in range(4):
                spread_mask[0, e, kt, ky, kt] = 1.0
                spread_mask[1, e, kt, ky, kt] = 1.0
                spread[ky, 0, e, 0, 0, e, kt, ky] = 1.0
                spread[ky, 0, e, 1, 1, e, kt, ky] = 1.0
            spread_mask[0, e, 4, ky, 0] = 1.0
            spread_mask[1, e, 4, ky, 1] = 1.0
            spread_mask[2, e, 4, ky, 0] = 1.0
            spread_mask[3, e, 4, ky, 1] = 1.0
            spread[ky, 1, e, 0, 0, e, 4, ky] = 1.0
            spread[ky, 1, e, 0, 1, e, 4, ky] = 1.0
            spread[ky, 1, e, 1, 2, e, 4, ky] = 1.0
            spread[ky, 1, e, 1, 3, e, 4, ky] = -1.0
    group = np.arange(128) % C
    lane = np.arange(C * C)
    by_in = (group[:, None] == lane[None, :] // C).astype(np.float64)
    by_out = (group[:, None] == lane[None, :] % C).astype(np.float64)
    return (
        pick.reshape(320, 128),
        pick_mask.reshape(320, 128),
        by_in,
        by_out,
        by_in.T,
        spread.reshape(64, 320),
        spread_mask.reshape(320, 128),
    )


def make_tables():
    t = {}
    t["col_f"], t["col_i"] = column_tables()
    t["time_f"], t["time_i"] = time_tables()
    t["reg_a"], t["reg_b"], t["reg_l"], t["reg_c"] = regroup_tables()
    t["row_f"], t["row_i"] = row_tables()
    t["pick"], t["pick_m"], t["by_in"], t["by_out"], t["by_in_t"], t["spread"], t["spread_m"] = (
        mixing_tables()
    )
    t["rep"] = (np.arange(256)[:, None] % C == np.arange(128)[None, :] % C).astype(np.float64)
    return {k: np.asarray(v, np.float32).astype(jnp.bfloat16) for k, v in t.items()}


PICKED = ("col_f", "col_i", "row_f", "row_i")
ORDER = (
    "col_f", "time_f", "rep", "reg_a", "reg_b", "reg_l", "row_f", "pick", "pick_m", "by_in",
    "by_out", "by_in_t", "spread", "spread_m", "row_i", "reg_c", "time_i", "col_i",
)


def mm(a, b):
    return jnp.dot(a, b, preferred_element_type=F32)


def mm_full(a, b):
    return jnp.dot(a, b, preferred_element_type=F32, precision=lax.Precision.HIGHEST)


def gelu_slope(values):
    normal_cdf = 0.5 * (1.0 + lax.erf(values * (1.0 / math.sqrt(2.0))))
    density = jnp.exp(-0.5 * values * values) * (1.0 / math.sqrt(2.0 * math.pi))
    return normal_cdf + values * density


def pre_gradient(cot, pre):
    return (cot.astype(F32) * gelu_slope(pre.astype(F32))).astype(BF16)


def column_time(field, col_f, time_f):
    y = mm(col_f, field).astype(BF16)
    return mm(jnp.concatenate([y[:64], y[64:]], axis=1), time_f)


def group_mask(shape):
    row = lax.broadcasted_iota(jnp.int32, shape, 0)
    lane = lax.broadcasted_iota(jnp.int32, shape, 1)
    return row, lane


def pack_bypass(product, rep):
    row, lane = group_mask((256, 256))
    kept = jnp.where(row // C == lane // C, product, 0.0)
    wide = mm_full(kept, rep.astype(F32))
    wide = wide.reshape(8, C, 128).sum(0)
    row, lane = group_mask((C, 128))
    kept = jnp.where(row % 4 == lane // C, wide, 0.0)
    row, lane = group_mask((8, C))
    return mm_full(jnp.where(row == lane // 4, 1.0, 0.0), kept)


def unpack_bypass(packed):
    row, lane = group_mask((C, 8))
    wide = mm_full(jnp.where(row // 4 == lane, 1.0, 0.0), packed)
    row, lane = group_mask((C, 128))
    kept = jnp.where(row % 4 == lane // C, wide, 0.0)
    row, lane = group_mask((128, C))
    return mm_full(kept, jnp.where(row % C == lane, 1.0, 0.0)) * BYPASS_SCALE


def block_bypass(bypass):
    row, lane = group_mask((256, C))
    tall = jnp.where(row % C == lane, 1.0, 0.0).astype(BF16)
    row, lane = group_mask((C, 256))
    flat = jnp.where(lane % C == row, 1.0, 0.0).astype(BF16)
    turned = lax.dot_general(tall, bypass, (((1,), (1,)), ((), ())), preferred_element_type=F32)
    full = mm(turned.astype(BF16), flat)
    row, lane = group_mask((256, 256))
    return jnp.where(row // C == lane // C, full, 0.0).astype(BF16)


def regroup_forward(total, reg_a, reg_b, reg_l):
    rows = total.astype(BF16)
    turned = mm(rows, reg_l).astype(BF16)
    return mm(reg_a, rows) + mm(reg_b, turned)


def mixing(modes, w_re, w_im, pick, pick_m, by_in, by_out, by_in_t, spread, spread_m):
    chosen = (mm(pick, modes) * pick_m.astype(F32)).astype(BF16)
    a = mm(chosen[:160], by_in)
    g = mm(chosen[160:], by_out)
    a_re, a_im, g_re, g_im = a[:80], a[80:], g[:80], g[80:]
    out_re = FACTOR * (a_re * g_re + a_im * g_im)
    out_im = FACTOR * (a_re * g_im - a_im * g_re)
    p_re = w_re * g_re + w_im * g_im
    p_im = w_re * g_im - w_im * g_re
    b_re = mm(p_re.astype(BF16), by_in_t) * FACTOR
    b_im = mm(p_im.astype(BF16), by_in_t) * FACTOR
    stack = jnp.concatenate([b_re, b_im, b_im, b_re], axis=0) * spread_m.astype(F32)
    return out_re, out_im, mm(spread, stack.astype(BF16))


def final_rows(low_re, low_im, high, time_i, col_i):
    z = jnp.concatenate([low_re, low_im, high], axis=1)
    u = mm(z, time_i).astype(BF16)
    return mm(col_i, jnp.concatenate([u[:, :256], u[:, 256:]], axis=0))


def rows_of(block, count):
    return block.astype(F32).reshape(count, 128).astype(BF16)


def kernel(inp, pre, cot, spec, byp, *refs):
    n = len(ORDER)
    tables = dict(zip(ORDER, refs[:n]))
    out_g, out_s, out_b = refs[n : n + 3]
    held = dict(zip(ORDER, refs[n + 3 : 2 * n + 3]))
    (
        grad, plus, pieces, recv_col, send_s, recv_s, rows_all, send_x, recv_x, send_q, recv_q,
        send_b, recv_b, recv_g, send_l, recv_l, send_c, recv_c,
        sum_a, sum_b, sum_c, sum_d, by_a, by_b, by_c, by_d,
        table_sem, send_sem, recv_sem,
    ) = refs[2 * n + 3 :]

    row = lax.axis_index("row")
    j = lax.axis_index("col")
    xx = row // 16
    q = row % 16
    yy = q // 4
    zh = (q // 2) % 2
    core = q % 2
    s = yy * 2 + core

    def col_peer(k):
        return row, (j + k) % 8

    def s_index(k):
        return (s + k) % 8

    def s_peer(k):
        other = s_index(k)
        return xx * 16 + (other // 2) * 4 + zh * 2 + other % 2, j

    def zh_peer():
        return xx * 16 + yy * 4 + (1 - zh) * 2 + core, j

    def x_peer(k):
        return ((xx + k) % 4) * 16 + q, j

    def q_index(k):
        return (q + k) % 16

    def q_peer(k):
        return xx * 16 + q_index(k), j

    barrier = pltpu.get_barrier_semaphore()
    everyone = (
        [col_peer(k) for k in range(1, 8)]
        + [q_peer(k) for k in range(1, 16)]
        + [x_peer(k) for k in range(1, 4)]
    )
    for peer in everyone:
        pl.semaphore_signal(barrier, inc=1, device_id=peer, device_id_type=MESH)

    index_of = {"col_f": j, "col_i": j, "row_f": xx, "row_i": xx * 2 + zh}
    loads = {}
    for at, name in enumerate(ORDER):
        source = tables[name].at[index_of[name]] if name in PICKED else tables[name]
        loads[name] = pltpu.make_async_copy(source, held[name], table_sem.at[at])
        loads[name].start()

    def table(name):
        return held[name][...]

    sent = []

    def send(source, target, peer):
        at = len(sent)
        copy = pltpu.make_async_remote_copy(
            src_ref=source,
            dst_ref=target,
            send_sem=send_sem.at[at],
            recv_sem=recv_sem.at[at],
            device_id=peer,
            device_id_type=MESH,
        )
        copy.start()
        sent.append(copy)
        return copy

    def arrive(copies):
        for copy in copies:
            copy.wait_recv()

    loads["col_f"].wait()
    loads["time_f"].wait()
    col_f = table("col_f")
    high = []
    for x in range(4):
        r = column_time(inp[x], col_f, held["time_f"][0])
        pieces[:, 0, x] = r[:, :128].reshape(8, 8, 128).astype(BF16)
        pieces[:, 1, x] = r[:, 128:256].reshape(8, 8, 128).astype(BF16)
        high.append(r[:, 256:])
    pl.semaphore_wait(barrier, len(everyone))
    first = []
    for k in range(1, 8):
        to = (j + k) % 8
        first.append(send(pieces.at[to, 0:2], recv_col.at[k - 1, 0:2], col_peer(k)))
    for x in range(4):
        g = pre_gradient(cot[x], pre[x])
        grad[x] = g
        r = column_time(g, col_f, held["time_f"][1])
        pieces[:, 2, x] = r[:, :128].reshape(8, 8, 128).astype(BF16)
        pieces[:, 3, x] = r[:, 128:256].reshape(8, 8, 128).astype(BF16)
        pieces[:, 4, x] = (high[x] + r[:, 256:]).reshape(8, 8, 128).astype(BF16)
    for k in range(1, 8):
        to = (j + k) % 8
        first.append(send(pieces.at[to, 2:5], recv_col.at[k - 1, 2:5], col_peer(k)))

    product = jnp.zeros((256, 256), F32)
    for x in range(4):
        product += lax.dot_general(
            inp[x], grad[x], (((0,), (0,)), ((), ())), preferred_element_type=F32
        )
    loads["rep"].wait()
    by_a[j] = pack_bypass(product, table("rep"))
    bypass_a = [send(by_a.at[j], by_a.at[j], col_peer(k)) for k in range(1, 8)]
    blocks = block_bypass(byp[...])
    for x in range(4):
        plus[x] = mm(grad[x], blocks)

    for name in ("reg_a", "reg_b", "reg_l"):
        loads[name].wait()
    arrive(first)
    total = pieces[j].astype(F32).reshape(160, 128)
    for k in range(7):
        total += recv_col[k].astype(F32).reshape(160, 128)
    grouped = regroup_forward(total, table("reg_a"), table("reg_b"), table("reg_l"))
    send_s[...] = grouped.reshape(8, 3, 8, 128).astype(BF16)
    recv_s[s] = send_s[s]
    second = [send(send_s.at[s_index(k)], recv_s.at[s], s_peer(k)) for k in range(1, 8)]

    arrive(bypass_a)
    by_b[s] = by_a[...].sum(0)
    bypass_b = [send(by_b.at[s], by_b.at[s], s_peer(k)) for k in range(1, 8)]

    arrive(second)
    rows_all[0, zh] = recv_s[:, zh]
    rows_all[1, zh] = recv_s[:, 2]
    third = [
        send(recv_s.at[:, 1 - zh], rows_all.at[0, zh], zh_peer()),
        send(recv_s.at[:, 2], rows_all.at[1, zh], zh_peer()),
    ]
    arrive(bypass_b)
    by_c[zh] = by_b[...].sum(0)
    bypass_c = [send(by_c.at[zh], by_c.at[zh], zh_peer())]

    loads["row_f"].wait()
    arrive(third)
    partial = mm(table("row_f"), rows_of(rows_all[...], 256))
    send_x[...] = partial.reshape(4, 16, 8, 128).astype(BF16)
    fourth = [
        send(send_x.at[(xx + k) % 4], recv_x.at[k - 1], x_peer(k)) for k in range(1, 4)
    ]
    arrive(bypass_c)
    by_d[xx] = by_c[...].sum(0)
    bypass_d = [send(by_d.at[xx], by_d.at[xx], x_peer(k)) for k in range(1, 4)]
    arrive(fourth)
    summed = send_x[xx].astype(F32)
    for k in range(3):
        summed += recv_x[k].astype(F32)
    send_q[...] = summed.astype(BF16)

    recv_q[q] = send_q[q]
    fifth = [send(send_q.at[q_index(k)], recv_q.at[q], q_peer(k)) for k in range(1, 16)]
    for name in ("pick", "pick_m", "by_in", "by_out", "by_in_t", "spread", "spread_m"):
        loads[name].wait()
    arrive(bypass_d)
    out_b[...] = unpack_bypass(by_d[...].sum(0))
    arrive(fifth)
    out_re, out_im, back = mixing(
        rows_of(recv_q[...], 128),
        spec[0].astype(F32),
        spec[1].astype(F32),
        *[
            table(name)
            for name in ("pick", "pick_m", "by_in", "by_out", "by_in_t", "spread", "spread_m")
        ],
    )
    send_b[...] = back.reshape(8, 8, 128).astype(BF16)
    recv_b[q] = send_b[s]
    sixth = []
    for k in range(1, 16):
        to = q_index(k)
        sixth.append(send(send_b.at[(to // 4) * 2 + to % 2], recv_b.at[q], q_peer(k)))
    out_s[0] = out_re
    out_s[1] = out_im

    arrive(sixth)
    recv_g[xx] = recv_b[...]
    seventh = [send(recv_b, recv_g.at[xx], x_peer(k)) for k in range(1, 4)]
    loads["row_i"].wait()
    loads["reg_c"].wait()
    arrive(seventh)
    lines = mm(table("row_i"), rows_of(recv_g[...], 512))
    send_l[...] = lines.reshape(8, 16, 128).astype(BF16)
    recv_l[s] = send_l[s]
    eighth = [send(send_l.at[s_index(k)], recv_l.at[s], s_peer(k)) for k in range(1, 8)]
    arrive(eighth)
    turned = mm(table("reg_c"), rows_of(recv_l[...], 128))
    send_c[...] = turned.reshape(4, 3, 8, 128).astype(BF16)
    recv_c[j] = send_c[...]
    ninth = [send(send_c, recv_c.at[j], col_peer(k)) for k in range(1, 8)]
    loads["time_i"].wait()
    loads["col_i"].wait()
    time_i = table("time_i")
    col_i = table("col_i")
    arrive(ninth)
    for x in range(4):
        parts = [rows_of(recv_c[:, x, tile], 64) for tile in range(3)]
        out_g[x] = (final_rows(*parts, time_i, col_i) + plus[x]).astype(BF16)

    for copy in sent:
        copy.wait_send()


N_COPIES = 14 + 7 + 7 + 7 + 2 + 1 + 3 + 3 + 15 + 15 + 3 + 7 + 7


def local(inputs, preactivation, cotangent, spectral, bypass, tables):
    weight = spectral.transpose(0, 1, 3, 2, 4).reshape(2, 80, C * C)
    vmem = pl.BlockSpec(memory_space=pltpu.VMEM)
    anywhere = pl.BlockSpec(memory_space=pl.ANY)
    held = [
        pltpu.VMEM(tables[k].shape[1:] if k in PICKED else tables[k].shape, BF16) for k in ORDER
    ]
    blocks = [
        pltpu.VMEM((4, 128, 256), BF16),
        pltpu.VMEM((4, 128, 256), F32),
        pltpu.VMEM((8, 5, 4, 8, 128), BF16),
        pltpu.VMEM((7, 5, 4, 8, 128), BF16),
        pltpu.VMEM((8, 3, 8, 128), BF16),
        pltpu.VMEM((8, 3, 8, 128), BF16),
        pltpu.VMEM((2, 2, 8, 8, 128), BF16),
        pltpu.VMEM((4, 16, 8, 128), BF16),
        pltpu.VMEM((3, 16, 8, 128), BF16),
        pltpu.VMEM((16, 8, 128), BF16),
        pltpu.VMEM((16, 8, 128), BF16),
        pltpu.VMEM((8, 8, 128), BF16),
        pltpu.VMEM((16, 8, 128), BF16),
        pltpu.VMEM((4, 16, 8, 128), BF16),
        pltpu.VMEM((8, 16, 128), BF16),
        pltpu.VMEM((8, 16, 128), BF16),
        pltpu.VMEM((4, 3, 8, 128), BF16),
        pltpu.VMEM((8, 4, 3, 8, 128), BF16),
        pltpu.VMEM((8, 128), F32),
        pltpu.VMEM((8, 128), F32),
        pltpu.VMEM((8, 128), F32),
        pltpu.VMEM((8, 128), F32),
        pltpu.VMEM((8, 8, 128), F32),
        pltpu.VMEM((8, 8, 128), F32),
        pltpu.VMEM((2, 8, 128), F32),
        pltpu.VMEM((4, 8, 128), F32),
        pltpu.SemaphoreType.DMA((len(ORDER),)),
        pltpu.SemaphoreType.DMA((N_COPIES,)),
        pltpu.SemaphoreType.DMA((N_COPIES,)),
    ]
    grad_inputs, grad_weight, grad_bypass = pl.pallas_call(
        kernel,
        out_shape=(
            jax.ShapeDtypeStruct((4, 128, 256), BF16),
            jax.ShapeDtypeStruct((2, 80, C * C), F32),
            jax.ShapeDtypeStruct((C, C), F32),
        ),
        in_specs=[vmem] * 5 + [anywhere] * len(ORDER),
        out_specs=(vmem, vmem, vmem),
        scratch_shapes=held + blocks,
        compiler_params=pltpu.CompilerParams(
            collective_id=0, has_side_effects=True, vmem_limit_bytes=48 * 1024 * 1024
        ),
        name="fno_backward",
    )(inputs, preactivation, cotangent, weight, bypass, *[tables[k] for k in ORDER])
    grad_spectral = grad_weight.reshape(2, 2, 5, 8, C * C).transpose(0, 1, 3, 2, 4)
    return (grad_inputs, grad_spectral, grad_bypass)


def solution(mesh):
    tables = make_tables()

    def step(*args):
        return local(*args, {k: jnp.asarray(v) for k, v in tables.items()})

    return jax.shard_map(
        step,
        mesh=mesh,
        in_specs=(
            P("row", "col", None),
            P("row", "col", None),
            P("row", "col", None),
            P(None, "row", "col", None, None),
            P(),
        ),
        out_specs=(P("row", "col", None), P(None, "row", "col", None, None), P()),
        check_vma=False,
    )
```

```python
import math

import jax
import jax.numpy as jnp
import numpy as np
from jax import lax
from jax.experimental import pallas as pl
from jax.experimental.pallas import tpu as pltpu
from jax.sharding import PartitionSpec as P

MESH = pl.DeviceIdType.MESH
F32 = jnp.float32
BF16 = jnp.bfloat16
NX, NY, NT, C = 256, 1024, 8, 32
KX, KY, KT = 128, 64, 5
FACTOR = 1.0 / math.sqrt(float(NX * NY * NT * KX * KY * KT))
BYPASS_SCALE = 1.0 / math.sqrt(float(NX * NY * NT))


def turns(a, b, n):
    angle = 2.0 * np.pi * (np.multiply.outer(a, b) % n) / n
    return np.cos(angle), np.sin(angle)


def column_tables():
    forward, inverse = [], []
    for j in range(8):
        cos, sin = turns(np.arange(64), 128 * j + np.arange(128), NY)
        forward.append(np.concatenate([cos, -sin], 0))
        inverse.append(np.concatenate([cos.T, -sin.T], 1))
    return np.stack(forward), np.stack(inverse)


def time_tables():
    cos, sin = turns(np.arange(NT), np.arange(KT), NT)
    eye = np.eye(C)
    low = np.zeros((2, NT, C, 2, 4, C))
    for t in range(NT):
        for k in range(4):
            low[0, t, :, 0, k, :] = eye * cos[t, k]
            low[1, t, :, 0, k, :] = eye * sin[t, k]
            low[0, t, :, 1, k, :] = -eye * sin[t, k]
            low[1, t, :, 1, k, :] = eye * cos[t, k]
    high = np.zeros((2, 2, NT, C, 2, 2, C))
    for f in range(2):
        for t in range(NT):
            high[f, 0, t, :, f, 0, :] = eye * cos[t, 4]
            high[f, 1, t, :, f, 1, :] = eye * cos[t, 4]
    forward = np.concatenate(
        [low.reshape(512, 256), high[0].reshape(512, 128), high[1].reshape(512, 128)], 1
    )
    inverse = np.zeros((3, 4, C, 2, NT, C))
    for t in range(NT):
        for k in range(4):
            inverse[0, k, :, 0, t, :] = eye * cos[t, k]
            inverse[1, k, :, 0, t, :] = -eye * sin[t, k]
            inverse[0, k, :, 1, t, :] = eye * sin[t, k]
            inverse[1, k, :, 1, t, :] = eye * cos[t, k]
        inverse[2, 0, :, 0, t, :] = eye * cos[t, 4]
        inverse[2, 1, :, 1, t, :] = eye * cos[t, 4]
    return forward, inverse.reshape(384, 512)


def regroup_tables():
    direct = np.zeros((8, 3, 2, 4, 5, 4, 8))
    swapped = np.zeros((8, 3, 2, 4, 5, 4, 8))
    back = np.zeros((4, 3, 8, 8, 2, 2, 4))
    for k in range(8):
        for x in range(4):
            for tile in range(5):
                direct[k, tile // 2, tile % 2, x, tile, x, k] = 1.0
            swapped[k, 2, 1, x, 4, x, k] = 1.0
            for tile in range(3):
                back[x, tile, k, k, tile // 2, tile % 2, x] = 1.0
    lanes = np.zeros((2, 2, C, 2, 2, C))
    for f in range(2):
        lanes[f, 1, :, f, 0, :] = np.eye(C)
        lanes[f, 0, :, f, 1, :] = -np.eye(C)
    return (
        direct.reshape(192, 160),
        swapped.reshape(192, 160),
        lanes.reshape(128, 128),
        back.reshape(96, 128),
    )


def row_tables():
    k = np.arange(KX)
    freq = np.where(k < KX // 2, k, k - KX) % NX
    cos, sin = turns(freq, np.arange(NX), NX)
    cos = cos.reshape(4, 16, 2, 4, 4, 2, 2, 4)
    sin = sin.reshape(4, 16, 2, 4, 4, 2, 2, 4)
    forward = np.zeros((4, 4, 16, 2, 2, 2, 2, 2, 4, 2, 2, 4))
    for xx in range(4):
        for slab in range(2):
            c = cos[:, :, :, xx].transpose(0, 1, 2, 4, 3, 5, 6)
            s = sin[:, :, :, xx].transpose(0, 1, 2, 4, 3, 5, 6)
            forward[xx, :, :, slab, :, 0, slab, :, :, :, 0, :] = c
            forward[xx, :, :, slab, :, 0, slab, :, :, :, 1, :] = s
            forward[xx, :, :, slab, :, 1, slab, :, :, :, 1, :] = c
            forward[xx, :, :, slab, :, 1, slab, :, :, :, 0, :] = -s
    forward = forward.reshape(4, 512, 256)
    inverse = np.zeros((4, 2, 4, 2, 2, 2, 4, 4, 16, 2, 2, 2))
    for xx in range(4):
        for zh in range(2):
            for slab in range(2):
                c = cos[:, :, :, xx, :, zh].transpose(3, 4, 5, 0, 1, 2)
                s = sin[:, :, :, xx, :, zh].transpose(3, 4, 5, 0, 1, 2)
                inverse[xx, zh, :, :, slab, 0, :, :, :, slab, :, 0] = c
                inverse[xx, zh, :, :, slab, 0, :, :, :, slab, :, 1] = -s
                inverse[xx, zh, :, :, slab, 1, :, :, :, slab, :, 1] = c
                inverse[xx, zh, :, :, slab, 1, :, :, :, slab, :, 0] = s
    return forward, inverse.reshape(8, 128, 512)


def mixing_tables():
    pick = np.zeros((2, 2, 2, 5, 8, 16, 2, 2, 2))
    pick_mask = np.zeros((2, 2, 2, 5, 8, 4, C))
    spread = np.zeros((8, 2, 2, 2, 4, 2, 5, 8))
    spread_mask = np.zeros((4, 2, 5, 8, 4, C))
    for ky in range(8):
        for e in range(2):
            for f in range(2):
                source = (ky // 2) * 4 + f * 2 + ky % 2
                for ri in range(2):
                    for kt in range(4):
                        pick[f, ri, e, kt, ky, source, 0, e, ri] = 1.0
                        pick_mask[f, ri, e, kt, ky, kt, :] = 1.0
                    pick[f, ri, e, 4, ky, source, 1, e, 0] = 1.0
                    pick_mask[f, ri, e, 4, ky, f * 2 + ri, :] = 1.0
            for kt in range(4):
                spread_mask[0, e, kt, ky, kt] = 1.0
                spread_mask[1, e, kt, ky, kt] = 1.0
                spread[ky, 0, e, 0, 0, e, kt, ky] = 1.0
                spread[ky, 0, e, 1, 1, e, kt, ky] = 1.0
            spread_mask[0, e, 4, ky, 0] = 1.0
            spread_mask[1, e, 4, ky, 1] = 1.0
            spread_mask[2, e, 4, ky, 0] = 1.0
            spread_mask[3, e, 4, ky, 1] = 1.0
            spread[ky, 1, e, 0, 0, e, 4, ky] = 1.0
            spread[ky, 1, e, 0, 1, e, 4, ky] = 1.0
            spread[ky, 1, e, 1, 2, e, 4, ky] = 1.0
            spread[ky, 1, e, 1, 3, e, 4, ky] = -1.0
    group = np.arange(128) % C
    lane = np.arange(C * C)
    by_in = (group[:, None] == lane[None, :] // C).astype(np.float64)
    by_out = (group[:, None] == lane[None, :256] % C).astype(np.float64)
    return (
        pick.reshape(320, 128),
        pick_mask.reshape(320, 128),
        by_in,
        by_out,
        by_in.T,
        spread.reshape(64, 320),
        spread_mask.reshape(320, 128),
    )


def make_tables():
    t = {}
    t["col_f"], t["col_i"] = column_tables()
    t["time_f"], t["time_i"] = time_tables()
    t["reg_a"], t["reg_b"], t["reg_l"], t["reg_c"] = regroup_tables()
    t["row_f"], t["row_i"] = row_tables()
    t["pick"], t["pick_m"], t["by_in"], t["by_out"], t["by_in_t"], t["spread"], t["spread_m"] = (
        mixing_tables()
    )
    return {k: np.asarray(v, np.float32).astype(jnp.bfloat16) for k, v in t.items()}


PICKED = ("col_f", "col_i", "row_f", "row_i")
ORDER = (
    "col_f", "time_f", "reg_a", "reg_b", "reg_l", "row_f", "pick", "pick_m", "by_in",
    "by_out", "by_in_t", "spread", "spread_m", "row_i", "reg_c", "time_i", "col_i",
)


def mm(a, b):
    return jnp.dot(a, b, preferred_element_type=F32)


def mm_full(a, b):
    return jnp.dot(a, b, preferred_element_type=F32, precision=lax.Precision.HIGHEST)


def gelu_slope(values):
    normal_cdf = 0.5 * (1.0 + lax.erf(values * (1.0 / math.sqrt(2.0))))
    density = jnp.exp(-0.5 * values * values) * (1.0 / math.sqrt(2.0 * math.pi))
    return normal_cdf + values * density


def pre_gradient(cot, pre):
    return (cot.astype(F32) * gelu_slope(pre.astype(F32))).astype(BF16)


def group_mask(shape):
    row = lax.broadcasted_iota(jnp.int32, shape, 0)
    lane = lax.broadcasted_iota(jnp.int32, shape, 1)
    return row, lane


def fold_lanes(values):
    values = values + pltpu.roll(values, 64, 1)
    return values + pltpu.roll(values, 32, 1)


def pack_bypass(product):
    row, lane = group_mask((256, 256))
    kept = jnp.where(row // C == lane // C, product, 0.0).reshape(8, C, 256).sum(0)
    wide = fold_lanes(kept[:, :128] + kept[:, 128:])
    row, lane = group_mask((C, 128))
    kept = jnp.where(row % 4 == lane // C, wide, 0.0)
    row, lane = group_mask((8, C))
    return mm_full(jnp.where(row == lane // 4, 1.0, 0.0), kept)


def unpack_bypass(packed):
    row, lane = group_mask((C, 8))
    wide = mm_full(jnp.where(row // 4 == lane, 1.0, 0.0), packed)
    row, lane = group_mask((C, 128))
    kept = fold_lanes(jnp.where(row % 4 == lane // C, wide, 0.0))
    return kept[:, :C] * BYPASS_SCALE


def block_bypass(bypass):
    row, lane = group_mask((256, C))
    tall = jnp.where(row % C == lane, 1.0, 0.0).astype(BF16)
    row, lane = group_mask((C, 256))
    flat = jnp.where(lane % C == row, 1.0, 0.0).astype(BF16)
    turned = lax.dot_general(tall, bypass, (((1,), (1,)), ((), ())), preferred_element_type=F32)
    full = mm(turned.astype(BF16), flat)
    row, lane = group_mask((256, 256))
    return jnp.where(row // C == lane // C, full, 0.0).astype(BF16)


def regroup_forward(total, reg_a, reg_b, reg_l):
    rows = total.astype(BF16)
    turned = mm(rows, reg_l).astype(BF16)
    return mm(reg_a, rows) + mm(reg_b, turned)


def final_rows(low_re, low_im, high, time_i, col_i):
    z = jnp.concatenate([low_re, low_im, high], axis=1)
    u = mm(z, time_i).astype(BF16)
    return mm(col_i, jnp.concatenate([u[:, :256], u[:, 256:]], axis=0))


def rows_of(block, count):
    return block.astype(F32).reshape(count, 128).astype(BF16)


def kernel(inp_hbm, pre_hbm, cot_hbm, spec_hbm, byp_hbm, *refs):
    n = len(ORDER)
    tables = dict(zip(ORDER, refs[:n]))
    out_g_hbm, out_s_hbm, out_b = refs[n : n + 3]
    held = dict(zip(ORDER, refs[n + 3 : 2 * n + 3]))
    (
        inp, pre, cot, spec, byp, out_g, out_s, arg_sem, out_sem,
        grad, plus, pieces, recv_col, send_s, recv_s, rows_all, send_x, recv_x, send_q, recv_q,
        send_b, recv_b, recv_g, send_l, recv_l, send_c, recv_c,
        sum_a, sum_b, sum_c, sum_d, by_a, by_b, by_c, by_d,
        lined, high, product, blocks, chosen, repeated,
        table_sem, send_sem, recv_sem,
    ) = refs[2 * n + 3 :]

    row = lax.axis_index("row")
    j = lax.axis_index("col")
    xx = row // 16
    q = row % 16
    yy = q // 4
    zh = (q // 2) % 2
    core = q % 2
    s = yy * 2 + core

    def col_peer(k):
        return row, (j + k) % 8

    def s_index(k):
        return (s + k) % 8

    def s_peer(k):
        other = s_index(k)
        return xx * 16 + (other // 2) * 4 + zh * 2 + other % 2, j

    def zh_peer():
        return xx * 16 + yy * 4 + (1 - zh) * 2 + core, j

    def x_peer(k):
        return ((xx + k) % 4) * 16 + q, j

    def q_index(k):
        return (q + k) % 16

    def q_peer(k):
        return xx * 16 + q_index(k), j

    barrier = pltpu.get_barrier_semaphore()
    everyone = (
        [col_peer(k) for k in range(1, 8)]
        + [q_peer(k) for k in range(1, 16)]
        + [x_peer(k) for k in range(1, 4)]
    )
    for peer in everyone:
        pl.semaphore_signal(barrier, inc=1, device_id=peer, device_id_type=MESH)

    index_of = {"col_f": j, "col_i": j, "row_f": xx, "row_i": xx * 2 + zh}
    loads = {}

    def load(name):
        source = tables[name].at[index_of[name]] if name in PICKED else tables[name]
        loads[name] = pltpu.make_async_copy(source, held[name], table_sem.at[ORDER.index(name)])
        loads[name].start()

    args = []
    for at, (source, target) in enumerate(
        ((inp_hbm, inp), (cot_hbm, cot), (pre_hbm, pre), (byp_hbm, byp), (spec_hbm, spec))
    ):
        args.append(pltpu.make_async_copy(source, target, arg_sem.at[at]))
    args[0].start()
    load("col_f")
    load("time_f")
    args[1].start()
    args[2].start()
    args[3].start()
    args[4].start()
    for name in ORDER[2:]:
        load(name)

    def table(name):
        return held[name][...]

    exchanges = []
    used = [0]

    def exchange(count, make):
        base = used[0]
        used[0] += count

        def copy(k):
            source, target, peer = make(k)
            return pltpu.make_async_remote_copy(
                src_ref=source,
                dst_ref=target,
                send_sem=send_sem.at[base + k],
                recv_sem=recv_sem.at[base + k],
                device_id=peer,
                device_id_type=MESH,
            )

        def start(k, carry):
            copy(k).start()
            return carry

        lax.fori_loop(0, count, start, 0)
        pair = copy, count
        exchanges.append(pair)
        return pair

    def arrive(pair, first=0, last=None):
        copy, count = pair

        def wait(k, carry):
            copy(k).wait_recv()
            return carry

        lax.fori_loop(first, count if last is None else last, wait, 0)

    loads["col_f"].wait()
    args[0].wait()

    def lines_in(x, carry):
        y = mm(held["col_f"][...], inp[x]).astype(BF16)
        lined[x, :, 0:256] = y[:64]
        lined[x, :, 256:512] = y[64:]
        return carry

    lax.fori_loop(0, 4, lines_in, 0)
    loads["time_f"].wait()
    r = mm(lined[...].reshape(256, 512), held["time_f"][:, 0:384])
    for x in range(4):
        rows = slice(64 * x, 64 * x + 64)
        pieces[:, 0, x] = r[rows, :128].reshape(8, 8, 128).astype(BF16)
        pieces[:, 1, x] = r[rows, 128:256].reshape(8, 8, 128).astype(BF16)
    high[...] = r[:, 256:]
    pl.semaphore_wait(barrier, len(everyone))
    first_in = exchange(
        7,
        lambda k: (
            pieces.at[(j + k + 1) % 8, 0:2],
            recv_col.at[k, 0:2],
            col_peer(k + 1),
        ),
    )
    args[1].wait()
    args[2].wait()

    def lines_grad(x, carry):
        g = pre_gradient(cot[x], pre[x])
        grad[x] = g
        y = mm(held["col_f"][...], g).astype(BF16)
        lined[x, :, 0:256] = y[:64]
        lined[x, :, 256:512] = y[64:]
        return carry

    lax.fori_loop(0, 4, lines_grad, 0)
    rows = lined[...].reshape(256, 512)
    r = mm(rows, held["time_f"][:, 0:256])
    top = high[...] + mm(rows, held["time_f"][:, 384:512])
    for x in range(4):
        rows = slice(64 * x, 64 * x + 64)
        pieces[:, 2, x] = r[rows, :128].reshape(8, 8, 128).astype(BF16)
        pieces[:, 3, x] = r[rows, 128:].reshape(8, 8, 128).astype(BF16)
        pieces[:, 4, x] = top[rows].reshape(8, 8, 128).astype(BF16)
    first_grad = exchange(
        7,
        lambda k: (
            pieces.at[(j + k + 1) % 8, 2:5],
            recv_col.at[k, 2:5],
            col_peer(k + 1),
        ),
    )

    product[...] = jnp.zeros((256, 256), F32)

    def add_product(x, carry):
        product[...] += lax.dot_general(
            inp[x], grad[x], (((0,), (0,)), ((), ())), preferred_element_type=F32
        )
        return carry

    lax.fori_loop(0, 4, add_product, 0)
    by_a[j] = pack_bypass(product[...])
    bypass_a = exchange(7, lambda k: (by_a.at[j], by_a.at[j], col_peer(k + 1)))
    args[3].wait()
    blocks[...] = block_bypass(byp[...])

    def pointwise(x, carry):
        plus[x] = mm(grad[x], blocks[...])
        return carry

    lax.fori_loop(0, 4, pointwise, 0)

    for name in ("reg_a", "reg_b", "reg_l"):
        loads[name].wait()
    arrive(first_in)
    arrive(first_grad)
    total = pieces[j].astype(F32).reshape(160, 128)
    for k in range(7):
        total += recv_col[k].astype(F32).reshape(160, 128)
    grouped = regroup_forward(total, table("reg_a"), table("reg_b"), table("reg_l"))
    send_s[...] = grouped.reshape(8, 3, 8, 128).astype(BF16)
    recv_s[s] = send_s[s]
    second = exchange(7, lambda k: (send_s.at[s_index(k + 1)], recv_s.at[s], s_peer(k + 1)))

    arrive(bypass_a)
    by_b[s] = by_a[...].sum(0)
    bypass_b = exchange(7, lambda k: (by_b.at[s], by_b.at[s], s_peer(k + 1)))

    arrive(second)
    third_a = exchange(1, lambda k: (recv_s.at[:, 1 - zh], rows_all.at[0, zh], zh_peer()))
    third_b = exchange(1, lambda k: (recv_s.at[:, 2], rows_all.at[1, zh], zh_peer()))
    rows_all[0, zh] = recv_s[:, zh]
    rows_all[1, zh] = recv_s[:, 2]
    arrive(bypass_b)
    by_c[zh] = by_b[...].sum(0)
    bypass_c = exchange(1, lambda k: (by_c.at[zh], by_c.at[zh], zh_peer()))

    loads["row_f"].wait()
    arrive(third_a)
    arrive(third_b)
    partial = mm(table("row_f"), rows_of(rows_all[...], 256))
    send_x[...] = partial.reshape(4, 16, 8, 128).astype(BF16)
    fourth = exchange(
        3, lambda k: (send_x.at[(xx + k + 1) % 4], recv_x.at[k], x_peer(k + 1))
    )
    arrive(bypass_c)
    by_d[xx] = by_c[...].sum(0)
    bypass_d = exchange(3, lambda k: (by_d.at[xx], by_d.at[xx], x_peer(k + 1)))
    arrive(fourth)
    summed = send_x[xx].astype(F32)
    for k in range(3):
        summed += recv_x[k].astype(F32)
    send_q[...] = summed.astype(BF16)

    fifth = exchange(15, lambda k: (send_q.at[q_index(k + 1)], recv_q.at[q], q_peer(k + 1)))
    recv_q[q] = send_q[q]
    for name in ("pick", "pick_m", "by_in", "by_out", "by_in_t", "spread", "spread_m"):
        loads[name].wait()
    args[4].wait()
    arrive(bypass_d)
    out_b[...] = unpack_bypass(by_d[...].sum(0))
    arrive(fifth)
    chosen[...] = (mm(table("pick"), rows_of(recv_q[...], 128)) * table("pick_m").astype(F32)).astype(BF16)
    repeated[...] = mm(chosen[160:320, :], table("by_out"))

    def mix(m, carry):
        lanes = pl.ds(pl.multiple_of(m * 256, 256), 256)
        a = mm(chosen[0:160, :], held["by_in"][:, lanes])
        a_re, a_im = a[:80], a[80:]
        g_re = repeated[0:80, :]
        g_im = repeated[80:160, :]
        w_re = spec[0, :, lanes].astype(F32)
        w_im = spec[1, :, lanes].astype(F32)
        out_s[0, :, lanes] = FACTOR * (a_re * g_re + a_im * g_im)
        out_s[1, :, lanes] = FACTOR * (a_re * g_im - a_im * g_re)
        p_re = (w_re * g_re + w_im * g_im).astype(BF16)
        p_im = (w_re * g_im - w_im * g_re).astype(BF16)
        turn = held["by_in_t"][lanes, :]
        return carry + mm(jnp.concatenate([p_re, p_im], axis=0), turn)

    b = lax.fori_loop(0, 4, mix, jnp.zeros((160, 128), F32)) * FACTOR
    b_re, b_im = b[:80], b[80:]
    stack = jnp.concatenate([b_re, b_im, b_im, b_re], axis=0) * table("spread_m").astype(F32)
    back = mm(table("spread"), stack.astype(BF16))
    send_b[...] = back.reshape(8, 8, 128).astype(BF16)

    def mode_home(k):
        to = q_index(k + 1)
        return send_b.at[(to // 4) * 2 + to % 2], recv_b.at[q], q_peer(k + 1)

    sixth = exchange(15, mode_home)
    recv_b[q] = send_b[s]
    out_copy_s = pltpu.make_async_copy(out_s, out_s_hbm, out_sem.at[4])
    out_copy_s.start()

    arrive(sixth)
    seventh = exchange(3, lambda k: (recv_b, recv_g.at[xx], x_peer(k + 1)))
    recv_g[xx] = recv_b[...]
    loads["row_i"].wait()
    loads["reg_c"].wait()
    arrive(seventh)
    lines = mm(table("row_i"), rows_of(recv_g[...], 512))
    send_l[...] = lines.reshape(8, 16, 128).astype(BF16)
    eighth = exchange(7, lambda k: (send_l.at[s_index(k + 1)], recv_l.at[s], s_peer(k + 1)))
    recv_l[s] = send_l[s]
    arrive(eighth)
    turned = mm(table("reg_c"), rows_of(recv_l[...], 128))
    send_c[...] = turned.reshape(4, 3, 8, 128).astype(BF16)
    ninth = exchange(
        14,
        lambda k: (
            send_c.at[pl.ds((k // 7) * 2, 2)],
            recv_c.at[j, pl.ds((k // 7) * 2, 2)],
            col_peer(k % 7 + 1),
        ),
    )
    recv_c[j] = send_c[...]
    loads["time_i"].wait()
    loads["col_i"].wait()

    def out_copy(x):
        return pltpu.make_async_copy(out_g.at[x], out_g_hbm.at[x], out_sem.at[x])

    def final(x, carry):
        parts = [rows_of(recv_c[:, x, tile], 64) for tile in range(3)]
        rows = final_rows(*parts, held["time_i"][...], held["col_i"][...])
        out_g[x] = (rows + plus[x]).astype(BF16)
        out_copy(x).start()
        return carry

    for half in range(2):
        arrive(ninth, 7 * half, 7 * half + 7)
        lax.fori_loop(2 * half, 2 * half + 2, final, 0)

    for copy, count in exchanges:

        def drain(k, carry, copy=copy):
            copy(k).wait_send()
            return carry

        lax.fori_loop(0, count, drain, 0)
    for x in range(4):
        out_copy(x).wait()
    out_copy_s.wait()


N_COPIES = 14 + 7 + 7 + 7 + 2 + 1 + 3 + 3 + 15 + 15 + 3 + 7 + 14


def local(inputs, preactivation, cotangent, spectral, bypass, tables):
    weight = spectral.transpose(0, 1, 3, 2, 4).reshape(2, 80, C * C)
    vmem = pl.BlockSpec(memory_space=pltpu.VMEM)
    anywhere = pl.BlockSpec(memory_space=pl.ANY)
    held = [
        pltpu.VMEM(tables[k].shape[1:] if k in PICKED else tables[k].shape, BF16) for k in ORDER
    ]
    blocks = [
        pltpu.VMEM((4, 128, 256), BF16),
        pltpu.VMEM((4, 128, 256), BF16),
        pltpu.VMEM((4, 128, 256), BF16),
        pltpu.VMEM((2, 80, C * C), BF16),
        pltpu.VMEM((C, C), BF16),
        pltpu.VMEM((4, 128, 256), BF16),
        pltpu.VMEM((2, 80, C * C), F32),
        pltpu.SemaphoreType.DMA((5,)),
        pltpu.SemaphoreType.DMA((5,)),
        pltpu.VMEM((4, 128, 256), BF16),
        pltpu.VMEM((4, 128, 256), F32),
        pltpu.VMEM((8, 5, 4, 8, 128), BF16),
        pltpu.VMEM((7, 5, 4, 8, 128), BF16),
        pltpu.VMEM((8, 3, 8, 128), BF16),
        pltpu.VMEM((8, 3, 8, 128), BF16),
        pltpu.VMEM((2, 2, 8, 8, 128), BF16),
        pltpu.VMEM((4, 16, 8, 128), BF16),
        pltpu.VMEM((3, 16, 8, 128), BF16),
        pltpu.VMEM((16, 8, 128), BF16),
        pltpu.VMEM((16, 8, 128), BF16),
        pltpu.VMEM((8, 8, 128), BF16),
        pltpu.VMEM((16, 8, 128), BF16),
        pltpu.VMEM((4, 16, 8, 128), BF16),
        pltpu.VMEM((8, 16, 128), BF16),
        pltpu.VMEM((8, 16, 128), BF16),
        pltpu.VMEM((4, 3, 8, 128), BF16),
        pltpu.VMEM((8, 4, 3, 8, 128), BF16),
        pltpu.VMEM((8, 128), F32),
        pltpu.VMEM((8, 128), F32),
        pltpu.VMEM((8, 128), F32),
        pltpu.VMEM((8, 128), F32),
        pltpu.VMEM((8, 8, 128), F32),
        pltpu.VMEM((8, 8, 128), F32),
        pltpu.VMEM((2, 8, 128), F32),
        pltpu.VMEM((4, 8, 128), F32),
        pltpu.VMEM((4, 64, 512), BF16),
        pltpu.VMEM((256, 128), F32),
        pltpu.VMEM((256, 256), F32),
        pltpu.VMEM((256, 256), BF16),
        pltpu.VMEM((320, 128), BF16),
        pltpu.VMEM((160, 256), F32),
        pltpu.SemaphoreType.DMA((len(ORDER),)),
        pltpu.SemaphoreType.DMA((N_COPIES,)),
        pltpu.SemaphoreType.DMA((N_COPIES,)),
    ]
    grad_inputs, grad_weight, grad_bypass = pl.pallas_call(
        kernel,
        out_shape=(
            jax.ShapeDtypeStruct((4, 128, 256), BF16),
            jax.ShapeDtypeStruct((2, 80, C * C), F32),
            jax.ShapeDtypeStruct((C, C), F32),
        ),
        in_specs=[anywhere] * (5 + len(ORDER)),
        out_specs=(anywhere, anywhere, vmem),
        scratch_shapes=held + blocks,
        compiler_params=pltpu.CompilerParams(
            collective_id=0, has_side_effects=True, vmem_limit_bytes=62 * 1024 * 1024
        ),
        name="fno_backward",
    )(inputs, preactivation, cotangent, weight, bypass, *[tables[k] for k in ORDER])
    grad_spectral = grad_weight.reshape(2, 2, 5, 8, C * C).transpose(0, 1, 3, 2, 4)
    return (grad_inputs, grad_spectral, grad_bypass)


def solution(mesh):
    tables = make_tables()

    def step(*args):
        return local(*args, {k: jnp.asarray(v) for k, v in tables.items()})

    return jax.shard_map(
        step,
        mesh=mesh,
        in_specs=(
            P("row", "col", None),
            P("row", "col", None),
            P("row", "col", None),
            P(None, "row", "col", None, None),
            P(),
        ),
        out_specs=(P("row", "col", None), P(None, "row", "col", None, None), P()),
        check_vma=False,
    )
```

```python
import math

import jax
import jax.numpy as jnp
import numpy as np
from jax import lax
from jax.experimental import pallas as pl
from jax.experimental.pallas import tpu as pltpu
from jax.sharding import PartitionSpec as P

MESH = pl.DeviceIdType.MESH
F32 = jnp.float32
BF16 = jnp.bfloat16
NX, NY, NT, C = 256, 1024, 8, 32
KX, KY, KT = 128, 64, 5
FACTOR = 1.0 / math.sqrt(float(NX * NY * NT * KX * KY * KT))
BYPASS_SCALE = 1.0 / math.sqrt(float(NX * NY * NT))


def turns(a, b, n):
    angle = 2.0 * np.pi * (np.multiply.outer(a, b) % n) / n
    return np.cos(angle), np.sin(angle)


def column_tables():
    forward, inverse = [], []
    for j in range(8):
        cos, sin = turns(np.arange(64), 128 * j + np.arange(128), NY)
        forward.append(np.concatenate([cos, -sin], 0))
        inverse.append(np.concatenate([cos.T, -sin.T], 1))
    return np.stack(forward), np.stack(inverse)


def time_tables():
    cos, sin = turns(np.arange(NT), np.arange(KT), NT)
    eye = np.eye(C)
    low = np.zeros((2, NT, C, 2, 4, C))
    for t in range(NT):
        for k in range(4):
            low[0, t, :, 0, k, :] = eye * cos[t, k]
            low[1, t, :, 0, k, :] = eye * sin[t, k]
            low[0, t, :, 1, k, :] = -eye * sin[t, k]
            low[1, t, :, 1, k, :] = eye * cos[t, k]
    high = np.zeros((2, 2, NT, C, 2, 2, C))
    for f in range(2):
        for t in range(NT):
            high[f, 0, t, :, f, 0, :] = eye * cos[t, 4]
            high[f, 1, t, :, f, 1, :] = eye * cos[t, 4]
    forward = np.concatenate(
        [low.reshape(512, 256), high[0].reshape(512, 128), high[1].reshape(512, 128)], 1
    )
    inverse = np.zeros((3, 4, C, 2, NT, C))
    for t in range(NT):
        for k in range(4):
            inverse[0, k, :, 0, t, :] = eye * cos[t, k]
            inverse[1, k, :, 0, t, :] = -eye * sin[t, k]
            inverse[0, k, :, 1, t, :] = eye * sin[t, k]
            inverse[1, k, :, 1, t, :] = eye * cos[t, k]
        inverse[2, 0, :, 0, t, :] = eye * cos[t, 4]
        inverse[2, 1, :, 1, t, :] = eye * cos[t, 4]
    return forward, inverse.reshape(384, 512)


def regroup_tables():
    direct = np.zeros((8, 3, 2, 4, 5, 4, 8))
    swapped = np.zeros((8, 3, 2, 4, 5, 4, 8))
    back = np.zeros((4, 3, 8, 8, 2, 2, 4))
    for k in range(8):
        for x in range(4):
            for tile in range(5):
                direct[k, tile // 2, tile % 2, x, tile, x, k] = 1.0
            swapped[k, 2, 1, x, 4, x, k] = 1.0
            for tile in range(3):
                back[x, tile, k, k, tile // 2, tile % 2, x] = 1.0
    lanes = np.zeros((2, 2, C, 2, 2, C))
    for f in range(2):
        lanes[f, 1, :, f, 0, :] = np.eye(C)
        lanes[f, 0, :, f, 1, :] = -np.eye(C)
    return (
        direct.reshape(192, 160),
        swapped.reshape(192, 160),
        lanes.reshape(128, 128),
        back.reshape(96, 128),
    )


def row_tables():
    k = np.arange(KX)
    freq = np.where(k < KX // 2, k, k - KX) % NX
    cos, sin = turns(freq, np.arange(NX), NX)
    cos = cos.reshape(4, 16, 2, 4, 4, 2, 2, 4)
    sin = sin.reshape(4, 16, 2, 4, 4, 2, 2, 4)
    forward = np.zeros((4, 2, 4, 16, 2, 2, 4, 2, 2, 4))
    for xx in range(4):
        for zh in range(2):
            c = cos[:, :, :, xx, :, zh]
            s = sin[:, :, :, xx, :, zh]
            forward[xx, zh, :, :, :, 0, :, :, 0, :] = c
            forward[xx, zh, :, :, :, 0, :, :, 1, :] = s
            forward[xx, zh, :, :, :, 1, :, :, 1, :] = c
            forward[xx, zh, :, :, :, 1, :, :, 0, :] = -s
    forward = forward.reshape(8, 256, 64)
    deal = np.zeros((16, 16, 3, 16, 2, 2))
    for q in range(16):
        for e in range(2):
            for ab in range(2):
                for slab in range(2):
                    deal[q, slab * 4 + e * 2 + ab, slab, q, e, ab] = 1.0
            deal[q, 8 + e, 2, q, e, 0] = 1.0
    inverse = np.zeros((4, 2, 4, 2, 2, 2, 4, 4, 16, 2, 2, 2))
    for xx in range(4):
        for zh in range(2):
            for slab in range(2):
                c = cos[:, :, :, xx, :, zh].transpose(3, 4, 5, 0, 1, 2)
                s = sin[:, :, :, xx, :, zh].transpose(3, 4, 5, 0, 1, 2)
                inverse[xx, zh, :, :, slab, 0, :, :, :, slab, :, 0] = c
                inverse[xx, zh, :, :, slab, 0, :, :, :, slab, :, 1] = -s
                inverse[xx, zh, :, :, slab, 1, :, :, :, slab, :, 1] = c
                inverse[xx, zh, :, :, slab, 1, :, :, :, slab, :, 0] = s
    return forward, inverse.reshape(8, 128, 512), deal.reshape(256, 192)


def mixing_tables():
    pick = np.zeros((2, 2, 2, 5, 8, 16, 16))
    pick_mask = np.zeros((2, 2, 2, 5, 8, 4, C))
    spread = np.zeros((8, 2, 2, 2, 4, 2, 5, 8))
    spread_mask = np.zeros((4, 2, 5, 8, 4, C))
    for ky in range(8):
        for e in range(2):
            for f in range(2):
                for ri in range(2):
                    for kt in range(4):
                        pick_mask[f, ri, e, kt, ky, kt, :] = 1.0
                    pick_mask[f, ri, e, 4, ky, f * 2 + ri, :] = 1.0
                    for zh in range(2):
                        source = (ky // 2) * 4 + zh * 2 + ky % 2
                        pick[f, ri, e, 0:4, ky, source, f * 4 + e * 2 + ri] = 1.0
                        pick[f, ri, e, 4, ky, source, 8 + e] = 1.0
            for kt in range(4):
                spread_mask[0, e, kt, ky, kt] = 1.0
                spread_mask[1, e, kt, ky, kt] = 1.0
                spread[ky, 0, e, 0, 0, e, kt, ky] = 1.0
                spread[ky, 0, e, 1, 1, e, kt, ky] = 1.0
            spread_mask[0, e, 4, ky, 0] = 1.0
            spread_mask[1, e, 4, ky, 1] = 1.0
            spread_mask[2, e, 4, ky, 0] = 1.0
            spread_mask[3, e, 4, ky, 1] = 1.0
            spread[ky, 1, e, 0, 0, e, 4, ky] = 1.0
            spread[ky, 1, e, 0, 1, e, 4, ky] = 1.0
            spread[ky, 1, e, 1, 2, e, 4, ky] = 1.0
            spread[ky, 1, e, 1, 3, e, 4, ky] = -1.0
    group = np.arange(128) % C
    lane = np.arange(C * C)
    by_in = (group[:, None] == lane[None, :] // C).astype(np.float64)
    by_out = (group[:, None] == lane[None, :256] % C).astype(np.float64)
    return (
        pick.reshape(320, 256),
        pick_mask.reshape(320, 128),
        by_in,
        by_out,
        by_in.T,
        spread.reshape(64, 320),
        spread_mask.reshape(320, 128),
    )


def make_tables():
    t = {}
    t["col_f"], t["col_i"] = column_tables()
    t["time_f"], t["time_i"] = time_tables()
    t["reg_a"], t["reg_b"], t["reg_l"], t["reg_c"] = regroup_tables()
    t["row_f"], t["row_i"], t["deal"] = row_tables()
    t["pick"], t["pick_m"], t["by_in"], t["by_out"], t["by_in_t"], t["spread"], t["spread_m"] = (
        mixing_tables()
    )
    return {k: np.asarray(v, np.float32).astype(jnp.bfloat16) for k, v in t.items()}


PICKED = ("col_f", "col_i", "row_f", "row_i")
ORDER = (
    "col_f", "time_f", "reg_a", "reg_b", "reg_l", "row_f", "deal", "pick", "pick_m", "by_in",
    "by_out", "by_in_t", "spread", "spread_m", "row_i", "reg_c", "time_i", "col_i",
)


def mm(a, b):
    return jnp.dot(a, b, preferred_element_type=F32)


def mm_full(a, b):
    return jnp.dot(a, b, preferred_element_type=F32, precision=lax.Precision.HIGHEST)


def gelu_slope(values):
    normal_cdf = 0.5 * (1.0 + lax.erf(values * (1.0 / math.sqrt(2.0))))
    density = jnp.exp(-0.5 * values * values) * (1.0 / math.sqrt(2.0 * math.pi))
    return normal_cdf + values * density


def pre_gradient(cot, pre):
    return (cot.astype(F32) * gelu_slope(pre.astype(F32))).astype(BF16)


def group_mask(shape):
    row = lax.broadcasted_iota(jnp.int32, shape, 0)
    lane = lax.broadcasted_iota(jnp.int32, shape, 1)
    return row, lane


def fold_lanes(values):
    values = values + pltpu.roll(values, 64, 1)
    return values + pltpu.roll(values, 32, 1)


def pack_bypass(product):
    row, lane = group_mask((256, 256))
    kept = jnp.where(row // C == lane // C, product, 0.0).reshape(8, C, 256).sum(0)
    wide = fold_lanes(kept[:, :128] + kept[:, 128:])
    row, lane = group_mask((C, 128))
    kept = jnp.where(row % 4 == lane // C, wide, 0.0)
    row, lane = group_mask((8, C))
    return mm_full(jnp.where(row == lane // 4, 1.0, 0.0), kept)


def unpack_bypass(packed):
    row, lane = group_mask((C, 8))
    wide = mm_full(jnp.where(row // 4 == lane, 1.0, 0.0), packed)
    row, lane = group_mask((C, 128))
    kept = fold_lanes(jnp.where(row % 4 == lane // C, wide, 0.0))
    return kept[:, :C] * BYPASS_SCALE


def block_bypass(bypass):
    row, lane = group_mask((256, C))
    tall = jnp.where(row % C == lane, 1.0, 0.0).astype(BF16)
    row, lane = group_mask((C, 256))
    flat = jnp.where(lane % C == row, 1.0, 0.0).astype(BF16)
    turned = lax.dot_general(tall, bypass, (((1,), (1,)), ((), ())), preferred_element_type=F32)
    full = mm(turned.astype(BF16), flat)
    row, lane = group_mask((256, 256))
    return jnp.where(row // C == lane // C, full, 0.0).astype(BF16)


def regroup_forward(total, reg_a, reg_b, reg_l):
    rows = total.astype(BF16)
    turned = mm(rows, reg_l).astype(BF16)
    return mm(reg_a, rows) + mm(reg_b, turned)


def final_rows(low_re, low_im, high, time_i, col_i):
    z = jnp.concatenate([low_re, low_im, high], axis=1)
    u = mm(z, time_i).astype(BF16)
    return mm(col_i, jnp.concatenate([u[:, :256], u[:, 256:]], axis=0))


def rows_of(block, count):
    return block.astype(F32).reshape(count, 128).astype(BF16)


def kernel(inp_hbm, pre_hbm, cot_hbm, spec_hbm, byp_hbm, *refs):
    n = len(ORDER)
    tables = dict(zip(ORDER, refs[:n]))
    out_g_hbm, out_s_hbm, out_b = refs[n : n + 3]
    held = dict(zip(ORDER, refs[n + 3 : 2 * n + 3]))
    (
        inp, pre, cot, spec, byp, out_g, out_s, arg_sem, out_sem,
        grad, plus, pieces, recv_col, send_s, recv_s, send_x, recv_x, send_q, recv_q,
        send_b, recv_b, recv_g, send_l, recv_l, send_c, recv_c,
        by_sum, wide_q, by_a, by_b, by_c, by_d, by_e,
        lined, high, product, blocks, chosen, repeated,
        table_sem, send_sem, recv_sem,
    ) = refs[2 * n + 3 :]

    row = lax.axis_index("row")
    j = lax.axis_index("col")
    xx = row // 16
    q = row % 16
    yy = q // 4
    zh = (q // 2) % 2
    core = q % 2
    s = yy * 2 + core

    def col_peer(k):
        return row, (j + k) % 8

    def s_index(k):
        return (s + k) % 8

    def s_peer(k):
        other = s_index(k)
        return xx * 16 + (other // 2) * 4 + zh * 2 + other % 2, j

    def zh_peer():
        return xx * 16 + yy * 4 + (1 - zh) * 2 + core, j

    def x_peer(k):
        return ((xx + k) % 4) * 16 + q, j

    def q_index(k):
        return (q + k) % 16

    def q_peer(k):
        return xx * 16 + q_index(k), j

    barrier = pltpu.get_barrier_semaphore()
    everyone = (
        [col_peer(k) for k in range(1, 8)]
        + [q_peer(k) for k in range(1, 16)]
        + [x_peer(k) for k in range(1, 4)]
    )
    for peer in everyone:
        pl.semaphore_signal(barrier, inc=1, device_id=peer, device_id_type=MESH)

    index_of = {"col_f": j, "col_i": j, "row_f": xx * 2 + zh, "row_i": xx * 2 + zh}
    loads = {}

    def load(name):
        source = tables[name].at[index_of[name]] if name in PICKED else tables[name]
        loads[name] = pltpu.make_async_copy(source, held[name], table_sem.at[ORDER.index(name)])
        loads[name].start()

    args = []
    for at, (source, target) in enumerate(
        ((inp_hbm, inp), (cot_hbm, cot), (pre_hbm, pre), (byp_hbm, byp), (spec_hbm, spec))
    ):
        args.append(pltpu.make_async_copy(source, target, arg_sem.at[at]))
    args[0].start()
    load("col_f")
    load("time_f")
    args[1].start()
    args[2].start()
    args[3].start()
    args[4].start()
    for name in ORDER[2:]:
        load(name)

    def table(name):
        return held[name][...]

    exchanges = []
    used = [0]

    def exchange(count, make):
        base = used[0]
        used[0] += count

        def copy(k):
            source, target, peer = make(k)
            return pltpu.make_async_remote_copy(
                src_ref=source,
                dst_ref=target,
                send_sem=send_sem.at[base + k],
                recv_sem=recv_sem.at[base + k],
                device_id=peer,
                device_id_type=MESH,
            )

        def start(k, carry):
            copy(k).start()
            return carry

        lax.fori_loop(0, count, start, 0)
        pair = copy, count
        exchanges.append(pair)
        return pair

    def arrive(pair, first=0, last=None):
        copy, count = pair

        def wait(k, carry):
            copy(k).wait_recv()
            return carry

        lax.fori_loop(first, count if last is None else last, wait, 0)

    loads["col_f"].wait()
    args[0].wait()

    def lines_in(x, carry):
        y = mm(held["col_f"][...], inp[x]).astype(BF16)
        lined[x, :, 0:256] = y[:64]
        lined[x, :, 256:512] = y[64:]
        return carry

    lax.fori_loop(0, 4, lines_in, 0)
    loads["time_f"].wait()
    r = mm(lined[...].reshape(256, 512), held["time_f"][:, 0:384])
    for x in range(4):
        rows = slice(64 * x, 64 * x + 64)
        pieces[:, 0, x] = r[rows, :128].reshape(8, 8, 128).astype(BF16)
        pieces[:, 1, x] = r[rows, 128:256].reshape(8, 8, 128).astype(BF16)
    high[...] = r[:, 256:]
    pl.semaphore_wait(barrier, len(everyone))
    first_in = exchange(
        7,
        lambda k: (
            pieces.at[(j + k + 1) % 8, 0:2],
            recv_col.at[k, 0:2],
            col_peer(k + 1),
        ),
    )
    args[1].wait()
    args[2].wait()

    def lines_grad(x, carry):
        g = pre_gradient(cot[x], pre[x])
        grad[x] = g
        y = mm(held["col_f"][...], g).astype(BF16)
        lined[x, :, 0:256] = y[:64]
        lined[x, :, 256:512] = y[64:]
        return carry

    lax.fori_loop(0, 4, lines_grad, 0)
    rows = lined[...].reshape(256, 512)
    r = mm(rows, held["time_f"][:, 0:256])
    top = high[...] + mm(rows, held["time_f"][:, 384:512])
    for x in range(4):
        rows = slice(64 * x, 64 * x + 64)
        pieces[:, 2, x] = r[rows, :128].reshape(8, 8, 128).astype(BF16)
        pieces[:, 3, x] = r[rows, 128:].reshape(8, 8, 128).astype(BF16)
        pieces[:, 4, x] = top[rows].reshape(8, 8, 128).astype(BF16)
    first_grad = exchange(
        7,
        lambda k: (
            pieces.at[(j + k + 1) % 8, 2:5],
            recv_col.at[k, 2:5],
            col_peer(k + 1),
        ),
    )

    product[...] = jnp.zeros((256, 256), F32)

    def add_product(x, carry):
        product[...] += lax.dot_general(
            inp[x], grad[x], (((0,), (0,)), ((), ())), preferred_element_type=F32
        )
        return carry

    lax.fori_loop(0, 4, add_product, 0)
    by_a[s] = pack_bypass(product[...])
    bypass_a = exchange(7, lambda k: (by_a.at[s], by_a.at[s], s_peer(k + 1)))
    args[3].wait()
    blocks[...] = block_bypass(byp[...])

    def pointwise(x, carry):
        plus[x] = mm(grad[x], blocks[...])
        return carry

    lax.fori_loop(0, 4, pointwise, 0)

    for name in ("reg_a", "reg_b", "reg_l"):
        loads[name].wait()
    arrive(first_in)
    arrive(first_grad)
    total = pieces[j].astype(F32).reshape(160, 128)
    for k in range(7):
        total += recv_col[k].astype(F32).reshape(160, 128)
    grouped = regroup_forward(total, table("reg_a"), table("reg_b"), table("reg_l"))
    send_s[...] = grouped.reshape(8, 3, 8, 128).astype(BF16)
    recv_s[s] = send_s[s]
    second = exchange(7, lambda k: (send_s.at[s_index(k + 1)], recv_s.at[s], s_peer(k + 1)))

    arrive(bypass_a)
    by_sum[...] = by_a[...].sum(0)
    by_b[xx] = by_sum[pl.ds(s, 1), :]
    bypass_b = exchange(3, lambda k: (by_b.at[xx], by_b.at[xx], x_peer(k + 1)))

    wide_q[...] = jnp.zeros((16, 16, 128), F32)
    loads["row_f"].wait()
    loads["deal"].wait()
    arrive(second)
    rows = jnp.concatenate([rows_of(recv_s[:, slab], 64) for slab in range(3)], axis=1)
    send_x[...] = mm(table("row_f"), rows).reshape(4, 64, 384).astype(BF16)
    fourth = exchange(
        3, lambda k: (send_x.at[(xx + k + 1) % 4], recv_x.at[k], x_peer(k + 1))
    )
    arrive(bypass_b)
    by_c[j] = by_b[...].sum(0)
    bypass_c = exchange(7, lambda k: (by_c.at[j], by_c.at[j], col_peer(k + 1)))
    arrive(fourth)
    summed = send_x[xx].astype(F32)
    for k in range(3):
        summed += recv_x[k].astype(F32)
    summed = summed.astype(BF16)
    summed = jnp.concatenate([summed[:, 128 * i : 128 * i + 128] for i in range(3)], axis=0)
    dealt = mm(table("deal"), summed).reshape(16, 16, 128)
    send_q[...] = dealt[:, 0:10].astype(BF16)

    fifth = exchange(15, lambda k: (send_q.at[q_index(k + 1)], recv_q.at[q], q_peer(k + 1)))
    recv_q[q] = send_q[q]
    for name in ("pick", "pick_m", "by_in", "by_out", "by_in_t", "spread", "spread_m"):
        loads[name].wait()
    args[4].wait()
    arrive(fifth)
    wide_q[:, 0:10] = recv_q[...].astype(F32)
    halves = wide_q[...].reshape(256, 128).astype(BF16)
    chosen[...] = (mm(table("pick"), halves) * table("pick_m").astype(F32)).astype(BF16)
    repeated[...] = mm(chosen[160:320, :], table("by_out"))

    def mix(m, carry):
        lanes = pl.ds(pl.multiple_of(m * 256, 256), 256)
        a = mm(chosen[0:160, :], held["by_in"][:, lanes])
        a_re, a_im = a[:80], a[80:]
        g_re = repeated[0:80, :]
        g_im = repeated[80:160, :]
        w_re = spec[0, :, lanes].astype(F32)
        w_im = spec[1, :, lanes].astype(F32)
        out_s[0, :, lanes] = FACTOR * (a_re * g_re + a_im * g_im)
        out_s[1, :, lanes] = FACTOR * (a_re * g_im - a_im * g_re)
        p_re = (w_re * g_re + w_im * g_im).astype(BF16)
        p_im = (w_re * g_im - w_im * g_re).astype(BF16)
        turn = held["by_in_t"][lanes, :]
        return carry + mm(jnp.concatenate([p_re, p_im], axis=0), turn)

    b = lax.fori_loop(0, 4, mix, jnp.zeros((160, 128), F32)) * FACTOR
    b_re, b_im = b[:80], b[80:]
    stack = jnp.concatenate([b_re, b_im, b_im, b_re], axis=0) * table("spread_m").astype(F32)
    back = mm(table("spread"), stack.astype(BF16))
    send_b[...] = back.reshape(8, 8, 128).astype(BF16)

    def mode_home(k):
        to = q_index(k + 1)
        return send_b.at[(to // 4) * 2 + to % 2], recv_b.at[q], q_peer(k + 1)

    sixth = exchange(15, mode_home)
    recv_b[q] = send_b[s]
    out_copy_s = pltpu.make_async_copy(out_s, out_s_hbm, out_sem.at[4])
    out_copy_s.start()
    arrive(bypass_c)
    by_d[zh] = by_c[...].sum(0)
    bypass_d = exchange(1, lambda k: (by_d.at[zh], by_d.at[zh], zh_peer()))

    arrive(sixth)
    seventh = exchange(3, lambda k: (recv_b, recv_g.at[xx], x_peer(k + 1)))
    recv_g[xx] = recv_b[...]
    loads["row_i"].wait()
    loads["reg_c"].wait()
    arrive(seventh)
    lines = mm(table("row_i"), rows_of(recv_g[...], 512))
    send_l[...] = lines.reshape(8, 16, 128).astype(BF16)
    eighth = exchange(7, lambda k: (send_l.at[s_index(k + 1)], recv_l.at[s], s_peer(k + 1)))
    recv_l[s] = send_l[s]
    arrive(bypass_d)
    by_e[s] = by_d[...].sum(0)
    bypass_e = exchange(7, lambda k: (by_e.at[s], by_e.at[s], s_peer(k + 1)))
    arrive(eighth)
    turned = mm(table("reg_c"), rows_of(recv_l[...], 128))
    send_c[...] = turned.reshape(4, 3, 8, 128).astype(BF16)
    ninth = exchange(
        14,
        lambda k: (
            send_c.at[pl.ds((k // 7) * 2, 2)],
            recv_c.at[j, pl.ds((k // 7) * 2, 2)],
            col_peer(k % 7 + 1),
        ),
    )
    recv_c[j] = send_c[...]
    loads["time_i"].wait()
    loads["col_i"].wait()
    arrive(bypass_e)
    out_b[...] = unpack_bypass(by_e[...].reshape(8, 128))

    def out_copy(x):
        return pltpu.make_async_copy(out_g.at[x], out_g_hbm.at[x], out_sem.at[x])

    def final(x, carry):
        parts = [rows_of(recv_c[:, x, tile], 64) for tile in range(3)]
        rows = final_rows(*parts, held["time_i"][...], held["col_i"][...])
        out_g[x] = (rows + plus[x]).astype(BF16)
        out_copy(x).start()
        return carry

    for half in range(2):
        arrive(ninth, 7 * half, 7 * half + 7)
        lax.fori_loop(2 * half, 2 * half + 2, final, 0)

    for copy, count in exchanges:

        def drain(k, carry, copy=copy):
            copy(k).wait_send()
            return carry

        lax.fori_loop(0, count, drain, 0)
    for x in range(4):
        out_copy(x).wait()
    out_copy_s.wait()


N_COPIES = 14 + 7 + 3 + 7 + 1 + 7 + 7 + 3 + 15 + 15 + 3 + 7 + 14


def local(inputs, preactivation, cotangent, spectral, bypass, tables):
    weight = spectral.transpose(0, 1, 3, 2, 4).reshape(2, 80, C * C)
    vmem = pl.BlockSpec(memory_space=pltpu.VMEM)
    anywhere = pl.BlockSpec(memory_space=pl.ANY)
    held = [
        pltpu.VMEM(tables[k].shape[1:] if k in PICKED else tables[k].shape, BF16) for k in ORDER
    ]
    blocks = [
        pltpu.VMEM((4, 128, 256), BF16),
        pltpu.VMEM((4, 128, 256), BF16),
        pltpu.VMEM((4, 128, 256), BF16),
        pltpu.VMEM((2, 80, C * C), BF16),
        pltpu.VMEM((C, C), BF16),
        pltpu.VMEM((4, 128, 256), BF16),
        pltpu.VMEM((2, 80, C * C), F32),
        pltpu.SemaphoreType.DMA((5,)),
        pltpu.SemaphoreType.DMA((5,)),
        pltpu.VMEM((4, 128, 256), BF16),
        pltpu.VMEM((4, 128, 256), F32),
        pltpu.VMEM((8, 5, 4, 8, 128), BF16),
        pltpu.VMEM((7, 5, 4, 8, 128), BF16),
        pltpu.VMEM((8, 3, 8, 128), BF16),
        pltpu.VMEM((8, 3, 8, 128), BF16),
        pltpu.VMEM((4, 64, 384), BF16),
        pltpu.VMEM((3, 64, 384), BF16),
        pltpu.VMEM((16, 10, 128), BF16),
        pltpu.VMEM((16, 10, 128), BF16),
        pltpu.VMEM((8, 8, 128), BF16),
        pltpu.VMEM((16, 8, 128), BF16),
        pltpu.VMEM((4, 16, 8, 128), BF16),
        pltpu.VMEM((8, 16, 128), BF16),
        pltpu.VMEM((8, 16, 128), BF16),
        pltpu.VMEM((4, 3, 8, 128), BF16),
        pltpu.VMEM((8, 4, 3, 8, 128), BF16),
        pltpu.VMEM((8, 128), F32),
        pltpu.VMEM((16, 16, 128), F32),
        pltpu.VMEM((8, 8, 128), F32),
        pltpu.VMEM((4, 1, 128), F32),
        pltpu.VMEM((8, 1, 128), F32),
        pltpu.VMEM((2, 1, 128), F32),
        pltpu.VMEM((8, 1, 128), F32),
        pltpu.VMEM((4, 64, 512), BF16),
        pltpu.VMEM((256, 128), F32),
        pltpu.VMEM((256, 256), F32),
        pltpu.VMEM((256, 256), BF16),
        pltpu.VMEM((320, 128), BF16),
        pltpu.VMEM((160, 256), F32),
        pltpu.SemaphoreType.DMA((len(ORDER),)),
        pltpu.SemaphoreType.DMA((N_COPIES,)),
        pltpu.SemaphoreType.DMA((N_COPIES,)),
    ]
    grad_inputs, grad_weight, grad_bypass = pl.pallas_call(
        kernel,
        out_shape=(
            jax.ShapeDtypeStruct((4, 128, 256), BF16),
            jax.ShapeDtypeStruct((2, 80, C * C), F32),
            jax.ShapeDtypeStruct((C, C), F32),
        ),
        in_specs=[anywhere] * (5 + len(ORDER)),
        out_specs=(anywhere, anywhere, vmem),
        scratch_shapes=held + blocks,
        compiler_params=pltpu.CompilerParams(
            collective_id=0, has_side_effects=True, vmem_limit_bytes=62 * 1024 * 1024
        ),
        name="fno_backward",
    )(inputs, preactivation, cotangent, weight, bypass, *[tables[k] for k in ORDER])
    grad_spectral = grad_weight.reshape(2, 2, 5, 8, C * C).transpose(0, 1, 3, 2, 4)
    return (grad_inputs, grad_spectral, grad_bypass)


def solution(mesh):
    tables = make_tables()

    def step(*args):
        return local(*args, {k: jnp.asarray(v) for k, v in tables.items()})

    return jax.shard_map(
        step,
        mesh=mesh,
        in_specs=(
            P("row", "col", None),
            P("row", "col", None),
            P("row", "col", None),
            P(None, "row", "col", None, None),
            P(),
        ),
        out_specs=(P("row", "col", None), P(None, "row", "col", None, None), P()),
        check_vma=False,
    )
```

```python
import math

import jax
import jax.numpy as jnp
import numpy as np
from jax import lax
from jax.experimental import pallas as pl
from jax.experimental.pallas import tpu as pltpu
from jax.sharding import PartitionSpec as P

MESH = pl.DeviceIdType.MESH
F32 = jnp.float32
BF16 = jnp.bfloat16
NX, NY, NT, C = 256, 1024, 8, 32
KX, KY, KT = 128, 64, 5
FACTOR = 1.0 / math.sqrt(float(NX * NY * NT * KX * KY * KT))
BYPASS_SCALE = 1.0 / math.sqrt(float(NX * NY * NT))


def turns(a, b, n):
    angle = 2.0 * np.pi * (np.multiply.outer(a, b) % n) / n
    return np.cos(angle), np.sin(angle)


def column_tables():
    forward, inverse = [], []
    for j in range(8):
        cos, sin = turns(np.arange(64), 128 * j + np.arange(128), NY)
        forward.append(np.concatenate([cos, -sin], 0))
        inverse.append(np.concatenate([cos.T, -sin.T], 1))
    return np.stack(forward), np.stack(inverse)


def time_tables():
    cos, sin = turns(np.arange(NT), np.arange(KT), NT)
    eye = np.eye(C)
    low = np.zeros((2, NT, C, 2, 4, C))
    for t in range(NT):
        for k in range(4):
            low[0, t, :, 0, k, :] = eye * cos[t, k]
            low[1, t, :, 0, k, :] = eye * sin[t, k]
            low[0, t, :, 1, k, :] = -eye * sin[t, k]
            low[1, t, :, 1, k, :] = eye * cos[t, k]
    high = np.zeros((2, 2, NT, C, 2, 2, C))
    for f in range(2):
        for t in range(NT):
            high[f, 0, t, :, f, 0, :] = eye * cos[t, 4]
            high[f, 1, t, :, f, 1, :] = eye * cos[t, 4]
    forward = np.concatenate(
        [low.reshape(512, 256), high[0].reshape(512, 128), high[1].reshape(512, 128)], 1
    )
    inverse = np.zeros((3, 4, C, 2, NT, C))
    for t in range(NT):
        for k in range(4):
            inverse[0, k, :, 0, t, :] = eye * cos[t, k]
            inverse[1, k, :, 0, t, :] = -eye * sin[t, k]
            inverse[0, k, :, 1, t, :] = eye * sin[t, k]
            inverse[1, k, :, 1, t, :] = eye * cos[t, k]
        inverse[2, 0, :, 0, t, :] = eye * cos[t, 4]
        inverse[2, 1, :, 1, t, :] = eye * cos[t, 4]
    return forward, inverse.reshape(384, 512)


def regroup_tables():
    direct = np.zeros((8, 3, 2, 4, 5, 4, 8))
    swapped = np.zeros((8, 3, 2, 4, 5, 4, 8))
    back = np.zeros((4, 3, 8, 8, 2, 2, 4))
    for k in range(8):
        for x in range(4):
            for tile in range(5):
                direct[k, tile // 2, tile % 2, x, tile, x, k] = 1.0
            swapped[k, 2, 1, x, 4, x, k] = 1.0
            for tile in range(3):
                back[x, tile, k, k, tile // 2, tile % 2, x] = 1.0
    lanes = np.zeros((2, 2, C, 2, 2, C))
    for f in range(2):
        lanes[f, 1, :, f, 0, :] = np.eye(C)
        lanes[f, 0, :, f, 1, :] = -np.eye(C)
    return (
        direct.reshape(192, 160),
        swapped.reshape(192, 160),
        lanes.reshape(128, 128),
        back.reshape(96, 128),
    )


def row_tables():
    k = np.arange(KX)
    freq = np.where(k < KX // 2, k, k - KX) % NX
    cos, sin = turns(freq, np.arange(NX), NX)
    cos = cos.reshape(4, 16, 2, 4, 4, 2, 2, 4)
    sin = sin.reshape(4, 16, 2, 4, 4, 2, 2, 4)
    forward = np.zeros((4, 2, 4, 16, 2, 2, 4, 2, 2, 4))
    for xx in range(4):
        for zh in range(2):
            c = cos[:, :, :, xx, :, zh]
            s = sin[:, :, :, xx, :, zh]
            forward[xx, zh, :, :, :, 0, :, :, 0, :] = c
            forward[xx, zh, :, :, :, 0, :, :, 1, :] = s
            forward[xx, zh, :, :, :, 1, :, :, 1, :] = c
            forward[xx, zh, :, :, :, 1, :, :, 0, :] = -s
    forward = forward.reshape(8, 256, 64)
    deal = np.zeros((16, 16, 3, 16, 2, 2))
    for q in range(16):
        for e in range(2):
            for ab in range(2):
                for slab in range(2):
                    deal[q, slab * 4 + e * 2 + ab, slab, q, e, ab] = 1.0
            deal[q, 8 + e, 2, q, e, 0] = 1.0
    inverse = np.zeros((4, 2, 4, 2, 2, 2, 4, 4, 16, 2, 2, 2))
    for xx in range(4):
        for zh in range(2):
            for slab in range(2):
                c = cos[:, :, :, xx, :, zh].transpose(3, 4, 5, 0, 1, 2)
                s = sin[:, :, :, xx, :, zh].transpose(3, 4, 5, 0, 1, 2)
                inverse[xx, zh, :, :, slab, 0, :, :, :, slab, :, 0] = c
                inverse[xx, zh, :, :, slab, 0, :, :, :, slab, :, 1] = -s
                inverse[xx, zh, :, :, slab, 1, :, :, :, slab, :, 1] = c
                inverse[xx, zh, :, :, slab, 1, :, :, :, slab, :, 0] = s
    return forward, inverse.reshape(8, 128, 512), deal.reshape(256, 192)


def mixing_tables():
    pick = np.zeros((2, 2, 2, 5, 8, 16, 16))
    pick_mask = np.zeros((2, 2, 2, 5, 8, 4, C))
    spread = np.zeros((8, 2, 2, 2, 4, 2, 5, 8))
    spread_mask = np.zeros((4, 2, 5, 8, 4, C))
    for ky in range(8):
        for e in range(2):
            for f in range(2):
                for ri in range(2):
                    for kt in range(4):
                        pick_mask[f, ri, e, kt, ky, kt, :] = 1.0
                    pick_mask[f, ri, e, 4, ky, f * 2 + ri, :] = 1.0
                    for zh in range(2):
                        source = (ky // 2) * 4 + zh * 2 + ky % 2
                        pick[f, ri, e, 0:4, ky, source, f * 4 + e * 2 + ri] = 1.0
                        pick[f, ri, e, 4, ky, source, 8 + e] = 1.0
            for kt in range(4):
                spread_mask[0, e, kt, ky, kt] = 1.0
                spread_mask[1, e, kt, ky, kt] = 1.0
                spread[ky, 0, e, 0, 0, e, kt, ky] = 1.0
                spread[ky, 0, e, 1, 1, e, kt, ky] = 1.0
            spread_mask[0, e, 4, ky, 0] = 1.0
            spread_mask[1, e, 4, ky, 1] = 1.0
            spread_mask[2, e, 4, ky, 0] = 1.0
            spread_mask[3, e, 4, ky, 1] = 1.0
            spread[ky, 1, e, 0, 0, e, 4, ky] = 1.0
            spread[ky, 1, e, 0, 1, e, 4, ky] = 1.0
            spread[ky, 1, e, 1, 2, e, 4, ky] = 1.0
            spread[ky, 1, e, 1, 3, e, 4, ky] = -1.0
    group = np.arange(128) % C
    lane = np.arange(C * C)
    by_in = (group[:, None] == lane[None, :] // C).astype(np.float64)
    by_out = (group[:, None] == lane[None, :256] % C).astype(np.float64)
    return (
        pick.reshape(320, 256),
        pick_mask.reshape(320, 128),
        by_in,
        by_out,
        by_in.T,
        spread.reshape(64, 320),
        spread_mask.reshape(320, 128),
    )


def make_tables():
    t = {}
    t["col_f"], t["col_i"] = column_tables()
    t["time_f"], t["time_i"] = time_tables()
    t["reg_a"], t["reg_b"], t["reg_l"], t["reg_c"] = regroup_tables()
    t["row_f"], t["row_i"], t["deal"] = row_tables()
    t["pick"], t["pick_m"], t["by_in"], t["by_out"], t["by_in_t"], t["spread"], t["spread_m"] = (
        mixing_tables()
    )
    return {k: np.asarray(v, np.float32).astype(jnp.bfloat16) for k, v in t.items()}


PICKED = ("col_f", "col_i", "row_f", "row_i")
ORDER = (
    "col_f", "time_f", "reg_a", "reg_b", "reg_l", "row_f", "deal", "pick", "pick_m", "by_in",
    "by_out", "by_in_t", "spread", "spread_m", "row_i", "reg_c", "time_i", "col_i",
)


def mm(a, b):
    return jnp.dot(a, b, preferred_element_type=F32)


def mm_full(a, b):
    return jnp.dot(a, b, preferred_element_type=F32, precision=lax.Precision.HIGHEST)


def gelu_slope(values):
    normal_cdf = 0.5 * (1.0 + lax.erf(values * (1.0 / math.sqrt(2.0))))
    density = jnp.exp(-0.5 * values * values) * (1.0 / math.sqrt(2.0 * math.pi))
    return normal_cdf + values * density


def pre_gradient(cot, pre):
    return (cot.astype(F32) * gelu_slope(pre.astype(F32))).astype(BF16)


def group_mask(shape):
    row = lax.broadcasted_iota(jnp.int32, shape, 0)
    lane = lax.broadcasted_iota(jnp.int32, shape, 1)
    return row, lane


def fold_lanes(values):
    values = values + pltpu.roll(values, 64, 1)
    return values + pltpu.roll(values, 32, 1)


def pack_bypass(product):
    row, lane = group_mask((256, 256))
    kept = jnp.where(row // C == lane // C, product, 0.0).reshape(8, C, 256).sum(0)
    wide = fold_lanes(kept[:, :128] + kept[:, 128:])
    row, lane = group_mask((C, 128))
    kept = jnp.where(row % 4 == lane // C, wide, 0.0)
    row, lane = group_mask((8, C))
    return mm_full(jnp.where(row == lane // 4, 1.0, 0.0), kept)


def unpack_bypass(packed):
    row, lane = group_mask((C, 8))
    wide = mm_full(jnp.where(row // 4 == lane, 1.0, 0.0), packed)
    row, lane = group_mask((C, 128))
    kept = fold_lanes(jnp.where(row % 4 == lane // C, wide, 0.0))
    return kept[:, :C] * BYPASS_SCALE


def block_bypass(bypass):
    row, lane = group_mask((256, C))
    tall = jnp.where(row % C == lane, 1.0, 0.0).astype(BF16)
    row, lane = group_mask((C, 256))
    flat = jnp.where(lane % C == row, 1.0, 0.0).astype(BF16)
    turned = lax.dot_general(tall, bypass, (((1,), (1,)), ((), ())), preferred_element_type=F32)
    full = mm(turned.astype(BF16), flat)
    row, lane = group_mask((256, 256))
    return jnp.where(row // C == lane // C, full, 0.0).astype(BF16)


def regroup_forward(total, reg_a, reg_b, reg_l):
    rows = total.astype(BF16)
    turned = mm(rows, reg_l).astype(BF16)
    return mm(reg_a, rows) + mm(reg_b, turned)


def final_rows(low_re, low_im, high, time_i, col_i):
    z = jnp.concatenate([low_re, low_im, high], axis=1)
    u = mm(z, time_i).astype(BF16)
    return mm(col_i, jnp.concatenate([u[:, :256], u[:, 256:]], axis=0))


def rows_of(block, count):
    return block.astype(F32).reshape(count, 128).astype(BF16)


def kernel(inp_hbm, pre_hbm, cot_hbm, spec_hbm, byp_hbm, *refs):
    n = len(ORDER)
    tables = dict(zip(ORDER, refs[:n]))
    out_g_hbm, out_s_hbm, out_b = refs[n : n + 3]
    held = dict(zip(ORDER, refs[n + 3 : 2 * n + 3]))
    (
        inp, pre, cot, spec, byp, out_g, out_s, arg_sem, out_sem,
        grad, plus, pieces, recv_col, send_s, recv_s, send_x, recv_x, send_q, recv_q,
        send_b, recv_b, recv_g, send_l, recv_l, send_c, recv_c,
        by_sum, wide_q, by_a, by_b, by_c, by_d, by_e,
        lined, high, product, blocks, chosen, repeated,
        table_sem, send_sem, recv_sem,
    ) = refs[2 * n + 3 :]

    row = lax.axis_index("row")
    j = lax.axis_index("col")
    xx = row // 16
    q = row % 16
    yy = q // 4
    zh = (q // 2) % 2
    core = q % 2
    s = yy * 2 + core

    def col_peer(k):
        return row, (j + k) % 8

    def s_index(k):
        return (s + k) % 8

    def q_of(other, half):
        return (other // 2) * 4 + half * 2 + other % 2

    def s_peer(k, half=zh):
        return xx * 16 + q_of(s_index(k), half), j

    def zh_peer():
        return s_peer(0, 1 - zh)

    def x_peer(k):
        return ((xx + k) % 4) * 16 + q, j

    barrier = pltpu.get_barrier_semaphore()
    everyone = (
        [col_peer(k) for k in range(1, 8)]
        + [s_peer(k) for k in range(1, 8)]
        + [s_peer(k, 1 - zh) for k in range(8)]
        + [x_peer(k) for k in range(1, 4)]
    )
    for peer in everyone:
        pl.semaphore_signal(barrier, inc=1, device_id=peer, device_id_type=MESH)

    index_of = {"col_f": j, "col_i": j, "row_f": xx * 2 + zh, "row_i": xx * 2 + zh}
    loads = {}

    def load(name):
        source = tables[name].at[index_of[name]] if name in PICKED else tables[name]
        loads[name] = pltpu.make_async_copy(source, held[name], table_sem.at[ORDER.index(name)])
        loads[name].start()

    args = []
    for at, (source, target) in enumerate(
        ((inp_hbm, inp), (cot_hbm, cot), (pre_hbm, pre), (byp_hbm, byp), (spec_hbm, spec))
    ):
        args.append(pltpu.make_async_copy(source, target, arg_sem.at[at]))
    args[0].start()
    load("col_f")
    load("time_f")
    args[1].start()
    args[2].start()
    args[3].start()
    args[4].start()
    for name in ORDER[2:]:
        load(name)

    def table(name):
        return held[name][...]

    exchanges = []
    used = [0]

    def exchange(count, make):
        base = used[0]
        used[0] += count

        def copy(k):
            source, target, peer = make(k)
            return pltpu.make_async_remote_copy(
                src_ref=source,
                dst_ref=target,
                send_sem=send_sem.at[base + k],
                recv_sem=recv_sem.at[base + k],
                device_id=peer,
                device_id_type=MESH,
            )

        def start(k, carry):
            copy(k).start()
            return carry

        lax.fori_loop(0, count, start, 0)
        pair = copy, count
        exchanges.append(pair)
        return pair

    def arrive(pair, first=0, last=None):
        copy, count = pair

        def wait(k, carry):
            copy(k).wait_recv()
            return carry

        lax.fori_loop(first, count if last is None else last, wait, 0)

    loads["col_f"].wait()
    args[0].wait()

    def lines_in(x, carry):
        y = mm(held["col_f"][...], inp[x]).astype(BF16)
        lined[x, :, 0:256] = y[:64]
        lined[x, :, 256:512] = y[64:]
        return carry

    lax.fori_loop(0, 4, lines_in, 0)
    loads["time_f"].wait()
    r = mm(lined[...].reshape(256, 512), held["time_f"][:, 0:384])
    for x in range(4):
        rows = slice(64 * x, 64 * x + 64)
        pieces[:, 0, x] = r[rows, :128].reshape(8, 8, 128).astype(BF16)
        pieces[:, 1, x] = r[rows, 128:256].reshape(8, 8, 128).astype(BF16)
    high[...] = r[:, 256:]
    pl.semaphore_wait(barrier, len(everyone))
    first_in = exchange(
        7,
        lambda k: (
            pieces.at[(j + k + 1) % 8, 0:2],
            recv_col.at[k, 0:2],
            col_peer(k + 1),
        ),
    )
    args[1].wait()
    args[2].wait()

    def lines_grad(x, carry):
        g = pre_gradient(cot[x], pre[x])
        grad[x] = g
        y = mm(held["col_f"][...], g).astype(BF16)
        lined[x, :, 0:256] = y[:64]
        lined[x, :, 256:512] = y[64:]
        return carry

    lax.fori_loop(0, 4, lines_grad, 0)
    rows = lined[...].reshape(256, 512)
    r = mm(rows, held["time_f"][:, 0:256])
    top = high[...] + mm(rows, held["time_f"][:, 384:512])
    for x in range(4):
        rows = slice(64 * x, 64 * x + 64)
        pieces[:, 2, x] = r[rows, :128].reshape(8, 8, 128).astype(BF16)
        pieces[:, 3, x] = r[rows, 128:].reshape(8, 8, 128).astype(BF16)
        pieces[:, 4, x] = top[rows].reshape(8, 8, 128).astype(BF16)
    first_grad = exchange(
        7,
        lambda k: (
            pieces.at[(j + k + 1) % 8, 2:5],
            recv_col.at[k, 2:5],
            col_peer(k + 1),
        ),
    )

    product[...] = jnp.zeros((256, 256), F32)

    def add_product(x, carry):
        product[...] += lax.dot_general(
            inp[x], grad[x], (((0,), (0,)), ((), ())), preferred_element_type=F32
        )
        return carry

    lax.fori_loop(0, 4, add_product, 0)
    by_a[s] = pack_bypass(product[...])
    bypass_a = exchange(7, lambda k: (by_a.at[s], by_a.at[s], s_peer(k + 1)))
    args[3].wait()
    blocks[...] = block_bypass(byp[...])

    def pointwise(x, carry):
        plus[x] = mm(grad[x], blocks[...])
        return carry

    lax.fori_loop(0, 4, pointwise, 0)

    for name in ("reg_a", "reg_b", "reg_l"):
        loads[name].wait()
    arrive(first_in)
    arrive(first_grad)
    total = pieces[j].astype(F32).reshape(160, 128)
    for k in range(7):
        total += recv_col[k].astype(F32).reshape(160, 128)
    grouped = regroup_forward(total, table("reg_a"), table("reg_b"), table("reg_l"))
    send_s[...] = grouped.reshape(8, 3, 8, 128).astype(BF16)
    recv_s[s] = send_s[s]
    second = exchange(7, lambda k: (send_s.at[s_index(k + 1)], recv_s.at[s], s_peer(k + 1)))

    arrive(bypass_a)
    by_sum[...] = by_a[...].sum(0)
    by_b[xx] = by_sum[pl.ds(s, 1), :]
    bypass_b = exchange(3, lambda k: (by_b.at[xx], by_b.at[xx], x_peer(k + 1)))

    wide_q[...] = jnp.zeros((16, 16, 128), F32)
    loads["row_f"].wait()
    loads["deal"].wait()
    arrive(second)
    rows = jnp.concatenate([rows_of(recv_s[:, slab], 64) for slab in range(3)], axis=1)
    send_x[...] = mm(table("row_f"), rows).reshape(4, 64, 384).astype(BF16)
    fourth = exchange(
        3, lambda k: (send_x.at[(xx + k + 1) % 4], recv_x.at[k], x_peer(k + 1))
    )
    arrive(bypass_b)
    by_c[j] = by_b[...].sum(0)
    bypass_c = exchange(7, lambda k: (by_c.at[j], by_c.at[j], col_peer(k + 1)))
    arrive(fourth)
    summed = send_x[xx].astype(F32)
    for k in range(3):
        summed += recv_x[k].astype(F32)
    summed = summed.astype(BF16)
    summed = jnp.concatenate([summed[:, 128 * i : 128 * i + 128] for i in range(3)], axis=0)
    dealt = mm(table("deal"), summed).reshape(16, 16, 128)
    send_q[...] = dealt[:, 0:10].astype(BF16)

    fifth_far = exchange(
        8, lambda k: (send_q.at[q_of(s_index(k), 1 - zh)], recv_q.at[q], s_peer(k, 1 - zh))
    )
    fifth = exchange(
        7, lambda k: (send_q.at[q_of(s_index(k + 1), zh)], recv_q.at[q], s_peer(k + 1, zh))
    )
    recv_q[q] = send_q[q]
    for name in ("pick", "pick_m", "by_in", "by_out", "by_in_t", "spread", "spread_m"):
        loads[name].wait()
    args[4].wait()
    arrive(fifth)
    arrive(fifth_far)
    wide_q[:, 0:10] = recv_q[...].astype(F32)
    halves = wide_q[...].reshape(256, 128).astype(BF16)
    chosen[...] = (mm(table("pick"), halves) * table("pick_m").astype(F32)).astype(BF16)
    repeated[...] = mm(chosen[160:320, :], table("by_out"))

    def mix(m, carry):
        lanes = pl.ds(pl.multiple_of(m * 256, 256), 256)
        a = mm(chosen[0:160, :], held["by_in"][:, lanes])
        a_re, a_im = a[:80], a[80:]
        g_re = repeated[0:80, :]
        g_im = repeated[80:160, :]
        w_re = spec[0, :, lanes].astype(F32)
        w_im = spec[1, :, lanes].astype(F32)
        out_s[0, :, lanes] = FACTOR * (a_re * g_re + a_im * g_im)
        out_s[1, :, lanes] = FACTOR * (a_re * g_im - a_im * g_re)
        p_re = (w_re * g_re + w_im * g_im).astype(BF16)
        p_im = (w_re * g_im - w_im * g_re).astype(BF16)
        turn = held["by_in_t"][lanes, :]
        return carry + mm(jnp.concatenate([p_re, p_im], axis=0), turn)

    b = lax.fori_loop(0, 4, mix, jnp.zeros((160, 128), F32)) * FACTOR
    b_re, b_im = b[:80], b[80:]
    stack = jnp.concatenate([b_re, b_im, b_im, b_re], axis=0) * table("spread_m").astype(F32)
    back = mm(table("spread"), stack.astype(BF16))
    send_b[...] = back.reshape(8, 8, 128).astype(BF16)

    sixth_far = exchange(
        8, lambda k: (send_b.at[s_index(k)], recv_b.at[q], s_peer(k, 1 - zh))
    )
    sixth = exchange(7, lambda k: (send_b.at[s_index(k + 1)], recv_b.at[q], s_peer(k + 1)))
    recv_b[q] = send_b[s]
    out_copy_s = pltpu.make_async_copy(out_s, out_s_hbm, out_sem.at[4])
    out_copy_s.start()
    arrive(bypass_c)
    by_d[zh] = by_c[...].sum(0)
    bypass_d = exchange(1, lambda k: (by_d.at[zh], by_d.at[zh], zh_peer()))

    arrive(sixth)
    arrive(sixth_far)
    seventh = exchange(3, lambda k: (recv_b, recv_g.at[xx], x_peer(k + 1)))
    recv_g[xx] = recv_b[...]
    loads["row_i"].wait()
    loads["reg_c"].wait()
    arrive(seventh)
    lines = mm(table("row_i"), rows_of(recv_g[...], 512))
    send_l[...] = lines.reshape(8, 16, 128).astype(BF16)
    eighth = exchange(7, lambda k: (send_l.at[s_index(k + 1)], recv_l.at[s], s_peer(k + 1)))
    recv_l[s] = send_l[s]
    arrive(bypass_d)
    by_e[s] = by_d[...].sum(0)
    bypass_e = exchange(7, lambda k: (by_e.at[s], by_e.at[s], s_peer(k + 1)))
    arrive(eighth)
    turned = mm(table("reg_c"), rows_of(recv_l[...], 128))
    send_c[...] = turned.reshape(4, 3, 8, 128).astype(BF16)
    halves = [pl.ds(0, 2), pl.ds(2, 2)]
    across = (j + 4) % 8

    def near(k):
        return (j // 4) * 4 + (j + k) % 4

    ninth_far = [
        exchange(1, lambda k, h=h: (send_c.at[h], recv_c.at[j, h], (row, across))) for h in halves
    ]
    ninth = exchange(
        6,
        lambda k: (
            send_c.at[pl.ds((k // 3) * 2, 2)],
            recv_c.at[j, pl.ds((k // 3) * 2, 2)],
            (row, near(k % 3 + 1)),
        ),
    )
    recv_c[j] = send_c[...]
    loads["time_i"].wait()
    loads["col_i"].wait()
    arrive(bypass_e)
    out_b[...] = unpack_bypass(by_e[...].reshape(8, 128))

    def out_copy(x):
        return pltpu.make_async_copy(out_g.at[x], out_g_hbm.at[x], out_sem.at[x])

    def final(x, carry):
        parts = [rows_of(recv_c[:, x, tile], 64) for tile in range(3)]
        rows = final_rows(*parts, held["time_i"][...], held["col_i"][...])
        out_g[x] = (rows + plus[x]).astype(BF16)
        out_copy(x).start()
        return carry

    passed = []
    for half in range(2):
        h = halves[half]
        arrive(ninth_far[half])
        passed.append(
            exchange(
                3, lambda k, h=h: (recv_c.at[across, h], recv_c.at[across, h], (row, near(k + 1)))
            )
        )
    for half in range(2):
        arrive(ninth, 3 * half, 3 * half + 3)
        arrive(passed[half])
        lax.fori_loop(2 * half, 2 * half + 2, final, 0)

    for copy, count in exchanges:

        def drain(k, carry, copy=copy):
            copy(k).wait_send()
            return carry

        lax.fori_loop(0, count, drain, 0)
    for x in range(4):
        out_copy(x).wait()
    out_copy_s.wait()


def deliver(g, w, b, to_g, to_w, to_b, sem):
    moves = [pltpu.make_async_copy(b, to_b, sem.at[6])]
    for ri in range(2):
        for half in range(2):
            rows = slice(40 * half, 40 * half + 40)
            moves.append(
                pltpu.make_async_copy(w.at[ri, rows], to_w.at[ri, rows], sem.at[2 * ri + half])
            )
    for half in range(2):
        rows = slice(2 * half, 2 * half + 2)
        moves.append(pltpu.make_async_copy(g.at[rows], to_g.at[rows], sem.at[4 + half]))
    for move in moves:
        move.start()
    for move in moves:
        move.wait()


N_COPIES = 14 + 7 + 3 + 7 + 1 + 7 + 7 + 3 + 15 + 15 + 3 + 7 + 14


def local(inputs, preactivation, cotangent, spectral, bypass, tables):
    weight = spectral.transpose(0, 1, 3, 2, 4).reshape(2, 80, C * C)
    vmem = pl.BlockSpec(memory_space=pltpu.VMEM)
    anywhere = pl.BlockSpec(memory_space=pl.ANY)
    held = [
        pltpu.VMEM(tables[k].shape[1:] if k in PICKED else tables[k].shape, BF16) for k in ORDER
    ]
    blocks = [
        pltpu.VMEM((4, 128, 256), BF16),
        pltpu.VMEM((4, 128, 256), BF16),
        pltpu.VMEM((4, 128, 256), BF16),
        pltpu.VMEM((2, 80, C * C), BF16),
        pltpu.VMEM((C, C), BF16),
        pltpu.VMEM((4, 128, 256), BF16),
        pltpu.VMEM((2, 80, C * C), F32),
        pltpu.SemaphoreType.DMA((5,)),
        pltpu.SemaphoreType.DMA((5,)),
        pltpu.VMEM((4, 128, 256), BF16),
        pltpu.VMEM((4, 128, 256), F32),
        pltpu.VMEM((8, 5, 4, 8, 128), BF16),
        pltpu.VMEM((7, 5, 4, 8, 128), BF16),
        pltpu.VMEM((8, 3, 8, 128), BF16),
        pltpu.VMEM((8, 3, 8, 128), BF16),
        pltpu.VMEM((4, 64, 384), BF16),
        pltpu.VMEM((3, 64, 384), BF16),
        pltpu.VMEM((16, 10, 128), BF16),
        pltpu.VMEM((16, 10, 128), BF16),
        pltpu.VMEM((8, 8, 128), BF16),
        pltpu.VMEM((16, 8, 128), BF16),
        pltpu.VMEM((4, 16, 8, 128), BF16),
        pltpu.VMEM((8, 16, 128), BF16),
        pltpu.VMEM((8, 16, 128), BF16),
        pltpu.VMEM((4, 3, 8, 128), BF16),
        pltpu.VMEM((8, 4, 3, 8, 128), BF16),
        pltpu.VMEM((8, 128), F32),
        pltpu.VMEM((16, 16, 128), F32),
        pltpu.VMEM((8, 8, 128), F32),
        pltpu.VMEM((4, 1, 128), F32),
        pltpu.VMEM((8, 1, 128), F32),
        pltpu.VMEM((2, 1, 128), F32),
        pltpu.VMEM((8, 1, 128), F32),
        pltpu.VMEM((4, 64, 512), BF16),
        pltpu.VMEM((256, 128), F32),
        pltpu.VMEM((256, 256), F32),
        pltpu.VMEM((256, 256), BF16),
        pltpu.VMEM((320, 128), BF16),
        pltpu.VMEM((160, 256), F32),
        pltpu.SemaphoreType.DMA((len(ORDER),)),
        pltpu.SemaphoreType.DMA((N_COPIES,)),
        pltpu.SemaphoreType.DMA((N_COPIES,)),
    ]
    results = pl.pallas_call(
        kernel,
        out_shape=(
            jax.ShapeDtypeStruct((4, 128, 256), BF16),
            jax.ShapeDtypeStruct((2, 80, C * C), F32),
            jax.ShapeDtypeStruct((C, C), F32),
        ),
        in_specs=[anywhere] * (5 + len(ORDER)),
        out_specs=(anywhere, anywhere, vmem),
        scratch_shapes=held + blocks,
        compiler_params=pltpu.CompilerParams(
            collective_id=0, has_side_effects=True, vmem_limit_bytes=62 * 1024 * 1024
        ),
        name="fno_backward",
    )(inputs, preactivation, cotangent, weight, bypass, *[tables[k] for k in ORDER])
    results = pl.pallas_call(
        deliver,
        out_shape=tuple(jax.ShapeDtypeStruct(o.shape, o.dtype) for o in results),
        in_specs=[anywhere] * 3,
        out_specs=(anywhere,) * 3,
        scratch_shapes=[pltpu.SemaphoreType.DMA((7,))],
        compiler_params=pltpu.CompilerParams(vmem_limit_bytes=62 * 1024 * 1024),
        name="deliver",
    )(*results)
    grad_inputs, grad_weight, grad_bypass = results
    grad_spectral = grad_weight.reshape(2, 2, 5, 8, C * C).transpose(0, 1, 3, 2, 4)
    return (grad_inputs, grad_spectral, grad_bypass)


def solution(mesh):
    tables = make_tables()

    def step(*args):
        return local(*args, {k: jnp.asarray(v) for k, v in tables.items()})

    return jax.shard_map(
        step,
        mesh=mesh,
        in_specs=(
            P("row", "col", None),
            P("row", "col", None),
            P("row", "col", None),
            P(None, "row", "col", None, None),
            P(),
        ),
        out_specs=(P("row", "col", None), P(None, "row", "col", None, None), P()),
        check_vma=False,
    )
```

```python
import math

import jax
import jax.numpy as jnp
import numpy as np
from jax import lax
from jax.experimental import pallas as pl
from jax.experimental.pallas import tpu as pltpu
from jax.sharding import PartitionSpec as P

MESH = pl.DeviceIdType.MESH
F32 = jnp.float32
BF16 = jnp.bfloat16
NX, NY, NT, C = 256, 1024, 8, 32
KX, KY, KT = 128, 64, 5
FACTOR = 1.0 / math.sqrt(float(NX * NY * NT * KX * KY * KT))
BYPASS_SCALE = 1.0 / math.sqrt(float(NX * NY * NT))


def turns(a, b, n):
    angle = 2.0 * np.pi * (np.multiply.outer(a, b) % n) / n
    return np.cos(angle), np.sin(angle)


def column_tables():
    forward, inverse = [], []
    for j in range(8):
        cos, sin = turns(np.arange(64), 128 * j + np.arange(128), NY)
        forward.append(np.concatenate([cos, -sin], 0))
        inverse.append(np.concatenate([cos.T, -sin.T], 1))
    return np.stack(forward), np.stack(inverse)


def time_tables():
    cos, sin = turns(np.arange(NT), np.arange(KT), NT)
    eye = np.eye(C)
    low = np.zeros((2, NT, C, 2, 4, C))
    for t in range(NT):
        for k in range(4):
            low[0, t, :, 0, k, :] = eye * cos[t, k]
            low[1, t, :, 0, k, :] = eye * sin[t, k]
            low[0, t, :, 1, k, :] = -eye * sin[t, k]
            low[1, t, :, 1, k, :] = eye * cos[t, k]
    high = np.zeros((2, 2, NT, C, 2, 2, C))
    for f in range(2):
        for t in range(NT):
            high[f, 0, t, :, f, 0, :] = eye * cos[t, 4]
            high[f, 1, t, :, f, 1, :] = eye * cos[t, 4]
    forward = np.concatenate(
        [low.reshape(512, 256), high[0].reshape(512, 128), high[1].reshape(512, 128)], 1
    )
    inverse = np.zeros((3, 4, C, 2, NT, C))
    for t in range(NT):
        for k in range(4):
            inverse[0, k, :, 0, t, :] = eye * cos[t, k]
            inverse[1, k, :, 0, t, :] = -eye * sin[t, k]
            inverse[0, k, :, 1, t, :] = eye * sin[t, k]
            inverse[1, k, :, 1, t, :] = eye * cos[t, k]
        inverse[2, 0, :, 0, t, :] = eye * cos[t, 4]
        inverse[2, 1, :, 1, t, :] = eye * cos[t, 4]
    return forward, inverse.reshape(384, 512)


def regroup_tables():
    direct = np.zeros((8, 3, 2, 4, 5, 4, 8))
    swapped = np.zeros((8, 3, 2, 4, 5, 4, 8))
    back = np.zeros((4, 3, 8, 8, 2, 2, 4))
    for k in range(8):
        for x in range(4):
            for tile in range(5):
                direct[k, tile // 2, tile % 2, x, tile, x, k] = 1.0
            swapped[k, 2, 1, x, 4, x, k] = 1.0
            for tile in range(3):
                back[x, tile, k, k, tile // 2, tile % 2, x] = 1.0
    lanes = np.zeros((2, 2, C, 2, 2, C))
    for f in range(2):
        lanes[f, 1, :, f, 0, :] = np.eye(C)
        lanes[f, 0, :, f, 1, :] = -np.eye(C)
    return (
        direct.reshape(192, 160),
        swapped.reshape(192, 160),
        lanes.reshape(128, 128),
        back.reshape(96, 128),
    )


def row_tables():
    k = np.arange(KX)
    freq = np.where(k < KX // 2, k, k - KX) % NX
    cos, sin = turns(freq, np.arange(NX), NX)
    cos = cos.reshape(4, 16, 2, 4, 4, 2, 2, 4)
    sin = sin.reshape(4, 16, 2, 4, 4, 2, 2, 4)
    forward = np.zeros((4, 4, 16, 2, 2, 4, 2, 2, 2, 4))
    for xx in range(4):
        c = cos[:, :, :, xx].transpose(0, 1, 2, 3, 5, 4, 6)
        s = sin[:, :, :, xx].transpose(0, 1, 2, 3, 5, 4, 6)
        forward[xx, :, :, :, 0, :, :, :, 0, :] = c
        forward[xx, :, :, :, 0, :, :, :, 1, :] = s
        forward[xx, :, :, :, 1, :, :, :, 1, :] = c
        forward[xx, :, :, :, 1, :, :, :, 0, :] = -s
    forward = forward.reshape(4, 256, 128)
    deal = np.zeros((16, 16, 3, 16, 2, 2))
    for q in range(16):
        for e in range(2):
            for ab in range(2):
                for slab in range(2):
                    deal[q, slab * 4 + e * 2 + ab, slab, q, e, ab] = 1.0
            deal[q, 8 + e, 2, q, e, 0] = 1.0
    inverse = np.zeros((4, 4, 2, 2, 2, 2, 4, 4, 16, 2, 2, 2))
    for xx in range(4):
        for slab in range(2):
            c = cos[:, :, :, xx].transpose(3, 5, 4, 6, 0, 1, 2)
            s = sin[:, :, :, xx].transpose(3, 5, 4, 6, 0, 1, 2)
            inverse[xx, :, :, :, slab, 0, :, :, :, slab, :, 0] = c
            inverse[xx, :, :, :, slab, 0, :, :, :, slab, :, 1] = -s
            inverse[xx, :, :, :, slab, 1, :, :, :, slab, :, 1] = c
            inverse[xx, :, :, :, slab, 1, :, :, :, slab, :, 0] = s
    return forward, inverse.reshape(4, 256, 512), deal.reshape(256, 192)


def mixing_tables():
    pick = np.zeros((2, 2, 2, 5, 8, 16, 16))
    pick_mask = np.zeros((2, 2, 2, 5, 8, 4, C))
    spread = np.zeros((8, 2, 2, 2, 4, 2, 5, 8))
    spread_mask = np.zeros((4, 2, 5, 8, 4, C))
    for ky in range(8):
        for e in range(2):
            for f in range(2):
                for ri in range(2):
                    for kt in range(4):
                        pick_mask[f, ri, e, kt, ky, kt, :] = 1.0
                    pick_mask[f, ri, e, 4, ky, f * 2 + ri, :] = 1.0
                    for zh in range(2):
                        source = (ky // 2) * 4 + zh * 2 + ky % 2
                        pick[f, ri, e, 0:4, ky, source, f * 4 + e * 2 + ri] = 1.0
                        pick[f, ri, e, 4, ky, source, 8 + e] = 1.0
            for kt in range(4):
                spread_mask[0, e, kt, ky, kt] = 1.0
                spread_mask[1, e, kt, ky, kt] = 1.0
                spread[ky, 0, e, 0, 0, e, kt, ky] = 1.0
                spread[ky, 0, e, 1, 1, e, kt, ky] = 1.0
            spread_mask[0, e, 4, ky, 0] = 1.0
            spread_mask[1, e, 4, ky, 1] = 1.0
            spread_mask[2, e, 4, ky, 0] = 1.0
            spread_mask[3, e, 4, ky, 1] = 1.0
            spread[ky, 1, e, 0, 0, e, 4, ky] = 1.0
            spread[ky, 1, e, 0, 1, e, 4, ky] = 1.0
            spread[ky, 1, e, 1, 2, e, 4, ky] = 1.0
            spread[ky, 1, e, 1, 3, e, 4, ky] = -1.0
    group = np.arange(128) % C
    lane = np.arange(C * C)
    by_in = (group[:, None] == lane[None, :] // C).astype(np.float64)
    by_out = (group[:, None] == lane[None, :256] % C).astype(np.float64)
    return (
        pick.reshape(320, 256),
        pick_mask.reshape(320, 128),
        by_in,
        by_out,
        by_in.T,
        spread.reshape(64, 320),
        spread_mask.reshape(320, 128),
    )


def make_tables():
    t = {}
    t["col_f"], t["col_i"] = column_tables()
    t["time_f"], t["time_i"] = time_tables()
    t["reg_a"], t["reg_b"], t["reg_l"], t["reg_c"] = regroup_tables()
    t["row_f"], t["row_i"], t["deal"] = row_tables()
    t["pick"], t["pick_m"], t["by_in"], t["by_out"], t["by_in_t"], t["spread"], t["spread_m"] = (
        mixing_tables()
    )
    return {k: np.asarray(v, np.float32).astype(jnp.bfloat16) for k, v in t.items()}


PICKED = ("col_f", "col_i", "row_f", "row_i")
ORDER = (
    "col_f", "time_f", "reg_a", "reg_b", "reg_l", "row_f", "deal", "pick", "pick_m", "by_in",
    "by_out", "by_in_t", "spread", "spread_m", "row_i", "reg_c", "time_i", "col_i",
)


def mm(a, b):
    return jnp.dot(a, b, preferred_element_type=F32)


def mm_full(a, b):
    return jnp.dot(a, b, preferred_element_type=F32, precision=lax.Precision.HIGHEST)


def gelu_slope(values):
    normal_cdf = 0.5 * (1.0 + lax.erf(values * (1.0 / math.sqrt(2.0))))
    density = jnp.exp(-0.5 * values * values) * (1.0 / math.sqrt(2.0 * math.pi))
    return normal_cdf + values * density


def pre_gradient(cot, pre):
    return (cot.astype(F32) * gelu_slope(pre.astype(F32))).astype(BF16)


def group_mask(shape):
    row = lax.broadcasted_iota(jnp.int32, shape, 0)
    lane = lax.broadcasted_iota(jnp.int32, shape, 1)
    return row, lane


def fold_lanes(values):
    values = values + pltpu.roll(values, 64, 1)
    return values + pltpu.roll(values, 32, 1)


def pack_bypass(product):
    row, lane = group_mask((256, 256))
    kept = jnp.where(row // C == lane // C, product, 0.0).reshape(8, C, 256).sum(0)
    wide = fold_lanes(kept[:, :128] + kept[:, 128:])
    row, lane = group_mask((C, 128))
    kept = jnp.where(row % 4 == lane // C, wide, 0.0)
    row, lane = group_mask((8, C))
    return mm_full(jnp.where(row == lane // 4, 1.0, 0.0), kept)


def unpack_bypass(packed):
    row, lane = group_mask((C, 8))
    wide = mm_full(jnp.where(row // 4 == lane, 1.0, 0.0), packed)
    row, lane = group_mask((C, 128))
    kept = fold_lanes(jnp.where(row % 4 == lane // C, wide, 0.0))
    return kept[:, :C] * BYPASS_SCALE


def block_bypass(bypass):
    row, lane = group_mask((256, C))
    tall = jnp.where(row % C == lane, 1.0, 0.0).astype(BF16)
    row, lane = group_mask((C, 256))
    flat = jnp.where(lane % C == row, 1.0, 0.0).astype(BF16)
    turned = lax.dot_general(tall, bypass, (((1,), (1,)), ((), ())), preferred_element_type=F32)
    full = mm(turned.astype(BF16), flat)
    row, lane = group_mask((256, 256))
    return jnp.where(row // C == lane // C, full, 0.0).astype(BF16)


def regroup_forward(total, reg_a, reg_b, reg_l):
    rows = total.astype(BF16)
    turned = mm(rows, reg_l).astype(BF16)
    return mm(reg_a, rows) + mm(reg_b, turned)


def final_rows(low_re, low_im, high, time_i, col_i):
    z = jnp.concatenate([low_re, low_im, high], axis=1)
    u = mm(z, time_i).astype(BF16)
    return mm(col_i, jnp.concatenate([u[:, :256], u[:, 256:]], axis=0))


def rows_of(block, count):
    return block.astype(F32).reshape(count, 128).astype(BF16)


def kernel(inp_hbm, pre_hbm, cot_hbm, spec_hbm, byp_hbm, *refs):
    n = len(ORDER)
    tables = dict(zip(ORDER, refs[:n]))
    out_g_hbm, out_s_hbm, out_b = refs[n : n + 3]
    held = dict(zip(ORDER, refs[n + 3 : 2 * n + 3]))
    (
        inp, pre, cot, spec, byp, out_g, out_s, arg_sem, out_sem,
        grad, plus, pieces, recv_col, send_s, recv_s, send_x, recv_x, send_q, recv_q,
        send_b, recv_b, recv_g, send_l, recv_l, send_c, recv_c,
        total, by_sum, wide_q, by_a, by_b, by_c, by_e,
        lined, high, product, blocks, chosen, repeated,
        table_sem, send_sem, recv_sem,
    ) = refs[2 * n + 3 :]

    row = lax.axis_index("row")
    j = lax.axis_index("col")
    xx = row // 16
    q = row % 16
    yy = q // 4
    zh = (q // 2) % 2
    core = q % 2
    s = yy * 2 + core

    z = zh * 8 + j

    def ring_step(k):
        d = 4 - (k + 1) // 2
        odd = k % 2
        return odd * d + (1 - odd) * (16 - d) + 8 * core * (1 - (k + 6) // 7)

    def z_index(o):
        return (z + o) % 16

    def z_peer(o):
        other = z_index(o)
        return xx * 16 + yy * 4 + (other // 8) * 2 + core, other % 8

    def s_index(k):
        return (s + k) % 8

    def q_of(other, half):
        return (other // 2) * 4 + half * 2 + other % 2

    def s_peer(k, half=zh):
        return xx * 16 + q_of(s_index(k), half), j


    def x_peer(k):
        return ((xx + k) % 4) * 16 + q, j

    barrier = pltpu.get_barrier_semaphore()
    everyone = (
        [z_peer(o) for o in range(1, 16)]
        + [s_peer(k) for k in range(1, 8)]
        + [s_peer(k, 1 - zh) for k in range(1, 8)]
        + [x_peer(k) for k in range(1, 4)]
    )
    for peer in everyone:
        pl.semaphore_signal(barrier, inc=1, device_id=peer, device_id_type=MESH)

    index_of = {"col_f": j, "col_i": j, "row_f": xx, "row_i": xx}
    loads = {}

    def load(name):
        source = tables[name].at[index_of[name]] if name in PICKED else tables[name]
        loads[name] = pltpu.make_async_copy(source, held[name], table_sem.at[ORDER.index(name)])
        loads[name].start()

    args = []
    for at, (source, target) in enumerate(
        ((inp_hbm, inp), (cot_hbm, cot), (pre_hbm, pre), (byp_hbm, byp), (spec_hbm, spec))
    ):
        args.append(pltpu.make_async_copy(source, target, arg_sem.at[at]))
    args[0].start()
    load("col_f")
    load("time_f")
    args[1].start()
    args[2].start()
    args[3].start()
    args[4].start()
    for name in ORDER[2:]:
        load(name)

    def table(name):
        return held[name][...]

    exchanges = []
    used = [0]

    def exchange(count, make):
        base = used[0]
        used[0] += count

        def copy(k):
            source, target, peer = make(k)
            return pltpu.make_async_remote_copy(
                src_ref=source,
                dst_ref=target,
                send_sem=send_sem.at[base + k],
                recv_sem=recv_sem.at[base + k],
                device_id=peer,
                device_id_type=MESH,
            )

        def start(k, carry):
            copy(k).start()
            return carry

        lax.fori_loop(0, count, start, 0)
        pair = copy, count
        exchanges.append(pair)
        return pair

    def arrive(pair, first=0, last=None):
        copy, count = pair

        def wait(k, carry):
            copy(k).wait_recv()
            return carry

        lax.fori_loop(first, count if last is None else last, wait, 0)

    loads["col_f"].wait()
    args[0].wait()

    def lines_in(x, carry):
        y = mm(held["col_f"][...], inp[x]).astype(BF16)
        lined[x, :, 0:256] = y[:64]
        lined[x, :, 256:512] = y[64:]
        return carry

    lax.fori_loop(0, 4, lines_in, 0)
    loads["time_f"].wait()
    r = mm(lined[...].reshape(256, 512), held["time_f"][:, 0:384])
    for x in range(4):
        rows = slice(64 * x, 64 * x + 64)
        pieces[:, 0, x] = r[rows, :128].reshape(8, 8, 128).astype(BF16)
        pieces[:, 1, x] = r[rows, 128:256].reshape(8, 8, 128).astype(BF16)
    high[...] = r[:, 256:]
    pl.semaphore_wait(barrier, len(everyone))
    first_in = exchange(
        7,
        lambda k: (
            pieces.at[z_index(ring_step(k)) % 8, 0:2],
            recv_col.at[k, 0:2],
            z_peer(ring_step(k)),
        ),
    )
    args[1].wait()
    args[2].wait()

    def lines_grad(x, carry):
        g = pre_gradient(cot[x], pre[x])
        grad[x] = g
        y = mm(held["col_f"][...], g).astype(BF16)
        lined[x, :, 0:256] = y[:64]
        lined[x, :, 256:512] = y[64:]
        return carry

    lax.fori_loop(0, 4, lines_grad, 0)
    rows = lined[...].reshape(256, 512)
    r = mm(rows, held["time_f"][:, 0:256])
    top = high[...] + mm(rows, held["time_f"][:, 384:512])
    for x in range(4):
        rows = slice(64 * x, 64 * x + 64)
        pieces[:, 2, x] = r[rows, :128].reshape(8, 8, 128).astype(BF16)
        pieces[:, 3, x] = r[rows, 128:].reshape(8, 8, 128).astype(BF16)
        pieces[:, 4, x] = top[rows].reshape(8, 8, 128).astype(BF16)
    first_grad = exchange(
        7,
        lambda k: (
            pieces.at[z_index(ring_step(k)) % 8, 2:5],
            recv_col.at[k, 2:5],
            z_peer(ring_step(k)),
        ),
    )

    product[...] = jnp.zeros((256, 256), F32)

    def add_product(x, carry):
        product[...] += lax.dot_general(
            inp[x], grad[x], (((0,), (0,)), ((), ())), preferred_element_type=F32
        )
        return carry

    lax.fori_loop(0, 4, add_product, 0)
    by_a[s] = pack_bypass(product[...])
    bypass_a = exchange(7, lambda k: (by_a.at[s], by_a.at[s], s_peer(k + 1)))
    args[3].wait()
    blocks[...] = block_bypass(byp[...])

    def pointwise(x, carry):
        plus[x] = mm(grad[x], blocks[...])
        return carry

    lax.fori_loop(0, 4, pointwise, 0)

    for name in ("reg_a", "reg_b", "reg_l"):
        loads[name].wait()
    arrive(first_in)
    arrive(first_grad)
    total[zh] = pieces[j].astype(F32).reshape(160, 128)
    total[1 - zh] = jnp.zeros((160, 128), F32)

    def add_terms(k, carry):
        half = z_index(32 - ring_step(k)) // 8
        total[half] += recv_col[k].astype(F32).reshape(160, 128)
        return carry

    lax.fori_loop(0, 7, add_terms, 0)
    for half in range(2):
        grouped = regroup_forward(total[half], table("reg_a"), table("reg_b"), table("reg_l"))
        send_s[:, half] = grouped.reshape(8, 3, 8, 128).astype(BF16)
    recv_s[s] = send_s[s]
    second = exchange(7, lambda k: (send_s.at[s_index(k + 1)], recv_s.at[s], s_peer(k + 1)))

    arrive(bypass_a)
    by_sum[...] = by_a[...].sum(0)
    by_b[xx] = by_sum[pl.ds(s, 1), :]
    bypass_b = exchange(3, lambda k: (by_b.at[xx], by_b.at[xx], x_peer(k + 1)))

    wide_q[...] = jnp.zeros((16, 16, 128), F32)
    loads["row_f"].wait()
    loads["deal"].wait()
    arrive(second)
    rows = jnp.concatenate([rows_of(recv_s[:, :, slab], 128) for slab in range(3)], axis=1)
    send_x[...] = mm(table("row_f"), rows).reshape(4, 64, 384).astype(BF16)
    fourth = exchange(
        3, lambda k: (send_x.at[(xx + k + 1) % 4], recv_x.at[k], x_peer(k + 1))
    )
    arrive(bypass_b)
    by_c[z] = by_b[...].sum(0)
    bypass_c = exchange(15, lambda k: (by_c.at[z], by_c.at[z], z_peer(k + 1)))
    arrive(fourth)
    summed = send_x[xx].astype(F32)
    for k in range(3):
        summed += recv_x[k].astype(F32)
    summed = summed.astype(BF16)
    summed = jnp.concatenate([summed[:, 128 * i : 128 * i + 128] for i in range(3)], axis=0)
    dealt = mm(table("deal"), summed).reshape(16, 16, 128)
    send_q[...] = dealt[:, 0:10].astype(BF16)

    fifth_far = exchange(
        8, lambda k: (send_q.at[q_of(s_index(k), 1 - zh)], recv_q.at[q], s_peer(k, 1 - zh))
    )
    fifth = exchange(
        7, lambda k: (send_q.at[q_of(s_index(k + 1), zh)], recv_q.at[q], s_peer(k + 1, zh))
    )
    recv_q[q] = send_q[q]
    for name in ("pick", "pick_m", "by_in", "by_out", "by_in_t", "spread", "spread_m"):
        loads[name].wait()
    args[4].wait()
    arrive(fifth)
    arrive(fifth_far)
    wide_q[:, 0:10] = recv_q[...].astype(F32)
    halves = wide_q[...].reshape(256, 128).astype(BF16)
    chosen[...] = (mm(table("pick"), halves) * table("pick_m").astype(F32)).astype(BF16)
    repeated[...] = mm(chosen[160:320, :], table("by_out"))

    def mix(m, carry):
        lanes = pl.ds(pl.multiple_of(m * 256, 256), 256)
        a = mm(chosen[0:160, :], held["by_in"][:, lanes])
        a_re, a_im = a[:80], a[80:]
        g_re = repeated[0:80, :]
        g_im = repeated[80:160, :]
        w_re = spec[0, :, lanes].astype(F32)
        w_im = spec[1, :, lanes].astype(F32)
        out_s[0, :, lanes] = FACTOR * (a_re * g_re + a_im * g_im)
        out_s[1, :, lanes] = FACTOR * (a_re * g_im - a_im * g_re)
        p_re = (w_re * g_re + w_im * g_im).astype(BF16)
        p_im = (w_re * g_im - w_im * g_re).astype(BF16)
        turn = held["by_in_t"][lanes, :]
        return carry + mm(jnp.concatenate([p_re, p_im], axis=0), turn)

    b = lax.fori_loop(0, 4, mix, jnp.zeros((160, 128), F32)) * FACTOR
    b_re, b_im = b[:80], b[80:]
    stack = jnp.concatenate([b_re, b_im, b_im, b_re], axis=0) * table("spread_m").astype(F32)
    back = mm(table("spread"), stack.astype(BF16))
    send_b[...] = back.reshape(8, 8, 128).astype(BF16)

    sixth_far = exchange(
        8, lambda k: (send_b.at[s_index(k)], recv_b.at[q], s_peer(k, 1 - zh))
    )
    sixth = exchange(7, lambda k: (send_b.at[s_index(k + 1)], recv_b.at[q], s_peer(k + 1)))
    recv_b[q] = send_b[s]
    out_copy_s = pltpu.make_async_copy(out_s, out_s_hbm, out_sem.at[4])
    out_copy_s.start()

    arrive(sixth)
    arrive(sixth_far)
    seventh = exchange(3, lambda k: (recv_b, recv_g.at[xx], x_peer(k + 1)))
    recv_g[xx] = recv_b[...]
    loads["row_i"].wait()
    loads["reg_c"].wait()
    arrive(seventh)
    lines = mm(table("row_i"), rows_of(recv_g[...], 512))
    send_l[...] = lines.reshape(8, 2, 16, 128).astype(BF16)
    eighth = exchange(7, lambda k: (send_l.at[s_index(k + 1)], recv_l.at[s], s_peer(k + 1)))
    recv_l[s] = send_l[s]
    arrive(bypass_c)
    by_e[s] = by_c[...].sum(0)
    bypass_e = exchange(7, lambda k: (by_e.at[s], by_e.at[s], s_peer(k + 1)))
    arrive(eighth)
    for half in range(2):
        turned = mm(table("reg_c"), rows_of(recv_l[:, half], 128))
        send_c[half] = turned.reshape(4, 3, 8, 128).astype(BF16)
    ninth = exchange(
        7,
        lambda k: (
            send_c.at[z_index(ring_step(k)) // 8],
            recv_c.at[j],
            z_peer(ring_step(k)),
        ),
    )
    recv_c[j] = send_c[zh]
    loads["time_i"].wait()
    loads["col_i"].wait()
    arrive(bypass_e)
    out_b[...] = unpack_bypass(by_e[...].reshape(8, 128))

    def out_copy(x):
        return pltpu.make_async_copy(out_g.at[x], out_g_hbm.at[x], out_sem.at[x])

    def final(x, carry):
        parts = [rows_of(recv_c[:, x, tile], 64) for tile in range(3)]
        rows = final_rows(*parts, held["time_i"][...], held["col_i"][...])
        out_g[x] = (rows + plus[x]).astype(BF16)
        out_copy(x).start()
        return carry

    arrive(ninth)
    lax.fori_loop(0, 4, final, 0)

    for copy, count in exchanges:

        def drain(k, carry, copy=copy):
            copy(k).wait_send()
            return carry

        lax.fori_loop(0, count, drain, 0)
    for x in range(4):
        out_copy(x).wait()
    out_copy_s.wait()


def deliver(g, w, b, to_g, to_w, to_b, held_g, held_w, held_b, sem_in, sem_out):
    pieces = [(b, held_b, to_b)]
    pieces += [(w.at[i, h], held_w.at[i, h], to_w.at[i, h]) for i in range(2) for h in HALVES]
    pieces += [(g.at[i], held_g.at[i], to_g.at[i]) for i in range(4)]
    fetch = [
        pltpu.make_async_copy(p[0], p[1], sem_in.at[i]) for i, p in enumerate(pieces)
    ]
    store = [
        pltpu.make_async_copy(p[1], p[2], sem_out.at[i]) for i, p in enumerate(pieces)
    ]
    for copy in fetch:
        copy.start()
    for i in range(len(pieces)):
        fetch[i].wait()
        store[i].start()
    for copy in store:
        copy.wait()


HALVES = (slice(0, 40), slice(40, 80))
N_COPIES = 14 + 7 + 3 + 15 + 7 + 7 + 3 + 15 + 15 + 3 + 7 + 7


def local(inputs, preactivation, cotangent, spectral, bypass, tables):
    weight = spectral.transpose(0, 1, 3, 2, 4).reshape(2, 80, C * C)
    vmem = pl.BlockSpec(memory_space=pltpu.VMEM)
    anywhere = pl.BlockSpec(memory_space=pl.ANY)
    held = [
        pltpu.VMEM(tables[k].shape[1:] if k in PICKED else tables[k].shape, BF16) for k in ORDER
    ]
    blocks = [
        pltpu.VMEM((4, 128, 256), BF16),
        pltpu.VMEM((4, 128, 256), BF16),
        pltpu.VMEM((4, 128, 256), BF16),
        pltpu.VMEM((2, 80, C * C), BF16),
        pltpu.VMEM((C, C), BF16),
        pltpu.VMEM((4, 128, 256), BF16),
        pltpu.VMEM((2, 80, C * C), F32),
        pltpu.SemaphoreType.DMA((5,)),
        pltpu.SemaphoreType.DMA((5,)),
        pltpu.VMEM((4, 128, 256), BF16),
        pltpu.VMEM((4, 128, 256), F32),
        pltpu.VMEM((8, 5, 4, 8, 128), BF16),
        pltpu.VMEM((7, 5, 4, 8, 128), BF16),
        pltpu.VMEM((8, 2, 3, 8, 128), BF16),
        pltpu.VMEM((8, 2, 3, 8, 128), BF16),
        pltpu.VMEM((4, 64, 384), BF16),
        pltpu.VMEM((3, 64, 384), BF16),
        pltpu.VMEM((16, 10, 128), BF16),
        pltpu.VMEM((16, 10, 128), BF16),
        pltpu.VMEM((8, 8, 128), BF16),
        pltpu.VMEM((16, 8, 128), BF16),
        pltpu.VMEM((4, 16, 8, 128), BF16),
        pltpu.VMEM((8, 2, 16, 128), BF16),
        pltpu.VMEM((8, 2, 16, 128), BF16),
        pltpu.VMEM((2, 4, 3, 8, 128), BF16),
        pltpu.VMEM((8, 4, 3, 8, 128), BF16),
        pltpu.VMEM((2, 160, 128), F32),
        pltpu.VMEM((8, 128), F32),
        pltpu.VMEM((16, 16, 128), F32),
        pltpu.VMEM((8, 8, 128), F32),
        pltpu.VMEM((4, 1, 128), F32),
        pltpu.VMEM((16, 1, 128), F32),
        pltpu.VMEM((8, 1, 128), F32),
        pltpu.VMEM((4, 64, 512), BF16),
        pltpu.VMEM((256, 128), F32),
        pltpu.VMEM((256, 256), F32),
        pltpu.VMEM((256, 256), BF16),
        pltpu.VMEM((320, 128), BF16),
        pltpu.VMEM((160, 256), F32),
        pltpu.SemaphoreType.DMA((len(ORDER),)),
        pltpu.SemaphoreType.DMA((N_COPIES,)),
        pltpu.SemaphoreType.DMA((N_COPIES,)),
    ]
    results = pl.pallas_call(
        kernel,
        out_shape=(
            jax.ShapeDtypeStruct((4, 128, 256), BF16),
            jax.ShapeDtypeStruct((2, 80, C * C), F32),
            jax.ShapeDtypeStruct((C, C), F32),
        ),
        in_specs=[anywhere] * (5 + len(ORDER)),
        out_specs=(anywhere, anywhere, vmem),
        scratch_shapes=held + blocks,
        compiler_params=pltpu.CompilerParams(
            collective_id=0, has_side_effects=True, vmem_limit_bytes=62 * 1024 * 1024
        ),
        name="fno_backward",
    )(inputs, preactivation, cotangent, weight, bypass, *[tables[k] for k in ORDER])
    results = pl.pallas_call(
        deliver,
        out_shape=tuple(jax.ShapeDtypeStruct(o.shape, o.dtype) for o in results),
        in_specs=[anywhere] * 3,
        out_specs=(anywhere,) * 3,
        scratch_shapes=[pltpu.VMEM(o.shape, o.dtype) for o in results]
        + [pltpu.SemaphoreType.DMA((9,)), pltpu.SemaphoreType.DMA((9,))],
        compiler_params=pltpu.CompilerParams(vmem_limit_bytes=62 * 1024 * 1024),
        name="deliver",
    )(*results)
    grad_inputs, grad_weight, grad_bypass = results
    grad_spectral = grad_weight.reshape(2, 2, 5, 8, C * C).transpose(0, 1, 3, 2, 4)
    return (grad_inputs, grad_spectral, grad_bypass)


def solution(mesh):
    tables = make_tables()

    def step(*args):
        return local(*args, {k: jnp.asarray(v) for k, v in tables.items()})

    return jax.shard_map(
        step,
        mesh=mesh,
        in_specs=(
            P("row", "col", None),
            P("row", "col", None),
            P("row", "col", None),
            P(None, "row", "col", None, None),
            P(),
        ),
        out_specs=(P("row", "col", None), P(None, "row", "col", None, None), P()),
        check_vma=False,
    )
```

```python
import math

import jax
import jax.numpy as jnp
import numpy as np
from jax import lax
from jax.experimental import pallas as pl
from jax.experimental.pallas import tpu as pltpu
from jax.sharding import PartitionSpec as P

MESH = pl.DeviceIdType.MESH
F32 = jnp.float32
BF16 = jnp.bfloat16
NX, NY, NT, C = 256, 1024, 8, 32
KX, KY, KT = 128, 64, 5
FACTOR = 1.0 / math.sqrt(float(NX * NY * NT * KX * KY * KT))
BYPASS_SCALE = 1.0 / math.sqrt(float(NX * NY * NT))


def turns(a, b, n):
    angle = 2.0 * np.pi * (np.multiply.outer(a, b) % n) / n
    return np.cos(angle), np.sin(angle)


def column_tables():
    forward, inverse = [], []
    for j in range(8):
        cos, sin = turns(np.arange(64), 128 * j + np.arange(128), NY)
        forward.append(np.concatenate([cos, -sin], 0))
        inverse.append(np.concatenate([cos.T, -sin.T], 1))
    return np.stack(forward), np.stack(inverse)


def time_tables():
    cos, sin = turns(np.arange(NT), np.arange(KT), NT)
    eye = np.eye(C)
    low = np.zeros((2, NT, C, 2, 4, C))
    for t in range(NT):
        for k in range(4):
            low[0, t, :, 0, k, :] = eye * cos[t, k]
            low[1, t, :, 0, k, :] = eye * sin[t, k]
            low[0, t, :, 1, k, :] = -eye * sin[t, k]
            low[1, t, :, 1, k, :] = eye * cos[t, k]
    high = np.zeros((2, 2, NT, C, 2, 2, C))
    for f in range(2):
        for t in range(NT):
            high[f, 0, t, :, f, 0, :] = eye * cos[t, 4]
            high[f, 1, t, :, f, 1, :] = eye * cos[t, 4]
    forward = np.concatenate(
        [low.reshape(512, 256), high[0].reshape(512, 128), high[1].reshape(512, 128)], 1
    )
    inverse = np.zeros((3, 4, C, 2, NT, C))
    for t in range(NT):
        for k in range(4):
            inverse[0, k, :, 0, t, :] = eye * cos[t, k]
            inverse[1, k, :, 0, t, :] = -eye * sin[t, k]
            inverse[0, k, :, 1, t, :] = eye * sin[t, k]
            inverse[1, k, :, 1, t, :] = eye * cos[t, k]
        inverse[2, 0, :, 0, t, :] = eye * cos[t, 4]
        inverse[2, 1, :, 1, t, :] = eye * cos[t, 4]
    return forward, inverse.reshape(384, 512)


def regroup_tables():
    direct = np.zeros((8, 3, 2, 4, 5, 4, 8))
    swapped = np.zeros((8, 3, 2, 4, 5, 4, 8))
    back = np.zeros((4, 3, 8, 8, 2, 2, 4))
    for k in range(8):
        for x in range(4):
            for tile in range(5):
                direct[k, tile // 2, tile % 2, x, tile, x, k] = 1.0
            swapped[k, 2, 1, x, 4, x, k] = 1.0
            for tile in range(3):
                back[x, tile, k, k, tile // 2, tile % 2, x] = 1.0
    return (
        direct.reshape(192, 160),
        swapped.reshape(192, 160)[:, 128:],
        back.reshape(96, 128),
    )


def row_tables():
    k = np.arange(KX)
    freq = np.where(k < KX // 2, k, k - KX) % NX
    cos, sin = turns(freq, np.arange(NX), NX)
    cos = cos.reshape(4, 16, 2, 4, 4, 2, 2, 4)
    sin = sin.reshape(4, 16, 2, 4, 4, 2, 2, 4)
    forward = np.zeros((4, 4, 16, 2, 2, 4, 2, 2, 2, 4))
    for xx in range(4):
        c = cos[:, :, :, xx].transpose(0, 1, 2, 3, 5, 4, 6)
        s = sin[:, :, :, xx].transpose(0, 1, 2, 3, 5, 4, 6)
        forward[xx, :, :, :, 0, :, :, :, 0, :] = c
        forward[xx, :, :, :, 0, :, :, :, 1, :] = s
        forward[xx, :, :, :, 1, :, :, :, 1, :] = c
        forward[xx, :, :, :, 1, :, :, :, 0, :] = -s
    forward = forward.reshape(4, 256, 128)
    deal = np.zeros((16, 16, 3, 16, 2, 2))
    for q in range(16):
        for e in range(2):
            for ab in range(2):
                for slab in range(2):
                    deal[q, slab * 4 + e * 2 + ab, slab, q, e, ab] = 1.0
            deal[q, 8 + e, 2, q, e, 0] = 1.0
    inverse = np.zeros((4, 4, 2, 2, 2, 2, 4, 4, 16, 2, 2, 2))
    for xx in range(4):
        for slab in range(2):
            c = cos[:, :, :, xx].transpose(3, 5, 4, 6, 0, 1, 2)
            s = sin[:, :, :, xx].transpose(3, 5, 4, 6, 0, 1, 2)
            inverse[xx, :, :, :, slab, 0, :, :, :, slab, :, 0] = c
            inverse[xx, :, :, :, slab, 0, :, :, :, slab, :, 1] = -s
            inverse[xx, :, :, :, slab, 1, :, :, :, slab, :, 1] = c
            inverse[xx, :, :, :, slab, 1, :, :, :, slab, :, 0] = s
    return forward, inverse.reshape(4, 256, 512), deal.reshape(256, 192)


def mixing_tables():
    pick = np.zeros((2, 2, 2, 5, 8, 16, 16))
    pick_mask = np.zeros((2, 2, 2, 5, 8, 4, C))
    spread = np.zeros((8, 2, 2, 2, 4, 2, 5, 8))
    spread_mask = np.zeros((4, 2, 5, 8, 4, C))
    for ky in range(8):
        for e in range(2):
            for f in range(2):
                for ri in range(2):
                    for kt in range(4):
                        pick_mask[f, ri, e, kt, ky, kt, :] = 1.0
                    pick_mask[f, ri, e, 4, ky, f * 2 + ri, :] = 1.0
                    for zh in range(2):
                        source = (ky // 2) * 4 + zh * 2 + ky % 2
                        pick[f, ri, e, 0:4, ky, source, f * 4 + e * 2 + ri] = 1.0
                        pick[f, ri, e, 4, ky, source, 8 + e] = 1.0
            for kt in range(4):
                spread_mask[0, e, kt, ky, kt] = 1.0
                spread_mask[1, e, kt, ky, kt] = 1.0
                spread[ky, 0, e, 0, 0, e, kt, ky] = 1.0
                spread[ky, 0, e, 1, 1, e, kt, ky] = 1.0
            spread_mask[0, e, 4, ky, 0] = 1.0
            spread_mask[1, e, 4, ky, 1] = 1.0
            spread_mask[2, e, 4, ky, 0] = 1.0
            spread_mask[3, e, 4, ky, 1] = 1.0
            spread[ky, 1, e, 0, 0, e, 4, ky] = 1.0
            spread[ky, 1, e, 0, 1, e, 4, ky] = 1.0
            spread[ky, 1, e, 1, 2, e, 4, ky] = 1.0
            spread[ky, 1, e, 1, 3, e, 4, ky] = -1.0
    group = np.arange(128) % C
    lane = np.arange(C * C)
    by_in = (group[:, None] == lane[None, :] // C).astype(np.float64)
    by_out = (group[:, None] == lane[None, :256] % C).astype(np.float64)
    return (
        pick.reshape(320, 256),
        pick_mask.reshape(320, 128),
        by_in,
        by_out,
        by_in.T,
        spread.reshape(64, 320),
        spread_mask.reshape(320, 128),
    )


def make_tables():
    t = {}
    t["col_f"], t["col_i"] = column_tables()
    t["time_f"], t["time_i"] = time_tables()
    t["reg_a"], t["reg_b"], t["reg_c"] = regroup_tables()
    t["row_f"], t["row_i"], t["deal"] = row_tables()
    t["pick"], t["pick_m"], t["by_in"], t["by_out"], t["by_in_t"], t["spread"], t["spread_m"] = (
        mixing_tables()
    )
    return {k: np.asarray(v, np.float32).astype(jnp.bfloat16) for k, v in t.items()}


PICKED = ("col_f", "col_i", "row_f", "row_i")
ORDER = (
    "col_f", "time_f", "reg_a", "reg_b", "row_f", "deal", "pick", "pick_m", "by_in",
    "by_out", "by_in_t", "spread", "spread_m", "row_i", "reg_c", "time_i", "col_i",
)


def mm(a, b):
    return jnp.dot(a, b, preferred_element_type=F32)


def mm_full(a, b):
    return jnp.dot(a, b, preferred_element_type=F32, precision=lax.Precision.HIGHEST)


def gelu_slope(values):
    normal_cdf = 0.5 * (1.0 + lax.erf(values * (1.0 / math.sqrt(2.0))))
    density = jnp.exp(-0.5 * values * values) * (1.0 / math.sqrt(2.0 * math.pi))
    return normal_cdf + values * density


def pre_gradient(cot, pre):
    return (cot.astype(F32) * gelu_slope(pre.astype(F32))).astype(BF16)


def group_mask(shape):
    row = lax.broadcasted_iota(jnp.int32, shape, 0)
    lane = lax.broadcasted_iota(jnp.int32, shape, 1)
    return row, lane


def fold_lanes(values):
    values = values + pltpu.roll(values, 64, 1)
    return values + pltpu.roll(values, 32, 1)


def pack_bypass(product):
    row, lane = group_mask((256, 256))
    kept = jnp.where(row // C == lane // C, product, 0.0).reshape(8, C, 256).sum(0)
    wide = fold_lanes(kept[:, :128] + kept[:, 128:])
    row, lane = group_mask((C, 128))
    kept = jnp.where(row % 4 == lane // C, wide, 0.0)
    row, lane = group_mask((8, C))
    return mm_full(jnp.where(row == lane // 4, 1.0, 0.0), kept)


def unpack_bypass(packed):
    row, lane = group_mask((C, 8))
    wide = mm_full(jnp.where(row // 4 == lane, 1.0, 0.0), packed)
    row, lane = group_mask((C, 128))
    kept = fold_lanes(jnp.where(row % 4 == lane // C, wide, 0.0))
    return kept[:, :C] * BYPASS_SCALE


def block_bypass(bypass):
    row, lane = group_mask((256, C))
    tall = jnp.where(row % C == lane, 1.0, 0.0).astype(BF16)
    row, lane = group_mask((C, 256))
    flat = jnp.where(lane % C == row, 1.0, 0.0).astype(BF16)
    turned = lax.dot_general(tall, bypass, (((1,), (1,)), ((), ())), preferred_element_type=F32)
    full = mm(turned.astype(BF16), flat)
    row, lane = group_mask((256, 256))
    return jnp.where(row // C == lane // C, full, 0.0).astype(BF16)


def regroup_forward(total, reg_a, reg_b):
    rows = total.astype(BF16)
    last = total[128:160]
    lane = lax.broadcasted_iota(jnp.int32, (C, 128), 1)
    real = (lane // C) % 2 == 0
    turned = jnp.where(real, pltpu.roll(last, 96, 1), -pltpu.roll(last, 32, 1))
    return mm(reg_a, rows) + mm(reg_b, turned.astype(BF16))


def final_rows(low_re, low_im, high, time_i, col_i):
    z = jnp.concatenate([low_re, low_im, high], axis=1)
    u = mm(z, time_i).astype(BF16)
    return mm(col_i, jnp.concatenate([u[:, :256], u[:, 256:]], axis=0))


def rows_of(block, count):
    return block.astype(F32).reshape(count, 128).astype(BF16)


def kernel(inp_hbm, pre_hbm, cot_hbm, spec_hbm, byp_hbm, *refs):
    n = len(ORDER)
    tables = dict(zip(ORDER, refs[:n]))
    out_g_hbm, out_s_hbm, out_b = refs[n : n + 3]
    held = dict(zip(ORDER, refs[n + 3 : 2 * n + 3]))
    (
        inp, pre, cot, spec, byp, out_g, out_s, arg_sem, out_sem,
        grad, plus, pieces, recv_col, send_s, recv_s, send_x, recv_x, send_q, recv_q,
        send_b, recv_b, recv_g, send_l, recv_l, send_c, recv_c,
        total, by_sum, wide_q, by_a, by_b, by_c, by_e,
        lined, high, product, blocks, chosen, repeated,
        table_sem, send_sem, recv_sem,
    ) = refs[2 * n + 3 :]

    row = lax.axis_index("row")
    j = lax.axis_index("col")
    xx = row // 16
    q = row % 16
    yy = q // 4
    zh = (q // 2) % 2
    core = q % 2
    s = yy * 2 + core

    z = zh * 8 + j

    def ring_step(k):
        d = 4 - lax.div(k + 1, 2)
        odd = lax.rem(k, 2)
        return odd * d + (1 - odd) * (16 - d) + 8 * core * (1 - lax.div(k + 6, 7))

    def z_index(o):
        return lax.rem(z + o, 16)

    def z_peer(o):
        other = z_index(o)
        return xx * 16 + yy * 4 + lax.div(other, 8) * 2 + core, lax.rem(other, 8)

    def s_index(k):
        return lax.rem(s + k, 8)

    def q_of(other, half):
        return lax.div(other, 2) * 4 + half * 2 + lax.rem(other, 2)

    def s_peer(k, half=zh):
        return xx * 16 + q_of(s_index(k), half), j


    def x_peer(k):
        return lax.rem(xx + k, 4) * 16 + q, j

    barrier = pltpu.get_barrier_semaphore()
    everyone = (
        [z_peer(o) for o in (1, 2, 3, 4, 12, 13, 14, 15)]
        + [s_peer(k) for k in range(1, 8)]
        + [x_peer(k) for k in range(1, 4)]
    )
    for peer in everyone:
        pl.semaphore_signal(barrier, inc=1, device_id=peer, device_id_type=MESH)

    index_of = {"col_f": j, "col_i": j, "row_f": xx, "row_i": xx}
    loads = {}

    def load(name):
        source = tables[name].at[index_of[name]] if name in PICKED else tables[name]
        loads[name] = pltpu.make_async_copy(source, held[name], table_sem.at[ORDER.index(name)])
        loads[name].start()

    args = []
    for at, (source, target) in enumerate(
        ((inp_hbm, inp), (cot_hbm, cot), (pre_hbm, pre), (byp_hbm, byp), (spec_hbm, spec))
    ):
        args.append(pltpu.make_async_copy(source, target, arg_sem.at[at]))
    args[0].start()
    load("col_f")
    load("time_f")
    args[1].start()
    args[2].start()
    args[3].start()
    args[4].start()
    for name in ORDER[2:]:
        load(name)

    def table(name):
        return held[name][...]

    exchanges = []
    used = [0]

    def exchange(count, make):
        base = used[0]
        used[0] += count

        def copy(k):
            source, target, peer = make(k)
            return pltpu.make_async_remote_copy(
                src_ref=source,
                dst_ref=target,
                send_sem=send_sem.at[base + k],
                recv_sem=recv_sem.at[base + k],
                device_id=peer,
                device_id_type=MESH,
            )

        def start(k, carry):
            copy(k).start()
            return carry

        lax.fori_loop(0, count, start, 0)
        pair = copy, count
        exchanges.append(pair)
        return pair

    def arrive(pair, first=0, last=None):
        copy, count = pair

        def wait(k, carry):
            copy(k).wait_recv()
            return carry

        lax.fori_loop(first, count if last is None else last, wait, 0)

    def drain():
        for copy, count in exchanges:

            def left(k, carry, copy=copy):
                copy(k).wait_send()
                return carry

            lax.fori_loop(0, count, left, 0)
        exchanges.clear()

    loads["col_f"].wait()
    args[0].wait()

    def lines_in(x, carry):
        y = mm(held["col_f"][...], inp[x]).astype(BF16)
        lined[x, :, 0:256] = y[:64]
        lined[x, :, 256:512] = y[64:]
        return carry

    lax.fori_loop(0, 4, lines_in, 0)
    loads["time_f"].wait()
    r = mm(lined[...].reshape(256, 512), held["time_f"][:, 0:384])
    for x in range(4):
        rows = slice(64 * x, 64 * x + 64)
        pieces[:, 0, x] = r[rows, :128].reshape(8, 8, 128).astype(BF16)
        pieces[:, 1, x] = r[rows, 128:256].reshape(8, 8, 128).astype(BF16)
    high[...] = r[:, 256:]
    pl.semaphore_wait(barrier, len(everyone))
    first_in = exchange(
        7,
        lambda k: (
            pieces.at[lax.rem(z_index(ring_step(k)), 8), 0:2],
            recv_col.at[k, 0:2],
            z_peer(ring_step(k)),
        ),
    )
    args[1].wait()
    args[2].wait()

    def lines_grad(x, carry):
        g = pre_gradient(cot[x], pre[x])
        grad[x] = g
        y = mm(held["col_f"][...], g).astype(BF16)
        lined[x, :, 0:256] = y[:64]
        lined[x, :, 256:512] = y[64:]
        return carry

    lax.fori_loop(0, 4, lines_grad, 0)
    rows = lined[...].reshape(256, 512)
    r = mm(rows, held["time_f"][:, 0:256])
    top = high[...] + mm(rows, held["time_f"][:, 384:512])
    for x in range(4):
        rows = slice(64 * x, 64 * x + 64)
        pieces[:, 2, x] = r[rows, :128].reshape(8, 8, 128).astype(BF16)
        pieces[:, 3, x] = r[rows, 128:].reshape(8, 8, 128).astype(BF16)
        pieces[:, 4, x] = top[rows].reshape(8, 8, 128).astype(BF16)
    first_grad = exchange(
        7,
        lambda k: (
            pieces.at[lax.rem(z_index(ring_step(k)), 8), 2:5],
            recv_col.at[k, 2:5],
            z_peer(ring_step(k)),
        ),
    )

    product[...] = jnp.zeros((256, 256), F32)

    def add_product(x, carry):
        product[...] += lax.dot_general(
            inp[x], grad[x], (((0,), (0,)), ((), ())), preferred_element_type=F32
        )
        return carry

    lax.fori_loop(0, 4, add_product, 0)
    by_a[s] = pack_bypass(product[...])
    bypass_a = exchange(7, lambda k: (by_a.at[s], by_a.at[s], s_peer(k + 1)))
    args[3].wait()
    blocks[...] = block_bypass(byp[...])

    def pointwise(x, carry):
        plus[x] = mm(grad[x], blocks[...])
        return carry

    lax.fori_loop(0, 4, pointwise, 0)

    for name in ("reg_a", "reg_b"):
        loads[name].wait()
    arrive(first_in)
    arrive(first_grad)
    total[zh] = pieces[j].astype(F32).reshape(160, 128)
    total[1 - zh] = jnp.zeros((160, 128), F32)

    def add_terms(k, carry):
        half = lax.div(z_index(32 - ring_step(k)), 8)
        total[half] += recv_col[k].astype(F32).reshape(160, 128)
        return carry

    lax.fori_loop(0, 7, add_terms, 0)
    for half in range(2):
        grouped = regroup_forward(total[half], table("reg_a"), table("reg_b"))
        send_s[:, half] = grouped.reshape(8, 3, 8, 128).astype(BF16)
    recv_s[s] = send_s[s]
    second = exchange(7, lambda k: (send_s.at[s_index(k + 1)], recv_s.at[s], s_peer(k + 1)))

    arrive(bypass_a)
    by_sum[...] = by_a[...].sum(0)
    by_b[xx] = by_sum[pl.ds(s, 1), :]
    bypass_b = exchange(3, lambda k: (by_b.at[xx], by_b.at[xx], x_peer(k + 1)))

    wide_q[...] = jnp.zeros((16, 16, 128), F32)
    loads["row_f"].wait()
    loads["deal"].wait()
    arrive(second)
    rows = jnp.concatenate([rows_of(recv_s[:, :, slab], 128) for slab in range(3)], axis=1)
    send_x[...] = mm(table("row_f"), rows).reshape(4, 64, 384).astype(BF16)
    fourth = exchange(
        3, lambda k: (send_x.at[lax.rem(xx + k + 1, 4)], recv_x.at[k], x_peer(k + 1))
    )
    arrive(fourth)
    summed = send_x[xx].astype(F32)
    for k in range(3):
        summed += recv_x[k].astype(F32)
    summed = summed.astype(BF16)
    summed = jnp.concatenate([summed[:, 128 * i : 128 * i + 128] for i in range(3)], axis=0)
    dealt = mm(table("deal"), summed).reshape(16, 16, 128)
    send_q[...] = dealt[:, 0:10].astype(BF16)

    earlier = list(exchanges)
    exchanges.clear()
    fifth_far = exchange(
        8, lambda k: (send_q.at[q_of(s_index(k), 1 - zh)], recv_q.at[q], s_peer(k, 1 - zh))
    )
    fifth = exchange(
        7, lambda k: (send_q.at[q_of(s_index(k + 1), zh)], recv_q.at[q], s_peer(k + 1, zh))
    )
    recv_q[q] = send_q[q]
    arrive(bypass_b)
    by_c[z] = by_b[...].sum(0)
    bypass_c = exchange(15, lambda k: (by_c.at[z], by_c.at[z], z_peer(k + 1)))
    later = list(exchanges)
    exchanges[:] = earlier
    drain()
    for name in ("pick", "pick_m", "by_in", "by_out", "by_in_t", "spread", "spread_m"):
        loads[name].wait()
    args[4].wait()
    arrive(fifth)
    arrive(fifth_far)
    wide_q[:, 0:10] = recv_q[...].astype(F32)
    halves = wide_q[...].reshape(256, 128).astype(BF16)
    chosen[...] = (mm(table("pick"), halves) * table("pick_m").astype(F32)).astype(BF16)
    repeated[...] = mm(chosen[160:320, :], table("by_out"))

    def mix(m, carry):
        lanes = pl.ds(pl.multiple_of(m * 256, 256), 256)
        a = mm(chosen[0:160, :], held["by_in"][:, lanes])
        a_re, a_im = a[:80], a[80:]
        g_re = repeated[0:80, :]
        g_im = repeated[80:160, :]
        w_re = spec[0, :, lanes].astype(F32)
        w_im = spec[1, :, lanes].astype(F32)
        out_s[0, :, lanes] = FACTOR * (a_re * g_re + a_im * g_im)
        out_s[1, :, lanes] = FACTOR * (a_re * g_im - a_im * g_re)
        p_re = (w_re * g_re + w_im * g_im).astype(BF16)
        p_im = (w_re * g_im - w_im * g_re).astype(BF16)
        turn = held["by_in_t"][lanes, :]
        return carry + mm(jnp.concatenate([p_re, p_im], axis=0), turn)

    b = lax.fori_loop(0, 4, mix, jnp.zeros((160, 128), F32)) * FACTOR
    b_re, b_im = b[:80], b[80:]
    stack = jnp.concatenate([b_re, b_im, b_im, b_re], axis=0) * table("spread_m").astype(F32)
    back = mm(table("spread"), stack.astype(BF16))
    send_b[...] = back.reshape(8, 8, 128).astype(BF16)

    sixth_far = exchange(
        8, lambda k: (send_b.at[s_index(k)], recv_b.at[q], s_peer(k, 1 - zh))
    )
    sixth = exchange(7, lambda k: (send_b.at[s_index(k + 1)], recv_b.at[q], s_peer(k + 1)))
    recv_b[q] = send_b[s]
    latest = exchanges[:]
    exchanges[:] = later
    drain()
    out_copy_s = pltpu.make_async_copy(out_s, out_s_hbm, out_sem.at[4])
    out_copy_s.start()

    arrive(sixth)
    arrive(sixth_far)
    seventh = exchange(3, lambda k: (recv_b, recv_g.at[xx], x_peer(k + 1)))
    recv_g[xx] = recv_b[...]
    loads["row_i"].wait()
    loads["reg_c"].wait()
    arrive(seventh)
    lines = mm(table("row_i"), rows_of(recv_g[...], 512))
    send_l[...] = lines.reshape(8, 2, 16, 128).astype(BF16)
    eighth = exchange(7, lambda k: (send_l.at[s_index(k + 1)], recv_l.at[s], s_peer(k + 1)))
    recv_l[s] = send_l[s]
    arrive(bypass_c)
    by_e[s] = by_c[...].sum(0)
    bypass_e = exchange(7, lambda k: (by_e.at[s], by_e.at[s], s_peer(k + 1)))
    arrive(eighth)
    for half in range(2):
        turned = mm(table("reg_c"), rows_of(recv_l[:, half], 128))
        send_c[half] = turned.reshape(4, 3, 8, 128).astype(BF16)
    ninth = exchange(
        7,
        lambda k: (
            send_c.at[lax.div(z_index(ring_step(k)), 8)],
            recv_c.at[j],
            z_peer(ring_step(k)),
        ),
    )
    recv_c[j] = send_c[zh]
    last = exchanges[:]
    exchanges[:] = latest + last[:-1]
    drain()
    exchanges[:] = last[-1:]
    loads["time_i"].wait()
    loads["col_i"].wait()
    arrive(bypass_e)
    out_b[...] = unpack_bypass(by_e[...].reshape(8, 128))

    def out_copy(x):
        return pltpu.make_async_copy(out_g.at[x], out_g_hbm.at[x], out_sem.at[x])

    def final(x, carry):
        parts = [rows_of(recv_c[:, x, tile], 64) for tile in range(3)]
        rows = final_rows(*parts, held["time_i"][...], held["col_i"][...])
        out_g[x] = (rows + plus[x]).astype(BF16)
        out_copy(x).start()
        return carry

    arrive(ninth)
    lax.fori_loop(0, 4, final, 0)

    drain()
    for x in range(4):
        out_copy(x).wait()
    out_copy_s.wait()


def deliver(g, w, b, to_g, to_w, to_b, held_g, held_w, held_b, sem_in, sem_out):
    pieces = [(b, held_b, to_b)]
    pieces += [(w.at[i, h], held_w.at[i, h], to_w.at[i, h]) for i in range(2) for h in HALVES]
    pieces += [(g.at[i], held_g.at[i], to_g.at[i]) for i in range(4)]
    fetch = [
        pltpu.make_async_copy(p[0], p[1], sem_in.at[i]) for i, p in enumerate(pieces)
    ]
    store = [
        pltpu.make_async_copy(p[1], p[2], sem_out.at[i]) for i, p in enumerate(pieces)
    ]
    for copy in fetch:
        copy.start()
    for i in range(len(pieces)):
        fetch[i].wait()
        store[i].start()
    for copy in store:
        copy.wait()


HALVES = (slice(0, 40), slice(40, 80))
N_COPIES = 14 + 7 + 3 + 15 + 7 + 7 + 3 + 15 + 15 + 3 + 7 + 7


def local(inputs, preactivation, cotangent, spectral, bypass, tables):
    weight = spectral.transpose(0, 1, 3, 2, 4).reshape(2, 80, C * C)
    vmem = pl.BlockSpec(memory_space=pltpu.VMEM)
    anywhere = pl.BlockSpec(memory_space=pl.ANY)
    held = [
        pltpu.VMEM(tables[k].shape[1:] if k in PICKED else tables[k].shape, BF16) for k in ORDER
    ]
    blocks = [
        pltpu.VMEM((4, 128, 256), BF16),
        pltpu.VMEM((4, 128, 256), BF16),
        pltpu.VMEM((4, 128, 256), BF16),
        pltpu.VMEM((2, 80, C * C), BF16),
        pltpu.VMEM((C, C), BF16),
        pltpu.VMEM((4, 128, 256), BF16),
        pltpu.VMEM((2, 80, C * C), F32),
        pltpu.SemaphoreType.DMA((5,)),
        pltpu.SemaphoreType.DMA((5,)),
        pltpu.VMEM((4, 128, 256), BF16),
        pltpu.VMEM((4, 128, 256), F32),
        pltpu.VMEM((8, 5, 4, 8, 128), BF16),
        pltpu.VMEM((7, 5, 4, 8, 128), BF16),
        pltpu.VMEM((8, 2, 3, 8, 128), BF16),
        pltpu.VMEM((8, 2, 3, 8, 128), BF16),
        pltpu.VMEM((4, 64, 384), BF16),
        pltpu.VMEM((3, 64, 384), BF16),
        pltpu.VMEM((16, 10, 128), BF16),
        pltpu.VMEM((16, 10, 128), BF16),
        pltpu.VMEM((8, 8, 128), BF16),
        pltpu.VMEM((16, 8, 128), BF16),
        pltpu.VMEM((4, 16, 8, 128), BF16),
        pltpu.VMEM((8, 2, 16, 128), BF16),
        pltpu.VMEM((8, 2, 16, 128), BF16),
        pltpu.VMEM((2, 4, 3, 8, 128), BF16),
        pltpu.VMEM((8, 4, 3, 8, 128), BF16),
        pltpu.VMEM((2, 160, 128), F32),
        pltpu.VMEM((8, 128), F32),
        pltpu.VMEM((16, 16, 128), F32),
        pltpu.VMEM((8, 8, 128), F32),
        pltpu.VMEM((4, 1, 128), F32),
        pltpu.VMEM((16, 1, 128), F32),
        pltpu.VMEM((8, 1, 128), F32),
        pltpu.VMEM((4, 64, 512), BF16),
        pltpu.VMEM((256, 128), F32),
        pltpu.VMEM((256, 256), F32),
        pltpu.VMEM((256, 256), BF16),
        pltpu.VMEM((320, 128), BF16),
        pltpu.VMEM((160, 256), F32),
        pltpu.SemaphoreType.DMA((len(ORDER),)),
        pltpu.SemaphoreType.DMA((N_COPIES,)),
        pltpu.SemaphoreType.DMA((N_COPIES,)),
    ]
    results = pl.pallas_call(
        kernel,
        out_shape=(
            jax.ShapeDtypeStruct((4, 128, 256), BF16),
            jax.ShapeDtypeStruct((2, 80, C * C), F32),
            jax.ShapeDtypeStruct((C, C), F32),
        ),
        in_specs=[anywhere] * (5 + len(ORDER)),
        out_specs=(anywhere, anywhere, vmem),
        scratch_shapes=held + blocks,
        compiler_params=pltpu.CompilerParams(
            collective_id=0, has_side_effects=True, vmem_limit_bytes=62 * 1024 * 1024
        ),
        name="fno_backward",
    )(inputs, preactivation, cotangent, weight, bypass, *[tables[k] for k in ORDER])
    results = pl.pallas_call(
        deliver,
        out_shape=tuple(jax.ShapeDtypeStruct(o.shape, o.dtype) for o in results),
        in_specs=[anywhere] * 3,
        out_specs=(anywhere,) * 3,
        scratch_shapes=[pltpu.VMEM(o.shape, o.dtype) for o in results]
        + [pltpu.SemaphoreType.DMA((9,)), pltpu.SemaphoreType.DMA((9,))],
        compiler_params=pltpu.CompilerParams(vmem_limit_bytes=62 * 1024 * 1024),
        name="deliver",
    )(*results)
    grad_inputs, grad_weight, grad_bypass = results
    grad_spectral = grad_weight.reshape(2, 2, 5, 8, C * C).transpose(0, 1, 3, 2, 4)
    return (grad_inputs, grad_spectral, grad_bypass)


def solution(mesh):
    tables = make_tables()

    def step(*args):
        return local(*args, {k: jnp.asarray(v) for k, v in tables.items()})

    return jax.shard_map(
        step,
        mesh=mesh,
        in_specs=(
            P("row", "col", None),
            P("row", "col", None),
            P("row", "col", None),
            P(None, "row", "col", None, None),
            P(),
        ),
        out_specs=(P("row", "col", None), P(None, "row", "col", None, None), P()),
        check_vma=False,
    )
```

```python
import math

import jax
import jax.numpy as jnp
import numpy as np
from jax import lax
from jax.experimental import pallas as pl
from jax.experimental.pallas import tpu as pltpu
from jax.sharding import PartitionSpec as P

MESH = pl.DeviceIdType.MESH
F32 = jnp.float32
BF16 = jnp.bfloat16
NX, NY, NT, C = 256, 1024, 8, 32
KX, KY, KT = 128, 64, 5
FACTOR = 1.0 / math.sqrt(float(NX * NY * NT * KX * KY * KT))
BYPASS_SCALE = 1.0 / math.sqrt(float(NX * NY * NT))


def turns(a, b, n):
    angle = 2.0 * np.pi * (np.multiply.outer(a, b) % n) / n
    return np.cos(angle), np.sin(angle)


def column_tables():
    forward, inverse = [], []
    for j in range(8):
        cos, sin = turns(np.arange(64), 128 * j + np.arange(128), NY)
        forward.append(np.concatenate([cos, -sin], 0))
        inverse.append(np.concatenate([cos.T, -sin.T], 1))
    return np.stack(forward), np.stack(inverse)


def time_tables():
    cos, sin = turns(np.arange(NT), np.arange(KT), NT)
    eye = np.eye(C)
    low = np.zeros((2, NT, C, 2, 4, C))
    for t in range(NT):
        for k in range(4):
            low[0, t, :, 0, k, :] = eye * cos[t, k]
            low[1, t, :, 0, k, :] = eye * sin[t, k]
            low[0, t, :, 1, k, :] = -eye * sin[t, k]
            low[1, t, :, 1, k, :] = eye * cos[t, k]
    high = np.zeros((2, 2, NT, C, 2, 2, C))
    for f in range(2):
        for t in range(NT):
            high[f, 0, t, :, f, 0, :] = eye * cos[t, 4]
            high[f, 1, t, :, f, 1, :] = eye * cos[t, 4]
    forward = np.concatenate(
        [low.reshape(512, 256), high[0].reshape(512, 128), high[1].reshape(512, 128)], 1
    )
    inverse = np.zeros((3, 4, C, 2, NT, C))
    for t in range(NT):
        for k in range(4):
            inverse[0, k, :, 0, t, :] = eye * cos[t, k]
            inverse[1, k, :, 0, t, :] = -eye * sin[t, k]
            inverse[0, k, :, 1, t, :] = eye * sin[t, k]
            inverse[1, k, :, 1, t, :] = eye * cos[t, k]
        inverse[2, 0, :, 0, t, :] = eye * cos[t, 4]
        inverse[2, 1, :, 1, t, :] = eye * cos[t, 4]
    return forward, inverse.reshape(384, 512)


def regroup_tables():
    direct = np.zeros((8, 3, 2, 4, 5, 4, 8))
    swapped = np.zeros((8, 3, 2, 4, 5, 4, 8))
    back = np.zeros((4, 3, 8, 8, 2, 2, 4))
    for k in range(8):
        for x in range(4):
            for tile in range(5):
                direct[k, tile // 2, tile % 2, x, tile, x, k] = 1.0
            swapped[k, 2, 1, x, 4, x, k] = 1.0
            for tile in range(3):
                back[x, tile, k, k, tile // 2, tile % 2, x] = 1.0
    return (
        direct.reshape(192, 160),
        swapped.reshape(192, 160)[:, 128:],
        back.reshape(96, 128),
    )


def row_tables():
    k = np.arange(KX)
    freq = np.where(k < KX // 2, k, k - KX) % NX
    cos, sin = turns(freq, np.arange(NX), NX)
    cos = cos.reshape(4, 16, 2, 4, 4, 2, 2, 4)
    sin = sin.reshape(4, 16, 2, 4, 4, 2, 2, 4)
    forward = np.zeros((4, 4, 16, 2, 2, 4, 2, 2, 2, 4))
    for xx in range(4):
        c = cos[:, :, :, xx].transpose(0, 1, 2, 3, 5, 4, 6)
        s = sin[:, :, :, xx].transpose(0, 1, 2, 3, 5, 4, 6)
        forward[xx, :, :, :, 0, :, :, :, 0, :] = c
        forward[xx, :, :, :, 0, :, :, :, 1, :] = s
        forward[xx, :, :, :, 1, :, :, :, 1, :] = c
        forward[xx, :, :, :, 1, :, :, :, 0, :] = -s
    forward = forward.reshape(4, 256, 128)
    deal = np.zeros((16, 16, 3, 16, 2, 2))
    for q in range(16):
        for e in range(2):
            for ab in range(2):
                for slab in range(2):
                    deal[q, slab * 4 + e * 2 + ab, slab, q, e, ab] = 1.0
            deal[q, 8 + e, 2, q, e, 0] = 1.0
    inverse = np.zeros((4, 4, 2, 2, 2, 2, 4, 4, 16, 2, 2, 2))
    for xx in range(4):
        for slab in range(2):
            c = cos[:, :, :, xx].transpose(3, 5, 4, 6, 0, 1, 2)
            s = sin[:, :, :, xx].transpose(3, 5, 4, 6, 0, 1, 2)
            inverse[xx, :, :, :, slab, 0, :, :, :, slab, :, 0] = c
            inverse[xx, :, :, :, slab, 0, :, :, :, slab, :, 1] = -s
            inverse[xx, :, :, :, slab, 1, :, :, :, slab, :, 1] = c
            inverse[xx, :, :, :, slab, 1, :, :, :, slab, :, 0] = s
    return forward, inverse.reshape(4, 256, 512), deal.reshape(256, 192)


def mixing_tables():
    pick = np.zeros((2, 2, 2, 5, 8, 16, 16))
    pick_mask = np.zeros((2, 2, 2, 5, 8, 4, C))
    spread = np.zeros((8, 2, 2, 2, 4, 2, 5, 8))
    spread_mask = np.zeros((4, 2, 5, 8, 4, C))
    for ky in range(8):
        for e in range(2):
            for f in range(2):
                for ri in range(2):
                    for kt in range(4):
                        pick_mask[f, ri, e, kt, ky, kt, :] = 1.0
                    pick_mask[f, ri, e, 4, ky, f * 2 + ri, :] = 1.0
                    for zh in range(2):
                        source = (ky // 2) * 4 + zh * 2 + ky % 2
                        pick[f, ri, e, 0:4, ky, source, f * 4 + e * 2 + ri] = 1.0
                        pick[f, ri, e, 4, ky, source, 8 + e] = 1.0
            for kt in range(4):
                spread_mask[0, e, kt, ky, kt] = 1.0
                spread_mask[1, e, kt, ky, kt] = 1.0
                spread[ky, 0, e, 0, 0, e, kt, ky] = 1.0
                spread[ky, 0, e, 1, 1, e, kt, ky] = 1.0
            spread_mask[0, e, 4, ky, 0] = 1.0
            spread_mask[1, e, 4, ky, 1] = 1.0
            spread_mask[2, e, 4, ky, 0] = 1.0
            spread_mask[3, e, 4, ky, 1] = 1.0
            spread[ky, 1, e, 0, 0, e, 4, ky] = 1.0
            spread[ky, 1, e, 0, 1, e, 4, ky] = 1.0
            spread[ky, 1, e, 1, 2, e, 4, ky] = 1.0
            spread[ky, 1, e, 1, 3, e, 4, ky] = -1.0
    group = np.arange(128) % C
    lane = np.arange(C * C)
    by_in = (group[:, None] == lane[None, :] // C).astype(np.float64)
    by_out = (group[:, None] == lane[None, :256] % C).astype(np.float64)
    return (
        pick.reshape(320, 256),
        pick_mask.reshape(320, 128),
        by_in,
        by_out,
        by_in.T,
        spread.reshape(64, 320),
        spread_mask.reshape(320, 128),
    )


def make_tables():
    t = {}
    t["col_f"], t["col_i"] = column_tables()
    t["time_f"], t["time_i"] = time_tables()
    t["reg_a"], t["reg_b"], t["reg_c"] = regroup_tables()
    t["row_f"], t["row_i"], t["deal"] = row_tables()
    t["pick"], t["pick_m"], t["by_in"], t["by_out"], t["by_in_t"], t["spread"], t["spread_m"] = (
        mixing_tables()
    )
    return {k: np.asarray(v, np.float32).astype(jnp.bfloat16) for k, v in t.items()}


PICKED = ("col_f", "col_i", "row_f", "row_i")
ORDER = (
    "col_f", "time_f", "reg_a", "reg_b", "row_f", "deal", "pick", "pick_m", "by_in",
    "by_out", "by_in_t", "spread", "spread_m", "row_i", "reg_c", "time_i", "col_i",
)


def mm(a, b):
    return jnp.dot(a, b, preferred_element_type=F32)


def mm_full(a, b):
    return jnp.dot(a, b, preferred_element_type=F32, precision=lax.Precision.HIGHEST)


def gelu_slope(values):
    normal_cdf = 0.5 * (1.0 + lax.erf(values * (1.0 / math.sqrt(2.0))))
    density = jnp.exp(-0.5 * values * values) * (1.0 / math.sqrt(2.0 * math.pi))
    return normal_cdf + values * density


def pre_gradient(cot, pre):
    return (cot.astype(F32) * gelu_slope(pre.astype(F32))).astype(BF16)


def group_mask(shape):
    row = lax.broadcasted_iota(jnp.int32, shape, 0)
    lane = lax.broadcasted_iota(jnp.int32, shape, 1)
    return row, lane


def fold_lanes(values):
    values = values + pltpu.roll(values, 64, 1)
    return values + pltpu.roll(values, 32, 1)


def pack_bypass(product):
    row, lane = group_mask((256, 256))
    kept = jnp.where(row // C == lane // C, product, 0.0).reshape(8, C, 256).sum(0)
    wide = fold_lanes(kept[:, :128] + kept[:, 128:])
    row, lane = group_mask((C, 128))
    kept = jnp.where(row % 4 == lane // C, wide, 0.0)
    row, lane = group_mask((8, C))
    return mm_full(jnp.where(row == lane // 4, 1.0, 0.0), kept)


def unpack_bypass(packed):
    row, lane = group_mask((C, 8))
    wide = mm_full(jnp.where(row // 4 == lane, 1.0, 0.0), packed)
    row, lane = group_mask((C, 128))
    kept = fold_lanes(jnp.where(row % 4 == lane // C, wide, 0.0))
    return kept[:, :C] * BYPASS_SCALE


def block_bypass(bypass):
    row, lane = group_mask((256, C))
    tall = jnp.where(row % C == lane, 1.0, 0.0).astype(BF16)
    row, lane = group_mask((C, 256))
    flat = jnp.where(lane % C == row, 1.0, 0.0).astype(BF16)
    turned = lax.dot_general(tall, bypass, (((1,), (1,)), ((), ())), preferred_element_type=F32)
    full = mm(turned.astype(BF16), flat)
    row, lane = group_mask((256, 256))
    return jnp.where(row // C == lane // C, full, 0.0).astype(BF16)


def regroup_forward(total, reg_a, reg_b):
    rows = total.astype(BF16)
    last = total[128:160]
    lane = lax.broadcasted_iota(jnp.int32, (C, 128), 1)
    real = (lane // C) % 2 == 0
    turned = jnp.where(real, pltpu.roll(last, 96, 1), -pltpu.roll(last, 32, 1))
    return mm(reg_a, rows) + mm(reg_b, turned.astype(BF16))


def final_rows(low_re, low_im, high, time_i, col_i):
    z = jnp.concatenate([low_re, low_im, high], axis=1)
    u = mm(z, time_i).astype(BF16)
    return mm(col_i, jnp.concatenate([u[:, :256], u[:, 256:]], axis=0))


def rows_of(block, count):
    return block.astype(F32).reshape(count, 128).astype(BF16)


def kernel(inp_hbm, pre_hbm, cot_hbm, spec_hbm, byp_hbm, *refs):
    n = len(ORDER)
    tables = dict(zip(ORDER, refs[:n]))
    out_g_hbm, out_s_hbm, out_b = refs[n : n + 3]
    held = dict(zip(ORDER, refs[n + 3 : 2 * n + 3]))
    (
        inp, pre, cot, spec, byp, out_g, out_s, arg_sem, out_sem,
        grad, plus, pieces, recv_col, send_s, recv_s, send_x, recv_x, send_q, recv_q,
        send_b, recv_b, recv_g, send_l, recv_l, send_c, recv_c,
        total, by_sum, wide_q, by_a, by_b, by_c, by_e,
        lined, high, product, blocks, chosen, repeated,
        table_sem, send_sem, recv_sem,
    ) = refs[2 * n + 3 :]

    row = lax.axis_index("row")
    j = lax.axis_index("col")
    xx = row // 16
    q = row % 16
    yy = q // 4
    zh = (q // 2) % 2
    core = q % 2
    s = yy * 2 + core

    z = zh * 8 + j

    def ring_step(k):
        d = 4 - lax.div(k + 1, 2)
        odd = lax.rem(k, 2)
        return odd * d + (1 - odd) * (16 - d) + 8 * core * (1 - lax.div(k + 6, 7))

    def z_index(o):
        return lax.rem(z + o, 16)

    def z_peer(o):
        other = z_index(o)
        return xx * 16 + yy * 4 + lax.div(other, 8) * 2 + core, lax.rem(other, 8)

    def s_index(k):
        return lax.rem(s + k, 8)

    def q_of(other, half):
        return lax.div(other, 2) * 4 + half * 2 + lax.rem(other, 2)

    def s_peer(k, half=zh):
        return xx * 16 + q_of(s_index(k), half), j


    def x_peer(k):
        return lax.rem(xx + k, 4) * 16 + q, j

    def far(k):
        return lax.rem(k + 1, 3) + 1

    barrier = pltpu.get_barrier_semaphore()
    everyone = (
        [z_peer(o) for o in (1, 2, 3, 4, 12, 13, 14, 15)]
        + [s_peer(k) for k in range(1, 8)]
        + [x_peer(k) for k in range(1, 4)]
    )
    for peer in everyone:
        pl.semaphore_signal(barrier, inc=1, device_id=peer, device_id_type=MESH)

    index_of = {"col_f": j, "col_i": j, "row_f": xx, "row_i": xx}
    loads = {}

    def load(name):
        source = tables[name].at[index_of[name]] if name in PICKED else tables[name]
        loads[name] = pltpu.make_async_copy(source, held[name], table_sem.at[ORDER.index(name)])
        loads[name].start()

    args = []
    for at, (source, target) in enumerate(
        ((inp_hbm, inp), (cot_hbm, cot), (pre_hbm, pre), (byp_hbm, byp), (spec_hbm, spec))
    ):
        args.append(pltpu.make_async_copy(source, target, arg_sem.at[at]))
    args[0].start()
    load("col_f")
    load("time_f")
    args[1].start()
    args[2].start()
    args[3].start()
    args[4].start()
    for name in ORDER[2:]:
        load(name)

    def table(name):
        return held[name][...]

    exchanges = []
    used = [0]

    def exchange(count, make):
        base = used[0]
        used[0] += count

        def copy(k):
            source, target, peer = make(k)
            return pltpu.make_async_remote_copy(
                src_ref=source,
                dst_ref=target,
                send_sem=send_sem.at[base + k],
                recv_sem=recv_sem.at[base + k],
                device_id=peer,
                device_id_type=MESH,
            )

        def start(k, carry):
            copy(k).start()
            return carry

        lax.fori_loop(0, count, start, 0)
        pair = copy, count
        exchanges.append(pair)
        return pair

    def arrive(pair, first=0, last=None):
        copy, count = pair

        def wait(k, carry):
            copy(k).wait_recv()
            return carry

        lax.fori_loop(first, count if last is None else last, wait, 0)

    def drain():
        for copy, count in exchanges:

            def left(k, carry, copy=copy):
                copy(k).wait_send()
                return carry

            lax.fori_loop(0, count, left, 0)
        exchanges.clear()

    loads["col_f"].wait()
    args[0].wait()

    def lines_in(x, carry):
        y = mm(held["col_f"][...], inp[x]).astype(BF16)
        lined[x, :, 0:256] = y[:64]
        lined[x, :, 256:512] = y[64:]
        return carry

    lax.fori_loop(0, 4, lines_in, 0)
    loads["time_f"].wait()
    r = mm(lined[...].reshape(256, 512), held["time_f"][:, 0:384])
    for x in range(4):
        rows = slice(64 * x, 64 * x + 64)
        pieces[:, 0, x] = r[rows, :128].reshape(8, 8, 128).astype(BF16)
        pieces[:, 1, x] = r[rows, 128:256].reshape(8, 8, 128).astype(BF16)
    high[...] = r[:, 256:]
    pl.semaphore_wait(barrier, len(everyone))
    first_in = exchange(
        7,
        lambda k: (
            pieces.at[lax.rem(z_index(ring_step(k)), 8), 0:2],
            recv_col.at[k, 0:2],
            z_peer(ring_step(k)),
        ),
    )
    args[1].wait()
    args[2].wait()

    def lines_grad(x, carry):
        g = pre_gradient(cot[x], pre[x])
        grad[x] = g
        y = mm(held["col_f"][...], g).astype(BF16)
        lined[x, :, 0:256] = y[:64]
        lined[x, :, 256:512] = y[64:]
        return carry

    lax.fori_loop(0, 4, lines_grad, 0)
    rows = lined[...].reshape(256, 512)
    r = mm(rows, held["time_f"][:, 0:256])
    top = high[...] + mm(rows, held["time_f"][:, 384:512])
    for x in range(4):
        rows = slice(64 * x, 64 * x + 64)
        pieces[:, 2, x] = r[rows, :128].reshape(8, 8, 128).astype(BF16)
        pieces[:, 3, x] = r[rows, 128:].reshape(8, 8, 128).astype(BF16)
        pieces[:, 4, x] = top[rows].reshape(8, 8, 128).astype(BF16)
    first_grad = exchange(
        7,
        lambda k: (
            pieces.at[lax.rem(z_index(ring_step(k)), 8), 2:5],
            recv_col.at[k, 2:5],
            z_peer(ring_step(k)),
        ),
    )

    product[...] = jnp.zeros((256, 256), F32)

    def add_product(x, carry):
        product[...] += lax.dot_general(
            inp[x], grad[x], (((0,), (0,)), ((), ())), preferred_element_type=F32
        )
        return carry

    lax.fori_loop(0, 4, add_product, 0)
    by_a[s] = pack_bypass(product[...])
    bypass_a = exchange(7, lambda k: (by_a.at[s], by_a.at[s], s_peer(k + 1)))
    args[3].wait()
    blocks[...] = block_bypass(byp[...])

    def pointwise(x, carry):
        plus[x] = mm(grad[x], blocks[...])
        return carry

    lax.fori_loop(0, 4, pointwise, 0)

    for name in ("reg_a", "reg_b"):
        loads[name].wait()
    arrive(first_in)
    arrive(first_grad)
    total[zh] = pieces[j].astype(F32).reshape(160, 128)
    total[1 - zh] = jnp.zeros((160, 128), F32)

    def add_terms(k, carry):
        half = lax.div(z_index(32 - ring_step(k)), 8)
        total[half] += recv_col[k].astype(F32).reshape(160, 128)
        return carry

    lax.fori_loop(0, 7, add_terms, 0)
    for half in range(2):
        grouped = regroup_forward(total[half], table("reg_a"), table("reg_b"))
        send_s[:, half] = grouped.reshape(8, 3, 8, 128).astype(BF16)
    recv_s[s] = send_s[s]
    second = exchange(7, lambda k: (send_s.at[s_index(k + 1)], recv_s.at[s], s_peer(k + 1)))

    arrive(bypass_a)
    by_sum[...] = by_a[...].sum(0)
    by_b[xx] = by_sum[pl.ds(s, 1), :]
    bypass_b = exchange(3, lambda k: (by_b.at[xx], by_b.at[xx], x_peer(k + 1)))

    wide_q[...] = jnp.zeros((16, 16, 128), F32)
    loads["row_f"].wait()
    loads["deal"].wait()
    arrive(second)
    rows = jnp.concatenate([rows_of(recv_s[:, :, slab], 128) for slab in range(3)], axis=1)
    send_x[...] = mm(table("row_f"), rows).reshape(4, 64, 384).astype(BF16)
    fourth = exchange(
        3, lambda k: (send_x.at[lax.rem(xx + far(k), 4)], recv_x.at[k], x_peer(far(k)))
    )
    arrive(fourth)
    summed = send_x[xx].astype(F32)
    for k in range(3):
        summed += recv_x[k].astype(F32)
    summed = summed.astype(BF16)
    summed = jnp.concatenate([summed[:, 128 * i : 128 * i + 128] for i in range(3)], axis=0)
    dealt = mm(table("deal"), summed).reshape(16, 16, 128)
    send_q[...] = dealt[:, 0:10].astype(BF16)

    earlier = list(exchanges)
    exchanges.clear()
    fifth_far = exchange(
        8, lambda k: (send_q.at[q_of(s_index(k), 1 - zh)], recv_q.at[q], s_peer(k, 1 - zh))
    )
    fifth = exchange(
        7, lambda k: (send_q.at[q_of(s_index(k + 1), zh)], recv_q.at[q], s_peer(k + 1, zh))
    )
    recv_q[q] = send_q[q]
    arrive(bypass_b)
    by_c[z] = by_b[...].sum(0)
    bypass_c = exchange(15, lambda k: (by_c.at[z], by_c.at[z], z_peer(k + 1)))
    later = list(exchanges)
    exchanges[:] = earlier
    drain()
    for name in ("pick", "pick_m", "by_in", "by_out", "by_in_t", "spread", "spread_m"):
        loads[name].wait()
    args[4].wait()
    arrive(fifth)
    arrive(fifth_far)
    wide_q[:, 0:10] = recv_q[...].astype(F32)
    halves = wide_q[...].reshape(256, 128).astype(BF16)
    chosen[...] = (mm(table("pick"), halves) * table("pick_m").astype(F32)).astype(BF16)
    repeated[...] = mm(chosen[160:320, :], table("by_out"))

    def mix(m, carry):
        lanes = pl.ds(pl.multiple_of(m * 256, 256), 256)
        a = mm(chosen[0:160, :], held["by_in"][:, lanes])
        a_re, a_im = a[:80], a[80:]
        g_re = repeated[0:80, :]
        g_im = repeated[80:160, :]
        w_re = spec[0, :, lanes].astype(F32)
        w_im = spec[1, :, lanes].astype(F32)
        out_s[0, :, lanes] = FACTOR * (a_re * g_re + a_im * g_im)
        out_s[1, :, lanes] = FACTOR * (a_re * g_im - a_im * g_re)
        p_re = (w_re * g_re + w_im * g_im).astype(BF16)
        p_im = (w_re * g_im - w_im * g_re).astype(BF16)
        turn = held["by_in_t"][lanes, :]
        return carry + mm(jnp.concatenate([p_re, p_im], axis=0), turn)

    b = lax.fori_loop(0, 4, mix, jnp.zeros((160, 128), F32)) * FACTOR
    b_re, b_im = b[:80], b[80:]
    stack = jnp.concatenate([b_re, b_im, b_im, b_re], axis=0) * table("spread_m").astype(F32)
    back = mm(table("spread"), stack.astype(BF16))
    send_b[...] = back.reshape(8, 8, 128).astype(BF16)

    sixth_far = exchange(
        8, lambda k: (send_b.at[s_index(k)], recv_b.at[q], s_peer(k, 1 - zh))
    )
    sixth = exchange(7, lambda k: (send_b.at[s_index(k + 1)], recv_b.at[q], s_peer(k + 1)))
    recv_b[q] = send_b[s]
    latest = exchanges[:]
    exchanges[:] = later
    drain()
    out_copy_s = pltpu.make_async_copy(out_s, out_s_hbm, out_sem.at[4])
    out_copy_s.start()

    arrive(sixth)
    arrive(sixth_far)
    seventh = exchange(3, lambda k: (recv_b, recv_g.at[xx], x_peer(far(k))))
    recv_g[xx] = recv_b[...]
    loads["row_i"].wait()
    loads["reg_c"].wait()
    arrive(seventh)
    lines = mm(table("row_i"), rows_of(recv_g[...], 512))
    send_l[...] = lines.reshape(8, 2, 16, 128).astype(BF16)
    eighth = exchange(7, lambda k: (send_l.at[s_index(k + 1)], recv_l.at[s], s_peer(k + 1)))
    recv_l[s] = send_l[s]
    arrive(bypass_c)
    by_e[s] = by_c[...].sum(0)
    bypass_e = exchange(7, lambda k: (by_e.at[s], by_e.at[s], s_peer(k + 1)))
    arrive(eighth)
    for half in range(2):
        turned = mm(table("reg_c"), rows_of(recv_l[:, half], 128))
        send_c[half] = turned.reshape(4, 3, 8, 128).astype(BF16)
    ninth = exchange(
        7,
        lambda k: (
            send_c.at[lax.div(z_index(ring_step(k)), 8)],
            recv_c.at[j],
            z_peer(ring_step(k)),
        ),
    )
    recv_c[j] = send_c[zh]
    last = exchanges[:]
    exchanges[:] = latest + last[:-1]
    drain()
    exchanges[:] = last[-1:]
    loads["time_i"].wait()
    loads["col_i"].wait()
    arrive(bypass_e)
    out_b[...] = unpack_bypass(by_e[...].reshape(8, 128))

    def out_copy(x):
        return pltpu.make_async_copy(out_g.at[x], out_g_hbm.at[x], out_sem.at[x])

    def final(x, carry):
        parts = [rows_of(recv_c[:, x, tile], 64) for tile in range(3)]
        rows = final_rows(*parts, held["time_i"][...], held["col_i"][...])
        out_g[x] = (rows + plus[x]).astype(BF16)
        out_copy(x).start()
        return carry

    arrive(ninth)
    lax.fori_loop(0, 4, final, 0)

    drain()
    for x in range(4):
        out_copy(x).wait()
    out_copy_s.wait()


def deliver(g, w, b, to_g, to_w, to_b, held_g, held_w, held_b, sem_in, sem_out):
    pieces = [(b, held_b, to_b)]
    pieces += [(w.at[i, h], held_w.at[i, h], to_w.at[i, h]) for i in range(2) for h in HALVES]
    pieces += [(g.at[i], held_g.at[i], to_g.at[i]) for i in range(4)]
    fetch = [
        pltpu.make_async_copy(p[0], p[1], sem_in.at[i]) for i, p in enumerate(pieces)
    ]
    store = [
        pltpu.make_async_copy(p[1], p[2], sem_out.at[i]) for i, p in enumerate(pieces)
    ]
    for copy in fetch:
        copy.start()
    for i in range(len(pieces)):
        fetch[i].wait()
        store[i].start()
    for copy in store:
        copy.wait()


HALVES = (slice(0, 40), slice(40, 80))
N_COPIES = 14 + 7 + 3 + 15 + 7 + 7 + 3 + 15 + 15 + 3 + 7 + 7


def local(inputs, preactivation, cotangent, spectral, bypass, tables):
    weight = spectral.transpose(0, 1, 3, 2, 4).reshape(2, 80, C * C)
    vmem = pl.BlockSpec(memory_space=pltpu.VMEM)
    anywhere = pl.BlockSpec(memory_space=pl.ANY)
    held = [
        pltpu.VMEM(tables[k].shape[1:] if k in PICKED else tables[k].shape, BF16) for k in ORDER
    ]
    blocks = [
        pltpu.VMEM((4, 128, 256), BF16),
        pltpu.VMEM((4, 128, 256), BF16),
        pltpu.VMEM((4, 128, 256), BF16),
        pltpu.VMEM((2, 80, C * C), BF16),
        pltpu.VMEM((C, C), BF16),
        pltpu.VMEM((4, 128, 256), BF16),
        pltpu.VMEM((2, 80, C * C), F32),
        pltpu.SemaphoreType.DMA((5,)),
        pltpu.SemaphoreType.DMA((5,)),
        pltpu.VMEM((4, 128, 256), BF16),
        pltpu.VMEM((4, 128, 256), F32),
        pltpu.VMEM((8, 5, 4, 8, 128), BF16),
        pltpu.VMEM((7, 5, 4, 8, 128), BF16),
        pltpu.VMEM((8, 2, 3, 8, 128), BF16),
        pltpu.VMEM((8, 2, 3, 8, 128), BF16),
        pltpu.VMEM((4, 64, 384), BF16),
        pltpu.VMEM((3, 64, 384), BF16),
        pltpu.VMEM((16, 10, 128), BF16),
        pltpu.VMEM((16, 10, 128), BF16),
        pltpu.VMEM((8, 8, 128), BF16),
        pltpu.VMEM((16, 8, 128), BF16),
        pltpu.VMEM((4, 16, 8, 128), BF16),
        pltpu.VMEM((8, 2, 16, 128), BF16),
        pltpu.VMEM((8, 2, 16, 128), BF16),
        pltpu.VMEM((2, 4, 3, 8, 128), BF16),
        pltpu.VMEM((8, 4, 3, 8, 128), BF16),
        pltpu.VMEM((2, 160, 128), F32),
        pltpu.VMEM((8, 128), F32),
        pltpu.VMEM((16, 16, 128), F32),
        pltpu.VMEM((8, 8, 128), F32),
        pltpu.VMEM((4, 1, 128), F32),
        pltpu.VMEM((16, 1, 128), F32),
        pltpu.VMEM((8, 1, 128), F32),
        pltpu.VMEM((4, 64, 512), BF16),
        pltpu.VMEM((256, 128), F32),
        pltpu.VMEM((256, 256), F32),
        pltpu.VMEM((256, 256), BF16),
        pltpu.VMEM((320, 128), BF16),
        pltpu.VMEM((160, 256), F32),
        pltpu.SemaphoreType.DMA((len(ORDER),)),
        pltpu.SemaphoreType.DMA((N_COPIES,)),
        pltpu.SemaphoreType.DMA((N_COPIES,)),
    ]
    results = pl.pallas_call(
        kernel,
        out_shape=(
            jax.ShapeDtypeStruct((4, 128, 256), BF16),
            jax.ShapeDtypeStruct((2, 80, C * C), F32),
            jax.ShapeDtypeStruct((C, C), F32),
        ),
        in_specs=[anywhere] * (5 + len(ORDER)),
        out_specs=(anywhere, anywhere, vmem),
        scratch_shapes=held + blocks,
        compiler_params=pltpu.CompilerParams(
            collective_id=0, has_side_effects=True, vmem_limit_bytes=62 * 1024 * 1024
        ),
        name="fno_backward",
    )(inputs, preactivation, cotangent, weight, bypass, *[tables[k] for k in ORDER])
    results = pl.pallas_call(
        deliver,
        out_shape=tuple(jax.ShapeDtypeStruct(o.shape, o.dtype) for o in results),
        in_specs=[anywhere] * 3,
        out_specs=(anywhere,) * 3,
        scratch_shapes=[pltpu.VMEM(o.shape, o.dtype) for o in results]
        + [pltpu.SemaphoreType.DMA((9,)), pltpu.SemaphoreType.DMA((9,))],
        compiler_params=pltpu.CompilerParams(vmem_limit_bytes=62 * 1024 * 1024),
        name="deliver",
    )(*results)
    grad_inputs, grad_weight, grad_bypass = results
    grad_spectral = grad_weight.reshape(2, 2, 5, 8, C * C).transpose(0, 1, 3, 2, 4)
    return (grad_inputs, grad_spectral, grad_bypass)


def solution(mesh):
    tables = make_tables()

    def step(*args):
        return local(*args, {k: jnp.asarray(v) for k, v in tables.items()})

    return jax.shard_map(
        step,
        mesh=mesh,
        in_specs=(
            P("row", "col", None),
            P("row", "col", None),
            P("row", "col", None),
            P(None, "row", "col", None, None),
            P(),
        ),
        out_specs=(P("row", "col", None), P(None, "row", "col", None, None), P()),
        check_vma=False,
    )
```
